512 devices in a mesh: lat: 16 (over z), lon: 32 (over x, y, core).
Axes of the slice: x: 4, y: 4, z: 16, core: 2. Of those that a mesh axis runs over, the one named last changes fastest.
Arguments:
- winds: float32 [2, 1024, 23040], P(None, 'lat', 'lon'), may hold values from -6 to 6
- thickness: float32 [1024, 23040], P('lat', 'lon'), may hold values from 0.5 to 1.5
- tracer: float32 [1024, 23040], P('lat', 'lon'), may hold values from -6 to 6
- cutoff: int32 [1024], P('lat'), may hold values from 1 to 1440, as said below
- damping: float32 [1024], P('lat'), may hold values from 0.2 to 1
Outputs:
- new_winds: float32 [2, 1024, 23040], P(None, 'lat', 'lon')
- new_thickness: float32 [1024, 23040], P('lat', 'lon')
- new_tracer: float32 [1024, 23040], P('lat', 'lon')
The draws below stay inside these ranges and needn't reach their ends.
Inputs may be any that keep to these rules, and one draw needn't show every extreme that they name: cutoff is a wavenumber of 1 to 1440.
All inputs are finite; a program needn't handle non-finite values.
Results may differ from the reference program's by a relative error of at most 0.0003.
Values sent between devices are 32-bit elements; how exact they have to be, the bound alone decides.
No kernel may reach another device: no remote copies, remote signals or barrier semaphores. Data moves between devices by JAX's collectives and lax.ppermute only.
A program may use at most 128 MiB of HBM per device.

```python
import jax
import jax.numpy as jnp
import numpy as np

NLON = 2880
LEV = 8
NLAT = 1024


def draw_cutoff(key, part):
    half_count = NLON // 2
    row_step = np.pi / NLAT
    latitude = -np.pi / 2 + (np.arange(NLAT) + 0.5) * row_step
    edge_angle = np.pi / 4 + row_step / 2
    cap_rows = np.minimum(half_count, np.maximum(1, np.floor(half_count * np.cos(latitude) / np.cos(edge_angle) + 0.5)))
    row_index = np.arange(NLAT)
    edge_rows = (row_index == NLAT // 4 - 1) | (row_index == NLAT - NLAT // 4)
    keep_mask = jnp.asarray(np.where(edge_rows, 0, 1).astype(np.int32))
    cap_table = jnp.asarray(cap_rows.astype(np.int32))
    noise = jax.random.randint(key, (NLAT,), 0, 1 << 20, dtype=jnp.int32)
    return cap_table - noise % (cap_table // 2 + 1) * keep_mask


def block_levels(stream_key, dims, shards, least, top_value):
    def one(position, blocks):
        steps = jax.random.uniform(jax.random.fold_in(jax.random.fold_in(stream_key, 6), position), (blocks,), jnp.float32, least / len(shards), top_value / len(shards))
        return jnp.repeat(jnp.exp(steps), dims[position] // blocks).reshape((-1,) + (1,) * (len(dims) - position - 1))

    loudness = one(*shards[0])
    for cut in shards[1:]:
        loudness = loudness * one(*cut)
    return loudness


def bell_draw(rng, shape, scale, most, shards=(), kind=jnp.bfloat16):
    factor_of = block_levels(rng, shape, shards, -0.22, 0.18) if shards else 1.0
    array = jax.random.normal(rng, shape, jnp.float32) * scale * factor_of
    return jnp.minimum(jnp.maximum(array, -most), most).astype(kind)


def setup_inputs(seed: int = 0) -> dict:
    splits = jax.random.split(jax.random.key(seed), 6)
    winds = bell_draw(splits[0], (2, NLAT, NLON * LEV), 1.0, 6.0, ((1, 16), (2, 32)), jnp.float32)
    thickness = jnp.clip(0.5 + 1.0 * jax.random.uniform(splits[1], (NLAT, NLON * LEV), jnp.float32) ** block_levels(splits[1], (NLAT, NLON * LEV), ((0, 16), (1, 32)), -0.2, 0.2), 0.5, 1.5)
    tracer = bell_draw(splits[2], (NLAT, NLON * LEV), 1.0, 6.0, ((0, 16), (1, 32)), jnp.float32)
    cutoff = draw_cutoff(jax.random.fold_in(splits[5], 71), 0)
    damping = jnp.clip(0.2 + 0.8 * jax.random.uniform(splits[4], (NLAT,), jnp.float32) ** block_levels(splits[4], (NLAT,), ((0, 16),), -0.2, 0.2), 0.2, 1.0)
    return {"winds": winds, "thickness": thickness, "tracer": tracer, "cutoff": cutoff, "damping": damping}


def east_of(values):
    return jnp.roll(values, -1, axis=-1)


def west_of(values):
    return jnp.roll(values, 1, axis=-1)


def antipode(values):
    return jnp.roll(values, NLON // 2, axis=-1)


def stencil(zonal, meridional, layer, tracer_mass):
    lon_step = 2.0 * jnp.pi / NLON
    lat_step = jnp.pi / NLAT
    time_step = lon_step
    centers = -jnp.pi / 2 + (jnp.arange(NLAT, dtype=jnp.float32) + 0.5) * lat_step
    cos_center = jnp.cos(centers)[:, None]
    faces = jnp.arange(NLAT + 1, dtype=jnp.float32)
    cos_face = jnp.where((faces == 0) | (faces == NLAT), 0.0, jnp.cos(-jnp.pi / 2 + faces * lat_step))[:, None]
    zero_row = jnp.zeros((LEV, 1, NLON), jnp.float32)
    flux_east = 0.25 * (zonal + east_of(zonal)) * (layer + east_of(layer))
    tracer_east = 0.25 * (zonal + east_of(zonal)) * (tracer_mass + east_of(tracer_mass))
    padded_wind = jnp.concatenate([zero_row, meridional, zero_row], axis=1)
    padded_layer = jnp.concatenate([zero_row, layer, zero_row], axis=1)
    padded_tracer = jnp.concatenate([zero_row, tracer_mass, zero_row], axis=1)
    wind_face = padded_wind[:, :-1] + padded_wind[:, 1:]
    flux_north = 0.25 * wind_face * (padded_layer[:, :-1] + padded_layer[:, 1:]) * cos_face
    tracer_north = 0.25 * wind_face * (padded_tracer[:, :-1] + padded_tracer[:, 1:]) * cos_face
    layer_div = ((flux_east - west_of(flux_east)) / lon_step + (flux_north[:, 1:] - flux_north[:, :-1]) / lat_step) / cos_center
    tracer_div = ((tracer_east - west_of(tracer_east)) / lon_step + (tracer_north[:, 1:] - tracer_north[:, :-1]) / lat_step) / cos_center
    new_layer = layer - time_step * layer_div
    new_tracer = tracer_mass - time_step * tracer_div
    north_rows = jnp.concatenate([layer[:, 1:], antipode(layer[:, -1:])], axis=1)
    south_rows = jnp.concatenate([antipode(layer[:, :1]), layer[:, :-1]], axis=1)
    new_zonal = zonal - time_step * (east_of(layer) - west_of(layer)) / (2.0 * lon_step * cos_center)
    new_meridional = meridional - time_step * (north_rows - south_rows) / (2.0 * lat_step)
    return new_zonal, new_meridional, new_layer, new_tracer


def unfold(values):
    return jnp.transpose(values.reshape(NLAT, NLON, LEV), (2, 0, 1))


def fold(values):
    return jnp.transpose(values, (1, 2, 0)).reshape(NLAT, NLON * LEV)


def reference(winds, thickness, tracer, cutoff, damping):
    fields = jnp.stack([unfold(winds[0]), unfold(winds[1]), unfold(thickness), unfold(tracer)])
    wavenumber = jnp.arange(NLON // 2 + 1, dtype=jnp.float32)
    cut_float = cutoff.astype(jnp.float32)[:, None]
    ratios = cut_float / jnp.maximum(wavenumber, 1.0)[None, :]
    row_index = jnp.arange(NLAT, dtype=jnp.int32)
    is_polar = (row_index < NLAT // 4) | (row_index >= NLAT - NLAT // 4)
    factor = jnp.where((wavenumber[None, :] > cut_float) & is_polar[:, None], damping[:, None] * ratios * ratios, 1.0)
    spectrum = jnp.fft.rfft(fields, axis=-1)
    filtered = jnp.fft.irfft(spectrum * factor, n=NLON, axis=-1).astype(jnp.float32)
    new_zonal, new_meridional, new_layer, new_tracer = stencil(filtered[0], filtered[1], filtered[2], filtered[3])
    return jnp.stack([fold(new_zonal), fold(new_meridional)]), fold(new_layer), fold(new_tracer)
```

```python
import functools
import math

import jax
import jax.numpy as jnp
import numpy as np
from jax import lax
from jax.experimental import pallas as pl
from jax.experimental.pallas import tpu as pltpu
from jax.sharding import PartitionSpec as P

LEV = 8
NLON = 2880
LANE = 128
TILES = NLON * LEV // LANE
STEP = LANE // LEV
WIDE = 768


def _lin(terms):
    total = None
    for weight, value in terms:
        if value is None or abs(weight) < 1e-12:
            continue
        if abs(weight - 1.0) < 1e-12:
            item = value
        else:
            item = value * np.float32(weight)
        total = item if total is None else total + item
    return total


def _odd_tables(size):
    half = (size - 1) // 2
    angle = [[2.0 * math.pi * ((j * k) % size) / size for j in range(half + 1)] for k in range(half + 1)]
    return half, angle


def odd_real_forward(values):
    size = len(values)
    half, angle = _odd_tables(size)
    plus = [values[j] + values[size - j] for j in range(1, half + 1)]
    minus = [values[j] - values[size - j] for j in range(1, half + 1)]
    out = [(_lin([(1.0, values[0])] + [(1.0, t) for t in plus]), None)]
    for k in range(1, half + 1):
        real = _lin([(1.0, values[0])] + [(math.cos(angle[k][j]), plus[j - 1]) for j in range(1, half + 1)])
        imag = _lin([(-math.sin(angle[k][j]), minus[j - 1]) for j in range(1, half + 1)])
        out.append((real, imag))
    return out


def odd_real_inverse(bins):
    half = len(bins) - 1
    size = 2 * half + 1
    _, angle = _odd_tables(size)
    doubled = [(b[0] * np.float32(2.0), b[1] * np.float32(2.0)) for b in bins[1:]]
    out = [None] * size
    out[0] = _lin([(1.0, bins[0][0])] + [(1.0, b[0]) for b in doubled])
    for n in range(1, half + 1):
        even = _lin([(1.0, bins[0][0])] + [(math.cos(angle[n][k]), doubled[k - 1][0]) for k in range(1, half + 1)])
        odd = _lin([(math.sin(angle[n][k]), doubled[k - 1][1]) for k in range(1, half + 1)])
        out[n] = even - odd
        out[size - n] = even + odd
    return out


def odd_complex(values, sign):
    size = len(values)
    half, angle = _odd_tables(size)
    out = [None] * size
    plus = [(values[j][0] + values[size - j][0], values[j][1] + values[size - j][1]) for j in range(1, half + 1)]
    minus = [(values[j][0] - values[size - j][0], values[j][1] - values[size - j][1]) for j in range(1, half + 1)]
    out[0] = tuple(_lin([(1.0, values[0][part])] + [(1.0, t[part]) for t in plus]) for part in (0, 1))
    for k in range(1, half + 1):
        base = [
            _lin([(1.0, values[0][part])] + [(math.cos(angle[k][j]), plus[j - 1][part]) for j in range(1, half + 1)])
            for part in (0, 1)
        ]
        turn = [_lin([(math.sin(angle[k][j]), minus[j - 1][part]) for j in range(1, half + 1)]) for part in (0, 1)]
        low = (base[0] + turn[1], base[1] - turn[0])
        high = (base[0] - turn[1], base[1] + turn[0])
        if sign < 0:
            out[k], out[size - k] = low, high
        else:
            out[k], out[size - k] = high, low
    return out


COMPLEX_CLASSES = [(0, 1), (0, 2), (2, 1), (2, 2), (1, 0), (1, 1), (1, 2), (1, 3), (1, 4)]


def _tile_of(a, b, c):
    return (45 * a + 36 * b + 20 * c) % TILES


def _bin_of(alpha, beta, gamma):
    for kappa in range(TILES):
        if kappa % 4 == alpha and kappa % 5 == beta and kappa % 9 == gamma:
            return kappa
    raise ValueError


def _bin_list():
    bins = []
    for alpha in (0, 2):
        bins += [(alpha, 0, gamma) for gamma in range(5)]
    for alpha, beta in COMPLEX_CLASSES:
        bins += [(alpha, beta, gamma) for gamma in range(9)]
    return bins


BINS = _bin_list()
COUNT = len(BINS)
SLOT = {key: index for index, key in enumerate(BINS)}
REAL_ROWS = {(0, 0): 0, (2, 0): 1}
COMPLEX_ROWS = {key: 2 + 2 * index for index, key in enumerate(COMPLEX_CLASSES)}


@functools.lru_cache(maxsize=1)
def tables():
    kappa = np.array([_bin_of(*key) for key in BINS])
    phase = (np.arange(LANE) // LEV)[None, :]
    turn = 2.0 * np.pi * ((kappa[:, None] * phase) % NLON) / NLON
    wave = kappa[:, None] + TILES * phase
    wave = np.minimum(wave, NLON - wave).astype(np.float64)
    rows = np.stack(
        [np.cos(turn), np.sin(turn), wave, 1.0 / (np.maximum(wave, 1.0) ** 2 * NLON)], axis=0
    ).astype(np.float32)
    s = np.arange(LANE) // LEV
    level = np.arange(LANE) % LEV
    same = (level[:, None] == level[None, :]).astype(np.float64)
    angle = 2.0 * np.pi * ((s[:, None] * s[None, :]) % STEP) / STEP
    cosines = np.cos(angle) * same
    sines = np.sin(angle) * same
    forward = np.block([[cosines, -sines], [sines, cosines]]).astype(np.float32)
    return rows, forward, forward.T.copy()


GROUP = 13


def filter_kernel(x_ref, cut_ref, rows_ref, forward_ref, inverse_ref, out_ref, full, mid, stage):
    sectors = x_ref.shape[0]
    span = x_ref.shape[2]
    for d in range(sectors):
        full[:, LANE + d * span : LANE + (d + 1) * span] = x_ref[d]

    def tile(p):
        return slice(LANE * (p + 1), LANE * (p + 2))

    for c in range(9):
        quarter = []
        for b in range(5):
            v = [full[:, tile(_tile_of(a, b, c))] for a in range(4)]
            even, odd = v[0] + v[2], v[1] + v[3]
            quarter.append((even + odd, even - odd, v[0] - v[2], v[3] - v[1]))
        zero = odd_real_forward([q[0] for q in quarter])
        two = odd_real_forward([q[1] for q in quarter])
        one = odd_complex([(q[2], q[3]) for q in quarter], -1)
        mid[0, c] = zero[0][0]
        mid[1, c] = two[0][0]
        pieces = {(0, 1): zero[1], (0, 2): zero[2], (2, 1): two[1], (2, 2): two[2]}
        for beta in range(5):
            pieces[(1, beta)] = one[beta]
        for key, value in pieces.items():
            row = COMPLEX_ROWS[key]
            mid[row, c] = value[0]
            mid[row + 1, c] = value[1]

    def put(slot, value):
        cos_row = rows_ref[0, slot : slot + 1, :]
        sin_row = rows_ref[1, slot : slot + 1, :]
        where = slice(8 * slot, 8 * slot + 8)
        if value[1] is None:
            stage[where, :LANE] = value[0] * cos_row
            stage[where, LANE:] = -(value[0] * sin_row)
        else:
            stage[where, :LANE] = value[0] * cos_row + value[1] * sin_row
            stage[where, LANE:] = value[1] * cos_row - value[0] * sin_row

    for key, row in REAL_ROWS.items():
        for gamma, value in enumerate(odd_real_forward([mid[row, c] for c in range(9)])):
            put(SLOT[(key[0], key[1], gamma)], value)
    for key, row in COMPLEX_ROWS.items():
        for gamma, value in enumerate(odd_complex([(mid[row, c], mid[row + 1, c]) for c in range(9)], -1)):
            put(SLOT[(key[0], key[1], gamma)], value)

    cut = cut_ref[0]
    gain = cut_ref[1]
    for start in range(0, COUNT, GROUP):
        where = slice(8 * start, 8 * (start + GROUP))
        spectrum = jnp.dot(
            stage[where, :], forward_ref[...], precision=lax.Precision.HIGHEST, preferred_element_type=jnp.float32
        )
        scaled = []
        for index in range(GROUP):
            slot = start + index
            wave = rows_ref[2, slot : slot + 1, :]
            decay = rows_ref[3, slot : slot + 1, :]
            factor = jnp.where(wave > cut, gain * decay, np.float32(1.0 / NLON))
            part = spectrum[8 * index : 8 * index + 8, :]
            scaled.append(part * jnp.concatenate([factor, factor], axis=1))
        stage[where, :] = jnp.dot(
            jnp.concatenate(scaled, axis=0),
            inverse_ref[...],
            precision=lax.Precision.HIGHEST,
            preferred_element_type=jnp.float32,
        )

    def take(slot, real):
        cos_row = rows_ref[0, slot : slot + 1, :]
        sin_row = rows_ref[1, slot : slot + 1, :]
        where = slice(8 * slot, 8 * slot + 8)
        re, im = stage[where, :LANE], stage[where, LANE:]
        if real:
            return (re * cos_row - im * sin_row, None)
        return (re * cos_row - im * sin_row, im * cos_row + re * sin_row)

    for key, row in REAL_ROWS.items():
        values = odd_real_inverse([take(SLOT[(key[0], key[1], gamma)], gamma == 0) for gamma in range(5)])
        for c in range(9):
            mid[row, c] = values[c]
    for key, row in COMPLEX_ROWS.items():
        values = odd_complex([take(SLOT[(key[0], key[1], gamma)], False) for gamma in range(9)], 1)
        for c in range(9):
            mid[row, c] = values[c][0]
            mid[row + 1, c] = values[c][1]

    for c in range(9):

        def piece(key):
            row = COMPLEX_ROWS[key]
            return (mid[row, c], mid[row + 1, c])

        zero = odd_real_inverse([(mid[0, c], None), piece((0, 1)), piece((0, 2))])
        two = odd_real_inverse([(mid[1, c], None), piece((2, 1)), piece((2, 2))])
        one = odd_complex([piece((1, beta)) for beta in range(5)], 1)
        for b in range(5):
            even, odd = zero[b] + two[b], zero[b] - two[b]
            re2, im2 = one[b][0] + one[b][0], one[b][1] + one[b][1]
            values = (even + re2, odd - im2, even - re2, odd + im2)
            for a in range(4):
                p = _tile_of(a, b, c)
                full[:, tile(p)] = values[a]
                if p == 0:
                    full[:, tile(TILES)] = values[a]
                if p == TILES - 1:
                    full[:, tile(-1)] = values[a]

    for d in range(sectors):
        first = LANE + d * span
        out_ref[d, :, 0 : span + LEV] = full[:, first : first + span + LEV]
        out_ref[d, :, span + LEV : WIDE - LEV] = jnp.zeros((8, WIDE - span - 2 * LEV), jnp.float32)
        out_ref[d, :, WIDE - LEV : WIDE] = full[:, first - LEV : first]


def filter_rows(blocks, cuts):
    rows, forward, inverse = tables()
    return pl.pallas_call(
        filter_kernel,
        out_shape=jax.ShapeDtypeStruct((blocks.shape[0], 8, WIDE), jnp.float32),
        in_specs=[pl.BlockSpec(memory_space=pltpu.VMEM)] * 5,
        out_specs=pl.BlockSpec(memory_space=pltpu.VMEM),
        scratch_shapes=[
            pltpu.VMEM((8, (TILES + 2) * LANE), jnp.float32),
            pltpu.VMEM((20, 9, 8, LANE), jnp.float32),
            pltpu.VMEM((8 * COUNT, 2 * LANE), jnp.float32),
        ],
        name="polar_filter",
    )(blocks, cuts, jnp.asarray(rows), jnp.asarray(forward), jnp.asarray(inverse))


def stencil_kernel(ratio, even_ref, field_ref, first_ref, second_ref, coef_ref, winds_ref, layer_ref, tracer_ref, tall):
    is_even = even_ref[0] > 0
    first = first_ref[...]
    second = second_ref[...]
    south = jnp.where(is_even, second, first)
    north = jnp.where(is_even, first, second)
    for f in range(3):
        tall[f, 7:8, :] = south[f : f + 1, :]
        tall[f, 72:73, :] = north[f : f + 1, :]
        for g in range(8):
            tall[f, 8 + 8 * g : 16 + 8 * g, :] = field_ref[8 * (f + 1) + g]

    def east(x):
        return pltpu.roll(x, WIDE - LEV, 1)

    def west(x):
        return pltpu.roll(x, LEV, 1)

    span = layer_ref.shape[1]
    for g in range(8):
        rows = slice(8 * g, 8 * g + 8)
        at = 8 + 8 * g
        u = field_ref[g]
        v, h, q = (tall[f, at : at + 8, :] for f in range(3))
        v_s, h_s, q_s = (tall[f, at - 1 : at + 7, :] for f in range(3))
        v_n, h_n, q_n = (tall[f, at + 1 : at + 9, :] for f in range(3))
        zonal = coef_ref[rows, 0:1]
        to_north = coef_ref[rows, 1:2]
        to_south = coef_ref[rows, 2:3]
        slope = coef_ref[rows, 3:4]
        h_e = east(h)
        su = u + east(u)
        fx = su * (h + h_e)
        gx = su * (q + east(q))
        wind_n = (v + v_n) * to_north
        wind_s = (v_s + v) * to_south
        new_h = h - (zonal * (fx - west(fx)) + (wind_n * (h + h_n) - wind_s * (h_s + h)))
        new_q = q - (zonal * (gx - west(gx)) + (wind_n * (q + q_n) - wind_s * (q_s + q)))
        new_u = u - slope * (h_e - west(h))
        new_v = v - np.float32(ratio) * (h_n - h_s)
        winds_ref[0, rows, :] = new_u[:, :span]
        winds_ref[1, rows, :] = new_v[:, :span]
        layer_ref[rows, :] = new_h[:, :span]
        tracer_ref[rows, :] = new_q[:, :span]


def stencil(even, fields, first, second, coef, ratio, row_count, width):
    vmem = pl.BlockSpec(memory_space=pltpu.VMEM)
    return pl.pallas_call(
        functools.partial(stencil_kernel, ratio),
        out_shape=(
            jax.ShapeDtypeStruct((2, row_count, width), jnp.float32),
            jax.ShapeDtypeStruct((row_count, width), jnp.float32),
            jax.ShapeDtypeStruct((row_count, width), jnp.float32),
        ),
        in_specs=[pl.BlockSpec(memory_space=pltpu.SMEM), vmem, vmem, vmem, vmem],
        out_specs=(vmem, vmem, vmem),
        scratch_shapes=[pltpu.VMEM((3, row_count + 16, WIDE), jnp.float32)],
        name="stencil",
    )(even, fields, first, second, coef)


def per_device(winds, thickness, tracer, cutoff, damping):
    lat_size = lax.axis_size("lat")
    lon_size = lax.axis_size("lon")
    band = lax.axis_index("lat")
    sector = lax.axis_index("lon")
    row_count, width = thickness.shape
    nlat = row_count * lat_size

    flat = jnp.concatenate([winds.reshape(2 * row_count, width), thickness, tracer], axis=0)
    blocks = flat.reshape(lon_size, 4 * row_count // lon_size, width)
    owned = lax.all_to_all(blocks, "lon", split_axis=0, concat_axis=0, tiled=True)

    is_polar = (band < lat_size // 4) | (band >= lat_size - lat_size // 4)
    group = sector % (row_count // 8)
    cut = lax.dynamic_slice_in_dim(cutoff.astype(jnp.float32), group * 8, 8)
    damp = lax.dynamic_slice_in_dim(damping, group * 8, 8)
    gain = damp * cut * cut
    cut = jnp.where(is_polar, cut, jnp.float32(NLON))
    cuts = jnp.broadcast_to(jnp.stack([cut, gain])[:, :, None], (2, 8, LANE))

    filtered = filter_rows(owned, cuts)
    fields = lax.all_to_all(filtered, "lon", split_axis=0, concat_axis=0, tiled=True)

    even = band % 2 == 0
    groups = row_count // 8
    low = jnp.stack([fields[f * groups, 0] for f in (1, 2, 3)])
    high = jnp.stack([fields[f * groups + groups - 1, 7] for f in (1, 2, 3)])
    pairs = {0: [], 1: []}
    for z in range(lat_size):
        for e in range(lon_size):
            here = z * lon_size + e
            across = z * lon_size + (e + lon_size // 2) % lon_size
            up = here + lon_size if z < lat_size - 1 else across
            down = here - lon_size if z > 0 else across
            pairs[0].append((here, up if z % 2 == 0 else down))
            pairs[1].append((here, down if z % 2 == 0 else up))
    first = lax.ppermute(jnp.where(even, high, low), ("lat", "lon"), pairs[0])
    second = lax.ppermute(jnp.where(even, low, high), ("lat", "lon"), pairs[1])

    lon_step = 2.0 * math.pi / NLON
    lat_step = math.pi / nlat
    rows = (band * row_count + jnp.arange(row_count, dtype=jnp.int32)).astype(jnp.float32)
    center = jnp.cos(-math.pi / 2 + (rows + 0.5) * lat_step)
    face = band * row_count + jnp.arange(row_count + 1, dtype=jnp.int32)
    cos_face = jnp.where(
        (face == 0) | (face == nlat), 0.0, jnp.cos(-math.pi / 2 + face.astype(jnp.float32) * lat_step)
    )
    quarter = 0.25 / center
    aspect = lon_step / lat_step
    coef = jnp.stack(
        [quarter, aspect * quarter * cos_face[1:], aspect * quarter * cos_face[:-1], 2.0 * quarter], axis=1
    )
    coef = jnp.pad(coef, ((0, 0), (0, LANE - 4)))
    return stencil(
        even.astype(jnp.int32)[None], fields, first, second, coef, lon_step / (2.0 * lat_step), row_count, width
    )


def solution(mesh):
    placed = (P(None, "lat", "lon"), P("lat", "lon"), P("lat", "lon"), P("lat"), P("lat"))
    return jax.shard_map(
        per_device,
        mesh=mesh,
        in_specs=placed,
        out_specs=(P(None, "lat", "lon"), P("lat", "lon"), P("lat", "lon")),
        check_vma=False,
    )
```

```python
import functools
import math

import jax
import jax.numpy as jnp
import numpy as np
from jax import lax
from jax.experimental import pallas as pl
from jax.experimental.pallas import tpu as pltpu
from jax.sharding import PartitionSpec as P

LEV = 8
NLON = 2880
LANE = 128
TILES = NLON * LEV // LANE
STEP = LANE // LEV
SMALL_GRANT = 12 << 20
WIDE = 768


def _lin(terms):
    total = None
    for weight, value in terms:
        if value is None or abs(weight) < 1e-12:
            continue
        if abs(weight - 1.0) < 1e-12:
            item = value
        else:
            item = value * np.float32(weight)
        total = item if total is None else total + item
    return total


def _odd_tables(size):
    half = (size - 1) // 2
    angle = [[2.0 * math.pi * ((j * k) % size) / size for j in range(half + 1)] for k in range(half + 1)]
    return half, angle


def odd_real_forward(values):
    size = len(values)
    half, angle = _odd_tables(size)
    plus = [values[j] + values[size - j] for j in range(1, half + 1)]
    minus = [values[j] - values[size - j] for j in range(1, half + 1)]
    out = [(_lin([(1.0, values[0])] + [(1.0, t) for t in plus]), None)]
    for k in range(1, half + 1):
        real = _lin([(1.0, values[0])] + [(math.cos(angle[k][j]), plus[j - 1]) for j in range(1, half + 1)])
        imag = _lin([(-math.sin(angle[k][j]), minus[j - 1]) for j in range(1, half + 1)])
        out.append((real, imag))
    return out


def odd_real_inverse(bins):
    half = len(bins) - 1
    size = 2 * half + 1
    _, angle = _odd_tables(size)
    doubled = [(b[0] * np.float32(2.0), b[1] * np.float32(2.0)) for b in bins[1:]]
    out = [None] * size
    out[0] = _lin([(1.0, bins[0][0])] + [(1.0, b[0]) for b in doubled])
    for n in range(1, half + 1):
        even = _lin([(1.0, bins[0][0])] + [(math.cos(angle[n][k]), doubled[k - 1][0]) for k in range(1, half + 1)])
        odd = _lin([(math.sin(angle[n][k]), doubled[k - 1][1]) for k in range(1, half + 1)])
        out[n] = even - odd
        out[size - n] = even + odd
    return out


def three(values, sign):
    (ar, ai), (br, bi), (cr, ci) = values
    tr, ti = br + cr, bi + ci
    mr, mi = ar - np.float32(0.5) * tr, ai - np.float32(0.5) * ti
    root = np.float32(sign * math.sqrt(0.75))
    er, ei = root * (br - cr), root * (bi - ci)
    return [(ar + tr, ai + ti), (mr - ei, mi + er), (mr + ei, mi - er)]


def nine(values, sign):
    inner = [three([values[n], values[n + 3], values[n + 6]], sign) for n in range(3)]
    out = [None] * 9
    for k in range(3):
        column = [inner[0][k]]
        for n in (1, 2):
            re, im = inner[n][k]
            if k:
                c = np.float32(math.cos(2.0 * math.pi * n * k / 9))
                s = np.float32(sign * math.sin(2.0 * math.pi * n * k / 9))
                re, im = re * c - im * s, re * s + im * c
            column.append((re, im))
        out[k], out[k + 3], out[k + 6] = three(column, sign)
    return out


def odd_complex(values, sign):
    size = len(values)
    if size == 9:
        return nine(values, sign)
    half, angle = _odd_tables(size)
    out = [None] * size
    plus = [(values[j][0] + values[size - j][0], values[j][1] + values[size - j][1]) for j in range(1, half + 1)]
    minus = [(values[j][0] - values[size - j][0], values[j][1] - values[size - j][1]) for j in range(1, half + 1)]
    out[0] = tuple(_lin([(1.0, values[0][part])] + [(1.0, t[part]) for t in plus]) for part in (0, 1))
    for k in range(1, half + 1):
        base = [
            _lin([(1.0, values[0][part])] + [(math.cos(angle[k][j]), plus[j - 1][part]) for j in range(1, half + 1)])
            for part in (0, 1)
        ]
        turn = [_lin([(math.sin(angle[k][j]), minus[j - 1][part]) for j in range(1, half + 1)]) for part in (0, 1)]
        low = (base[0] + turn[1], base[1] - turn[0])
        high = (base[0] - turn[1], base[1] + turn[0])
        if sign < 0:
            out[k], out[size - k] = low, high
        else:
            out[k], out[size - k] = high, low
    return out


COMPLEX_CLASSES = [(0, 1), (0, 2), (2, 1), (2, 2), (1, 0), (1, 1), (1, 2), (1, 3), (1, 4)]


def _tile_of(a, b, c):
    return (45 * a + 36 * b + 20 * c) % TILES


def _bin_of(alpha, beta, gamma):
    for kappa in range(TILES):
        if kappa % 4 == alpha and kappa % 5 == beta and kappa % 9 == gamma:
            return kappa
    raise ValueError


def _bin_list():
    bins = []
    for alpha in (0, 2):
        bins += [(alpha, 0, gamma) for gamma in range(5)]
    for alpha, beta in COMPLEX_CLASSES:
        bins += [(alpha, beta, gamma) for gamma in range(9)]
    return bins


BINS = _bin_list()
COUNT = len(BINS)
SLOT = {key: index for index, key in enumerate(BINS)}
REAL_ROWS = {(0, 0): 0, (2, 0): 1}
COMPLEX_ROWS = {key: 2 + 2 * index for index, key in enumerate(COMPLEX_CLASSES)}


@functools.lru_cache(maxsize=1)
def tables():
    kappa = np.array([_bin_of(*key) for key in BINS])
    phase = (np.arange(LANE) // LEV)[None, :]
    turn = 2.0 * np.pi * ((kappa[:, None] * phase) % NLON) / NLON
    wave = kappa[:, None] + TILES * phase
    wave = np.minimum(wave, NLON - wave).astype(np.float64)
    rows = np.stack(
        [np.cos(turn), np.sin(turn), wave, 1.0 / (np.maximum(wave, 1.0) ** 2 * NLON)], axis=0
    ).astype(np.float32)
    s = np.arange(LANE) // LEV
    level = np.arange(LANE) % LEV
    same = (level[:, None] == level[None, :]).astype(np.float64)
    angle = 2.0 * np.pi * ((s[:, None] * s[None, :]) % STEP) / STEP
    cosines = np.cos(angle) * same
    sines = np.sin(angle) * same
    forward = np.block([[cosines, -sines], [sines, cosines]]).astype(np.float32)

    def split(matrix):
        high = matrix.astype(jnp.bfloat16)
        low = (matrix - high.astype(np.float32)).astype(jnp.bfloat16)
        return np.concatenate([high, high, low], axis=0)

    return rows, split(forward), split(forward.T)


def split_dot(value, matrix):
    high = value.astype(jnp.bfloat16)
    low = (value - high.astype(jnp.float32)).astype(jnp.bfloat16)
    return jnp.dot(jnp.concatenate([high, low, high], axis=1), matrix, preferred_element_type=jnp.float32)


GROUP = 91


def filter_kernel(x_ref, cut_ref, rows_ref, forward_ref, inverse_ref, out_ref, full, mid, stage):
    sectors = x_ref.shape[0]
    span = x_ref.shape[2]
    lane = lax.broadcasted_iota(jnp.int32, (8, LANE), 1)
    turned = {}

    def source(d, t):
        if (d, t) not in turned:
            value = x_ref[d, :, LANE * t : min(LANE * (t + 1), span)]
            if value.shape[1] < LANE:
                value = jnp.concatenate([value, jnp.zeros((8, LANE - value.shape[1]), jnp.float32)], axis=1)
            shift = d * span % LANE
            turned[(d, t)] = pltpu.roll(value, shift, 1) if shift else value
        return turned[(d, t)]

    for p in range(TILES):
        edges = []
        for j in range(0, LANE, LEV):
            d, rest = divmod(LANE * p + j, span)
            key = (d, rest // LANE)
            if not edges or edges[-1][1:] != key:
                edges.append((j,) + key)
        value = source(*edges[-1][1:])
        for (_, d, t), (stop, _, _) in reversed(list(zip(edges[:-1], edges[1:]))):
            value = jnp.where(lane < stop, source(d, t), value)
        full[:, LANE * (p + 1) : LANE * (p + 2)] = value

    def tile(p):
        return slice(LANE * (p + 1), LANE * (p + 2))

    for c in range(9):
        quarter = []
        for b in range(5):
            v = [full[:, tile(_tile_of(a, b, c))] for a in range(4)]
            even, odd = v[0] + v[2], v[1] + v[3]
            quarter.append((even + odd, even - odd, v[0] - v[2], v[3] - v[1]))
        zero = odd_real_forward([q[0] for q in quarter])
        two = odd_real_forward([q[1] for q in quarter])
        one = odd_complex([(q[2], q[3]) for q in quarter], -1)
        mid[0, c] = zero[0][0]
        mid[1, c] = two[0][0]
        pieces = {(0, 1): zero[1], (0, 2): zero[2], (2, 1): two[1], (2, 2): two[2]}
        for beta in range(5):
            pieces[(1, beta)] = one[beta]
        for key, value in pieces.items():
            row = COMPLEX_ROWS[key]
            mid[row, c] = value[0]
            mid[row + 1, c] = value[1]

    def put(slot, value):
        cos_row = rows_ref[0, slot : slot + 1, :]
        sin_row = rows_ref[1, slot : slot + 1, :]
        where = slice(8 * slot, 8 * slot + 8)
        if value[1] is None:
            stage[where, :LANE] = value[0] * cos_row
            stage[where, LANE:] = -(value[0] * sin_row)
        else:
            stage[where, :LANE] = value[0] * cos_row + value[1] * sin_row
            stage[where, LANE:] = value[1] * cos_row - value[0] * sin_row

    for key, row in REAL_ROWS.items():
        for gamma, value in enumerate(odd_real_forward([mid[row, c] for c in range(9)])):
            put(SLOT[(key[0], key[1], gamma)], value)
    for key, row in COMPLEX_ROWS.items():
        for gamma, value in enumerate(odd_complex([(mid[row, c], mid[row + 1, c]) for c in range(9)], -1)):
            put(SLOT[(key[0], key[1], gamma)], value)

    cut = jnp.broadcast_to(cut_ref[:, 0:1], (8, LANE))
    gain = jnp.broadcast_to(cut_ref[:, 1:2], (8, LANE))
    for start in range(0, COUNT, GROUP):
        where = slice(8 * start, 8 * (start + GROUP))
        spectrum = split_dot(stage[where, :], forward_ref[...])
        scaled = []
        for index in range(GROUP):
            slot = start + index
            wave = rows_ref[2, slot : slot + 1, :]
            decay = rows_ref[3, slot : slot + 1, :]
            factor = jnp.where(wave > cut, gain * decay, np.float32(1.0 / NLON))
            part = spectrum[8 * index : 8 * index + 8, :]
            scaled.append(part * jnp.concatenate([factor, factor], axis=1))
        stage[where, :] = split_dot(jnp.concatenate(scaled, axis=0), inverse_ref[...])

    def take(slot, real):
        cos_row = rows_ref[0, slot : slot + 1, :]
        sin_row = rows_ref[1, slot : slot + 1, :]
        where = slice(8 * slot, 8 * slot + 8)
        re, im = stage[where, :LANE], stage[where, LANE:]
        if real:
            return (re * cos_row - im * sin_row, None)
        return (re * cos_row - im * sin_row, im * cos_row + re * sin_row)

    for key, row in REAL_ROWS.items():
        values = odd_real_inverse([take(SLOT[(key[0], key[1], gamma)], gamma == 0) for gamma in range(5)])
        for c in range(9):
            mid[row, c] = values[c]
    for key, row in COMPLEX_ROWS.items():
        values = odd_complex([take(SLOT[(key[0], key[1], gamma)], False) for gamma in range(9)], 1)
        for c in range(9):
            mid[row, c] = values[c][0]
            mid[row + 1, c] = values[c][1]

    for c in range(9):

        def piece(key):
            row = COMPLEX_ROWS[key]
            return (mid[row, c], mid[row + 1, c])

        zero = odd_real_inverse([(mid[0, c], None), piece((0, 1)), piece((0, 2))])
        two = odd_real_inverse([(mid[1, c], None), piece((2, 1)), piece((2, 2))])
        one = odd_complex([piece((1, beta)) for beta in range(5)], 1)
        for b in range(5):
            even, odd = zero[b] + two[b], zero[b] - two[b]
            re2, im2 = one[b][0] + one[b][0], one[b][1] + one[b][1]
            values = (even + re2, odd - im2, even - re2, odd + im2)
            for a in range(4):
                p = _tile_of(a, b, c)
                full[:, tile(p)] = values[a]
                if p == 0:
                    full[:, tile(TILES)] = values[a]
                if p == TILES - 1:
                    full[:, tile(-1)] = values[a]

    for d in range(sectors):
        first, shift = divmod(LANE + d * span, LANE)
        pieces = []
        for t in range(span // LANE + 2):
            piece = full[:, LANE * (first + t) : LANE * (first + t + 1)]
            pieces.append(pltpu.roll(piece, LANE - shift, 1) if shift else piece)
        west = pieces[0] if shift else full[:, LANE * (first - 1) : LANE * first]
        for t in range(WIDE // LANE):
            value = jnp.where(lane < LANE - shift, pieces[t], pieces[t + 1]) if shift else pieces[t]
            if t == WIDE // LANE - 1:
                value = jnp.where(lane < LANE - LEV, value, west)
            out_ref[d, :, LANE * t : LANE * (t + 1)] = value


def filter_rows(blocks, cuts):
    rows, forward, inverse = tables()
    return pl.pallas_call(
        filter_kernel,
        out_shape=jax.ShapeDtypeStruct((blocks.shape[0], 8, WIDE), jnp.float32),
        in_specs=[pl.BlockSpec(memory_space=pltpu.VMEM)] * 5,
        out_specs=pl.BlockSpec(memory_space=pltpu.VMEM),
        scratch_shapes=[
            pltpu.VMEM((8, (TILES + 2) * LANE), jnp.float32),
            pltpu.VMEM((20, 9, 8, LANE), jnp.float32),
            pltpu.VMEM((8 * COUNT, 2 * LANE), jnp.float32),
        ],
        compiler_params=pltpu.CompilerParams(vmem_limit_bytes=SMALL_GRANT),
        name="polar_filter",
    )(blocks, cuts, jnp.asarray(rows), jnp.asarray(forward), jnp.asarray(inverse))


def pack_kernel(pieces, winds_ref, layer_ref, tracer_ref, out_ref, buffer, in_sem, out_sem):
    blocks = layer_ref.shape[0]
    sources = [(winds_ref, 2 * blocks, 0), (layer_ref, blocks, 2 * blocks), (tracer_ref, blocks, 3 * blocks)]
    size = 4 * blocks // pieces
    inward, outward = [], []
    for ref, count, base in sources:
        for start in range(0, count, size):
            index = (base + start) // size
            here = slice(base + start, base + start + size)
            inward.append(pltpu.make_async_copy(ref.at[start : start + size], buffer.at[here], in_sem.at[index]))
            outward.append(pltpu.make_async_copy(buffer.at[here], out_ref.at[here], out_sem.at[index]))
    for copy in inward:
        copy.start()
    for first, then in zip(inward, outward):
        first.wait()
        then.start()
    for copy in outward:
        copy.wait()


def pack(winds, thickness, tracer):
    row_count, width = thickness.shape
    blocks = row_count // 8
    pieces = 4
    anywhere = pl.BlockSpec(memory_space=pl.ANY)
    return pl.pallas_call(
        functools.partial(pack_kernel, pieces),
        out_shape=jax.ShapeDtypeStruct((4 * blocks, 8, width), jnp.float32),
        in_specs=[anywhere, anywhere, anywhere],
        out_specs=anywhere,
        scratch_shapes=[
            pltpu.VMEM((4 * blocks, 8, width), jnp.float32),
            pltpu.SemaphoreType.DMA((pieces,)),
            pltpu.SemaphoreType.DMA((pieces,)),
        ],
        name="pack",
    )(
        winds.reshape(2 * blocks, 8, width),
        thickness.reshape(blocks, 8, width),
        tracer.reshape(blocks, 8, width),
    )


def stencil_kernel(ratio, even_ref, field_ref, first_ref, second_ref, coef_ref, winds_ref, layer_ref, tracer_ref, tall):
    is_even = even_ref[0] > 0
    first = first_ref[...]
    second = second_ref[...]
    south = jnp.where(is_even, second, first)
    north = jnp.where(is_even, first, second)
    for f in range(3):
        tall[f, 7:8, :] = south[f : f + 1, :]
        tall[f, 72:73, :] = north[f : f + 1, :]
        for g in range(8):
            tall[f, 8 + 8 * g : 16 + 8 * g, :] = field_ref[8 * (f + 1) + g]

    def east(x):
        return pltpu.roll(x, WIDE - LEV, 1)

    def west(x):
        return pltpu.roll(x, LEV, 1)

    span = layer_ref.shape[1]
    for g in range(8):
        rows = slice(8 * g, 8 * g + 8)
        at = 8 + 8 * g
        u = field_ref[g]
        v, h, q = (tall[f, at : at + 8, :] for f in range(3))
        v_s, h_s, q_s = (tall[f, at - 1 : at + 7, :] for f in range(3))
        v_n, h_n, q_n = (tall[f, at + 1 : at + 9, :] for f in range(3))
        zonal = coef_ref[rows, 0:1]
        to_north = coef_ref[rows, 1:2]
        to_south = coef_ref[rows, 2:3]
        slope = coef_ref[rows, 3:4]
        h_e = east(h)
        su = u + east(u)
        fx = su * (h + h_e)
        gx = su * (q + east(q))
        wind_n = (v + v_n) * to_north
        wind_s = (v_s + v) * to_south
        new_h = h - (zonal * (fx - west(fx)) + (wind_n * (h + h_n) - wind_s * (h_s + h)))
        new_q = q - (zonal * (gx - west(gx)) + (wind_n * (q + q_n) - wind_s * (q_s + q)))
        new_u = u - slope * (h_e - west(h))
        new_v = v - np.float32(ratio) * (h_n - h_s)
        winds_ref[0, rows, :] = new_u[:, :span]
        winds_ref[1, rows, :] = new_v[:, :span]
        layer_ref[rows, :] = new_h[:, :span]
        tracer_ref[rows, :] = new_q[:, :span]


def stencil(even, fields, first, second, coef, ratio, row_count, width):
    vmem = pl.BlockSpec(memory_space=pltpu.VMEM)
    return pl.pallas_call(
        functools.partial(stencil_kernel, ratio),
        out_shape=(
            jax.ShapeDtypeStruct((2, row_count, width), jnp.float32),
            jax.ShapeDtypeStruct((row_count, width), jnp.float32),
            jax.ShapeDtypeStruct((row_count, width), jnp.float32),
        ),
        in_specs=[pl.BlockSpec(memory_space=pltpu.SMEM), vmem, vmem, vmem, vmem],
        out_specs=(vmem, vmem, vmem),
        scratch_shapes=[pltpu.VMEM((3, row_count + 16, WIDE), jnp.float32)],
        compiler_params=pltpu.CompilerParams(vmem_limit_bytes=SMALL_GRANT),
        name="stencil",
    )(even, fields, first, second, coef)


def per_device(winds, thickness, tracer, cutoff, damping):
    lat_size = lax.axis_size("lat")
    lon_size = lax.axis_size("lon")
    band = lax.axis_index("lat")
    sector = lax.axis_index("lon")
    row_count, width = thickness.shape
    nlat = row_count * lat_size

    blocks = pack(winds, thickness, tracer)
    owned = lax.all_to_all(blocks, "lon", split_axis=0, concat_axis=0, tiled=True)

    is_polar = (band < lat_size // 4) | (band >= lat_size - lat_size // 4)
    group = sector % (row_count // 8)
    cut = lax.dynamic_slice_in_dim(cutoff.astype(jnp.float32), group * 8, 8)
    damp = lax.dynamic_slice_in_dim(damping, group * 8, 8)
    gain = damp * cut * cut
    cut = jnp.where(is_polar, cut, jnp.float32(NLON))
    cuts = jnp.stack([cut, gain], axis=1)

    filtered = filter_rows(owned, cuts)
    fields = lax.all_to_all(filtered, "lon", split_axis=0, concat_axis=0, tiled=True)

    even = band % 2 == 0
    groups = row_count // 8
    low = jnp.stack([fields[f * groups, 0] for f in (1, 2, 3)])
    high = jnp.stack([fields[f * groups + groups - 1, 7] for f in (1, 2, 3)])
    pairs = {0: [], 1: []}
    for z in range(lat_size):
        for e in range(lon_size):
            here = z * lon_size + e
            across = z * lon_size + (e + lon_size // 2) % lon_size
            up = here + lon_size if z < lat_size - 1 else across
            down = here - lon_size if z > 0 else across
            pairs[0].append((here, up if z % 2 == 0 else down))
            pairs[1].append((here, down if z % 2 == 0 else up))
    first = lax.ppermute(jnp.where(even, high, low), ("lat", "lon"), pairs[0])
    second = lax.ppermute(jnp.where(even, low, high), ("lat", "lon"), pairs[1])

    lon_step = 2.0 * math.pi / NLON
    lat_step = math.pi / nlat
    rows = (band * row_count + jnp.arange(row_count, dtype=jnp.int32)).astype(jnp.float32)
    center = jnp.cos(-math.pi / 2 + (rows + 0.5) * lat_step)
    face = band * row_count + jnp.arange(row_count + 1, dtype=jnp.int32)
    cos_face = jnp.where(
        (face == 0) | (face == nlat), 0.0, jnp.cos(-math.pi / 2 + face.astype(jnp.float32) * lat_step)
    )
    quarter = 0.25 / center
    aspect = lon_step / lat_step
    coef = jnp.stack(
        [quarter, aspect * quarter * cos_face[1:], aspect * quarter * cos_face[:-1], 2.0 * quarter], axis=1
    )
    return stencil(
        even.astype(jnp.int32)[None], fields, first, second, coef, lon_step / (2.0 * lat_step), row_count, width
    )


def solution(mesh):
    placed = (P(None, "lat", "lon"), P("lat", "lon"), P("lat", "lon"), P("lat"), P("lat"))
    return jax.shard_map(
        per_device,
        mesh=mesh,
        in_specs=placed,
        out_specs=(P(None, "lat", "lon"), P("lat", "lon"), P("lat", "lon")),
        check_vma=False,
    )
```

```python
import functools
import math

import jax
import jax.numpy as jnp
import numpy as np
from jax import lax
from jax.experimental import pallas as pl
from jax.experimental.pallas import tpu as pltpu
from jax.sharding import PartitionSpec as P

LEV = 8
NLON = 2880
LANE = 128
TILES = NLON * LEV // LANE
STEP = LANE // LEV
BATCH = 4
SMALL_GRANT = 12 << 20
WIDE = 768


def _lin(terms):
    total = None
    for weight, value in terms:
        if value is None or abs(weight) < 1e-12:
            continue
        if abs(weight - 1.0) < 1e-12:
            item = value
        else:
            item = value * np.float32(weight)
        total = item if total is None else total + item
    return total


def _odd_tables(size):
    half = (size - 1) // 2
    angle = [[2.0 * math.pi * ((j * k) % size) / size for j in range(half + 1)] for k in range(half + 1)]
    return half, angle


def odd_real_forward(values):
    size = len(values)
    half, angle = _odd_tables(size)
    plus = [values[j] + values[size - j] for j in range(1, half + 1)]
    minus = [values[j] - values[size - j] for j in range(1, half + 1)]
    out = [(_lin([(1.0, values[0])] + [(1.0, t) for t in plus]), None)]
    for k in range(1, half + 1):
        real = _lin([(1.0, values[0])] + [(math.cos(angle[k][j]), plus[j - 1]) for j in range(1, half + 1)])
        imag = _lin([(-math.sin(angle[k][j]), minus[j - 1]) for j in range(1, half + 1)])
        out.append((real, imag))
    return out


def odd_real_inverse(bins):
    half = len(bins) - 1
    size = 2 * half + 1
    _, angle = _odd_tables(size)
    doubled = [(b[0] * np.float32(2.0), b[1] * np.float32(2.0)) for b in bins[1:]]
    out = [None] * size
    out[0] = _lin([(1.0, bins[0][0])] + [(1.0, b[0]) for b in doubled])
    for n in range(1, half + 1):
        even = _lin([(1.0, bins[0][0])] + [(math.cos(angle[n][k]), doubled[k - 1][0]) for k in range(1, half + 1)])
        odd = _lin([(math.sin(angle[n][k]), doubled[k - 1][1]) for k in range(1, half + 1)])
        out[n] = even - odd
        out[size - n] = even + odd
    return out


def three(values, sign):
    (ar, ai), (br, bi), (cr, ci) = values
    tr, ti = br + cr, bi + ci
    mr, mi = ar - np.float32(0.5) * tr, ai - np.float32(0.5) * ti
    root = np.float32(sign * math.sqrt(0.75))
    er, ei = root * (br - cr), root * (bi - ci)
    return [(ar + tr, ai + ti), (mr - ei, mi + er), (mr + ei, mi - er)]


def nine(values, sign):
    inner = [three([values[n], values[n + 3], values[n + 6]], sign) for n in range(3)]
    out = [None] * 9
    for k in range(3):
        column = [inner[0][k]]
        for n in (1, 2):
            re, im = inner[n][k]
            if k:
                c = np.float32(math.cos(2.0 * math.pi * n * k / 9))
                s = np.float32(sign * math.sin(2.0 * math.pi * n * k / 9))
                re, im = re * c - im * s, re * s + im * c
            column.append((re, im))
        out[k], out[k + 3], out[k + 6] = three(column, sign)
    return out


def odd_complex(values, sign):
    size = len(values)
    if size == 9:
        return nine(values, sign)
    half, angle = _odd_tables(size)
    out = [None] * size
    plus = [(values[j][0] + values[size - j][0], values[j][1] + values[size - j][1]) for j in range(1, half + 1)]
    minus = [(values[j][0] - values[size - j][0], values[j][1] - values[size - j][1]) for j in range(1, half + 1)]
    out[0] = tuple(_lin([(1.0, values[0][part])] + [(1.0, t[part]) for t in plus]) for part in (0, 1))
    for k in range(1, half + 1):
        base = [
            _lin([(1.0, values[0][part])] + [(math.cos(angle[k][j]), plus[j - 1][part]) for j in range(1, half + 1)])
            for part in (0, 1)
        ]
        turn = [_lin([(math.sin(angle[k][j]), minus[j - 1][part]) for j in range(1, half + 1)]) for part in (0, 1)]
        low = (base[0] + turn[1], base[1] - turn[0])
        high = (base[0] - turn[1], base[1] + turn[0])
        if sign < 0:
            out[k], out[size - k] = low, high
        else:
            out[k], out[size - k] = high, low
    return out


COMPLEX_CLASSES = [(0, 1), (0, 2), (2, 1), (2, 2), (1, 0), (1, 1), (1, 2), (1, 3), (1, 4)]


def _tile_of(a, b, c):
    return (45 * a + 36 * b + 20 * c) % TILES


def _bin_of(alpha, beta, gamma):
    for kappa in range(TILES):
        if kappa % 4 == alpha and kappa % 5 == beta and kappa % 9 == gamma:
            return kappa
    raise ValueError


def _bin_list():
    bins = []
    for alpha in (0, 2):
        bins += [(alpha, 0, gamma) for gamma in range(5)]
    for alpha, beta in COMPLEX_CLASSES:
        bins += [(alpha, beta, gamma) for gamma in range(9)]
    return bins


BINS = _bin_list()
COUNT = len(BINS)
SLOT = {key: index for index, key in enumerate(BINS)}
REAL_ROWS = {(0, 0): 0, (2, 0): 1}
COMPLEX_ROWS = {key: 2 + 2 * index for index, key in enumerate(COMPLEX_CLASSES)}


@functools.lru_cache(maxsize=1)
def tables():
    kappa = np.array([_bin_of(*key) for key in BINS])
    phase = (np.arange(LANE) // LEV)[None, :]
    turn = 2.0 * np.pi * ((kappa[:, None] * phase) % NLON) / NLON
    wave = kappa[:, None] + TILES * phase
    wave = np.minimum(wave, NLON - wave).astype(np.float64)
    rows = np.stack(
        [np.cos(turn), np.sin(turn), wave, 1.0 / (np.maximum(wave, 1.0) ** 2 * NLON)], axis=0
    ).astype(np.float32)
    s = np.arange(LANE) // LEV
    level = np.arange(LANE) % LEV
    same = (level[:, None] == level[None, :]).astype(np.float64)
    angle = 2.0 * np.pi * ((s[:, None] * s[None, :]) % STEP) / STEP
    cosines = np.cos(angle) * same
    sines = np.sin(angle) * same
    forward = np.block([[cosines, -sines], [sines, cosines]]).astype(np.float32)

    def split(matrix):
        high = matrix.astype(jnp.bfloat16)
        low = (matrix - high.astype(np.float32)).astype(jnp.bfloat16)
        return np.concatenate([high, high, low], axis=0)

    return rows, split(forward), split(forward.T)


def split_dot(value, matrix):
    high = value.astype(jnp.bfloat16)
    low = (value - high.astype(jnp.float32)).astype(jnp.bfloat16)
    return jnp.dot(jnp.concatenate([high, low, high], axis=1), matrix, preferred_element_type=jnp.float32)


ALL_CLASSES = [(0, 0), (2, 0)] + COMPLEX_CLASSES
CLASS_CUTS = (0, 4, 6, 8, 11)
CLASS_GROUPS = [ALL_CLASSES[first:last] for first, last in zip(CLASS_CUTS[:-1], CLASS_CUTS[1:])]


def filter_kernel(x_ref, cut_ref, rows_ref, forward_ref, inverse_ref, out_ref, full, mid, stage, result, sem):
    sectors = x_ref.shape[0]
    span = x_ref.shape[2]
    lane = lax.broadcasted_iota(jnp.int32, (8, LANE), 1)
    turned = {}

    def source(d, t):
        if (d, t) not in turned:
            value = x_ref[d, :, LANE * t : min(LANE * (t + 1), span)]
            if value.shape[1] < LANE:
                value = jnp.concatenate([value, jnp.zeros((8, LANE - value.shape[1]), jnp.float32)], axis=1)
            shift = d * span % LANE
            turned[(d, t)] = pltpu.roll(value, shift, 1) if shift else value
        return turned[(d, t)]

    for p in range(TILES):
        edges = []
        for j in range(0, LANE, LEV):
            d, rest = divmod(LANE * p + j, span)
            key = (d, rest // LANE)
            if not edges or edges[-1][1:] != key:
                edges.append((j,) + key)
        value = source(*edges[-1][1:])
        for (_, d, t), (stop, _, _) in reversed(list(zip(edges[:-1], edges[1:]))):
            value = jnp.where(lane < stop, source(d, t), value)
        full[:, LANE * (p + 1) : LANE * (p + 2)] = value

    def tile(p):
        return slice(LANE * (p + 1), LANE * (p + 2))

    for c in range(9):
        quarter = []
        for b in range(5):
            v = [full[:, tile(_tile_of(a, b, c))] for a in range(4)]
            even, odd = v[0] + v[2], v[1] + v[3]
            quarter.append((even + odd, even - odd, v[0] - v[2], v[3] - v[1]))
        zero = odd_real_forward([q[0] for q in quarter])
        two = odd_real_forward([q[1] for q in quarter])
        one = odd_complex([(q[2], q[3]) for q in quarter], -1)
        mid[0, c] = zero[0][0]
        mid[1, c] = two[0][0]
        pieces = {(0, 1): zero[1], (0, 2): zero[2], (2, 1): two[1], (2, 2): two[2]}
        for beta in range(5):
            pieces[(1, beta)] = one[beta]
        for key, value in pieces.items():
            row = COMPLEX_ROWS[key]
            mid[row, c] = value[0]
            mid[row + 1, c] = value[1]

    def put(slot, value):
        cos_row = rows_ref[0, slot : slot + 1, :]
        sin_row = rows_ref[1, slot : slot + 1, :]
        where = slice(8 * slot, 8 * slot + 8)
        if value[1] is None:
            stage[where, :LANE] = value[0] * cos_row
            stage[where, LANE:] = -(value[0] * sin_row)
        else:
            stage[where, :LANE] = value[0] * cos_row + value[1] * sin_row
            stage[where, LANE:] = value[1] * cos_row - value[0] * sin_row

    def take(slot, real):
        cos_row = rows_ref[0, slot : slot + 1, :]
        sin_row = rows_ref[1, slot : slot + 1, :]
        where = slice(8 * slot, 8 * slot + 8)
        re, im = stage[where, :LANE], stage[where, LANE:]
        if real:
            return (re * cos_row - im * sin_row, None)
        return (re * cos_row - im * sin_row, im * cos_row + re * sin_row)

    cut = jnp.broadcast_to(cut_ref[:, 0:1], (8, LANE))
    gain = jnp.broadcast_to(cut_ref[:, 1:2], (8, LANE))
    for classes in CLASS_GROUPS:
        slots = [SLOT[key] for key in BINS if key[:2] in classes]
        start, count = slots[0], len(slots)
        for key in classes:
            if key in REAL_ROWS:
                row = REAL_ROWS[key]
                values = odd_real_forward([mid[row, c] for c in range(9)])
            else:
                row = COMPLEX_ROWS[key]
                values = odd_complex([(mid[row, c], mid[row + 1, c]) for c in range(9)], -1)
            for gamma, value in enumerate(values):
                put(SLOT[key + (gamma,)], value)
        where = slice(8 * start, 8 * (start + count))
        spectrum = split_dot(stage[where, :], forward_ref[...])
        scaled = []
        for index in range(count):
            slot = start + index
            wave = rows_ref[2, slot : slot + 1, :]
            decay = rows_ref[3, slot : slot + 1, :]
            factor = jnp.where(wave > cut, gain * decay, np.float32(1.0 / NLON))
            part = spectrum[8 * index : 8 * index + 8, :]
            scaled.append(part * jnp.concatenate([factor, factor], axis=1))
        stage[where, :] = split_dot(jnp.concatenate(scaled, axis=0), inverse_ref[...])
        for key in classes:
            if key in REAL_ROWS:
                row = REAL_ROWS[key]
                values = odd_real_inverse([take(SLOT[key + (gamma,)], gamma == 0) for gamma in range(5)])
                for c in range(9):
                    mid[row, c] = values[c]
            else:
                row = COMPLEX_ROWS[key]
                values = odd_complex([take(SLOT[key + (gamma,)], False) for gamma in range(9)], 1)
                for c in range(9):
                    mid[row, c] = values[c][0]
                    mid[row + 1, c] = values[c][1]

    for c in range(9):

        def piece(key):
            row = COMPLEX_ROWS[key]
            return (mid[row, c], mid[row + 1, c])

        zero = odd_real_inverse([(mid[0, c], None), piece((0, 1)), piece((0, 2))])
        two = odd_real_inverse([(mid[1, c], None), piece((2, 1)), piece((2, 2))])
        one = odd_complex([piece((1, beta)) for beta in range(5)], 1)
        for b in range(5):
            even, odd = zero[b] + two[b], zero[b] - two[b]
            re2, im2 = one[b][0] + one[b][0], one[b][1] + one[b][1]
            values = (even + re2, odd - im2, even - re2, odd + im2)
            for a in range(4):
                p = _tile_of(a, b, c)
                full[:, tile(p)] = values[a]
                if p == 0:
                    full[:, tile(TILES)] = values[a]
                if p == TILES - 1:
                    full[:, tile(-1)] = values[a]

    writes = []
    for d in range(sectors):
        first, shift = divmod(LANE + d * span, LANE)
        pieces = []
        for t in range(span // LANE + 2):
            piece = full[:, LANE * (first + t) : LANE * (first + t + 1)]
            pieces.append(pltpu.roll(piece, LANE - shift, 1) if shift else piece)
        west = pieces[0] if shift else full[:, LANE * (first - 1) : LANE * first]
        for t in range(WIDE // LANE):
            value = jnp.where(lane < LANE - shift, pieces[t], pieces[t + 1]) if shift else pieces[t]
            if t == WIDE // LANE - 1:
                value = jnp.where(lane < LANE - LEV, value, west)
            result[d, :, LANE * t : LANE * (t + 1)] = value
        if d % BATCH == BATCH - 1:
            here = slice(d + 1 - BATCH, d + 1)
            writes.append(pltpu.make_async_copy(result.at[here], out_ref.at[here], sem.at[d // BATCH]))
            writes[-1].start()
    for write in writes:
        write.wait()


def filter_rows(blocks, cuts):
    rows, forward, inverse = tables()
    return pl.pallas_call(
        filter_kernel,
        out_shape=jax.ShapeDtypeStruct((blocks.shape[0], 8, WIDE), jnp.float32),
        in_specs=[pl.BlockSpec(memory_space=pltpu.VMEM)] * 5,
        out_specs=pl.BlockSpec(memory_space=pl.ANY),
        scratch_shapes=[
            pltpu.VMEM((8, (TILES + 2) * LANE), jnp.float32),
            pltpu.VMEM((20, 9, 8, LANE), jnp.float32),
            pltpu.VMEM((8 * COUNT, 2 * LANE), jnp.float32),
            pltpu.VMEM((blocks.shape[0], 8, WIDE), jnp.float32),
            pltpu.SemaphoreType.DMA((blocks.shape[0] // BATCH,)),
        ],
        compiler_params=pltpu.CompilerParams(vmem_limit_bytes=SMALL_GRANT),
        name="polar_filter",
    )(blocks, cuts, jnp.asarray(rows), jnp.asarray(forward), jnp.asarray(inverse))


def pack_kernel(pieces, winds_ref, layer_ref, tracer_ref, out_ref, buffer, in_sem, out_sem):
    blocks = layer_ref.shape[0]
    sources = [(winds_ref, 2 * blocks, 0), (layer_ref, blocks, 2 * blocks), (tracer_ref, blocks, 3 * blocks)]
    size = 4 * blocks // pieces
    inward, outward = [], []
    for ref, count, base in sources:
        for start in range(0, count, size):
            index = (base + start) // size
            here = slice(base + start, base + start + size)
            inward.append(pltpu.make_async_copy(ref.at[start : start + size], buffer.at[here], in_sem.at[index]))
            outward.append(pltpu.make_async_copy(buffer.at[here], out_ref.at[here], out_sem.at[index]))
    for copy in inward:
        copy.start()
    for first, then in zip(inward, outward):
        first.wait()
        then.start()
    for copy in outward:
        copy.wait()


def pack(winds, thickness, tracer):
    row_count, width = thickness.shape
    blocks = row_count // 8
    pieces = 4
    anywhere = pl.BlockSpec(memory_space=pl.ANY)
    return pl.pallas_call(
        functools.partial(pack_kernel, pieces),
        out_shape=jax.ShapeDtypeStruct((4 * blocks, 8, width), jnp.float32),
        in_specs=[anywhere, anywhere, anywhere],
        out_specs=anywhere,
        scratch_shapes=[
            pltpu.VMEM((4 * blocks, 8, width), jnp.float32),
            pltpu.SemaphoreType.DMA((pieces,)),
            pltpu.SemaphoreType.DMA((pieces,)),
        ],
        name="pack",
    )(
        winds.reshape(2 * blocks, 8, width),
        thickness.reshape(blocks, 8, width),
        tracer.reshape(blocks, 8, width),
    )


def east(x):
    return pltpu.roll(x, WIDE - LEV, 1)


def west(x):
    return pltpu.roll(x, LEV, 1)


def update(ratio, u, mid_rows, south_rows, north_rows, coef):
    v, h, q = mid_rows
    v_s, h_s, q_s = south_rows
    v_n, h_n, q_n = north_rows
    zonal, to_north, to_south, slope = (coef[:, k : k + 1] for k in range(4))
    h_e = east(h)
    su = u + east(u)
    fx = su * (h + h_e)
    gx = su * (q + east(q))
    wind_n = (v + v_n) * to_north
    wind_s = (v_s + v) * to_south
    new_h = h - (zonal * (fx - west(fx)) + (wind_n * (h + h_n) - wind_s * (h_s + h)))
    new_q = q - (zonal * (gx - west(gx)) + (wind_n * (q + q_n) - wind_s * (q_s + q)))
    new_v = v - np.float32(ratio) * (h_n - h_s)
    return slope * (h_e - west(h)), new_v, new_h, new_q


def main_kernel(ratio, field_ref, coef_ref, winds_ref, layer_ref, tracer_ref):
    groups = field_ref.shape[0] // 4
    span = layer_ref.shape[1]
    sub = lax.broadcasted_iota(jnp.int32, (8, WIDE), 0)

    def shifted(f, g):
        x = field_ref[groups * f + g]
        below = field_ref[groups * f + max(g - 1, 0)]
        above = field_ref[groups * f + min(g + 1, groups - 1)]
        south = jnp.where(sub == 0, pltpu.roll(below, 1, 0), pltpu.roll(x, 1, 0))
        north = jnp.where(sub == 7, pltpu.roll(above, 7, 0), pltpu.roll(x, 7, 0))
        return x, south, north

    for g in range(groups):
        rows = slice(8 * g, 8 * g + 8)
        u = field_ref[g]
        mid_rows, south_rows, north_rows = zip(*(shifted(f, g) for f in (1, 2, 3)))
        du, new_v, new_h, new_q = update(ratio, u, mid_rows, south_rows, north_rows, coef_ref[rows, :])
        winds_ref[0, rows, :] = (u - du)[:, :span]
        winds_ref[1, rows, :] = new_v[:, :span]
        layer_ref[rows, :] = new_h[:, :span]
        tracer_ref[rows, :] = new_q[:, :span]


def edge_kernel(
    ratio, even_ref, field_ref, first_ref, second_ref, coef_ref, w_in, l_in, t_in, winds_ref, layer_ref, tracer_ref, out, sem
):
    del w_in, l_in, t_in
    groups = field_ref.shape[0] // 4
    is_even = even_ref[0] > 0
    span = layer_ref.shape[1]
    sub = lax.broadcasted_iota(jnp.int32, (8, WIDE), 0)
    writes = []
    for side, g in enumerate((0, groups - 1)):
        rows = slice(8 * g, 8 * g + 8)
        near, far = (second_ref, first_ref) if side == 0 else (first_ref, second_ref)
        mid_rows, south_rows, north_rows = [], [], []
        for f in (1, 2, 3):
            x = field_ref[groups * f + g]
            halo = jnp.where(is_even, near[f - 1 : f, :], far[f - 1 : f, :])
            if side == 0:
                south = jnp.where(sub == 0, halo, pltpu.roll(x, 1, 0))
                north = jnp.where(sub == 7, pltpu.roll(field_ref[groups * f + g + 1], 7, 0), pltpu.roll(x, 7, 0))
            else:
                south = jnp.where(sub == 0, pltpu.roll(field_ref[groups * f + g - 1], 1, 0), pltpu.roll(x, 1, 0))
                north = jnp.where(sub == 7, halo, pltpu.roll(x, 7, 0))
            mid_rows.append(x)
            south_rows.append(south)
            north_rows.append(north)
        _, new_v, new_h, new_q = update(ratio, field_ref[g], mid_rows, south_rows, north_rows, coef_ref[rows, :])
        for k, (value, target) in enumerate(
            ((new_v, winds_ref.at[1, rows]), (new_h, layer_ref.at[rows]), (new_q, tracer_ref.at[rows]))
        ):
            out[side, k] = value[:, :span]
            writes.append(pltpu.make_async_copy(out.at[side, k], target, sem.at[side, k]))
            writes[-1].start()
    for write in writes:
        write.wait()


def stencil_main(fields, coef, ratio, row_count, width):
    vmem = pl.BlockSpec(memory_space=pltpu.VMEM)
    return pl.pallas_call(
        functools.partial(main_kernel, ratio),
        out_shape=(
            jax.ShapeDtypeStruct((2, row_count, width), jnp.float32),
            jax.ShapeDtypeStruct((row_count, width), jnp.float32),
            jax.ShapeDtypeStruct((row_count, width), jnp.float32),
        ),
        in_specs=[vmem, vmem],
        out_specs=(vmem, vmem, vmem),
        compiler_params=pltpu.CompilerParams(vmem_limit_bytes=SMALL_GRANT),
        cost_estimate=pl.CostEstimate(flops=10_000_000, bytes_accessed=1_600_000, transcendentals=0),
        name="stencil_main",
    )(fields, coef)


def stencil_edge(even, fields, first, second, coef, outs, ratio):
    vmem = pl.BlockSpec(memory_space=pltpu.VMEM)
    anywhere = pl.BlockSpec(memory_space=pl.ANY)
    width = outs[1].shape[1]
    return pl.pallas_call(
        functools.partial(edge_kernel, ratio),
        out_shape=tuple(jax.ShapeDtypeStruct(out.shape, jnp.float32) for out in outs),
        in_specs=[pl.BlockSpec(memory_space=pltpu.SMEM), vmem, vmem, vmem, vmem, anywhere, anywhere, anywhere],
        out_specs=(anywhere, anywhere, anywhere),
        scratch_shapes=[pltpu.VMEM((2, 3, 8, width), jnp.float32), pltpu.SemaphoreType.DMA((2, 3))],
        input_output_aliases={5: 0, 6: 1, 7: 2},
        compiler_params=pltpu.CompilerParams(vmem_limit_bytes=SMALL_GRANT),
        name="stencil_edge",
    )(even, fields, first, second, coef, *outs)


def per_device(winds, thickness, tracer, cutoff, damping):
    lat_size = lax.axis_size("lat")
    lon_size = lax.axis_size("lon")
    band = lax.axis_index("lat")
    sector = lax.axis_index("lon")
    row_count, width = thickness.shape
    nlat = row_count * lat_size

    blocks = pack(winds, thickness, tracer)
    owned = lax.all_to_all(blocks, "lon", split_axis=0, concat_axis=0, tiled=True)

    is_polar = (band < lat_size // 4) | (band >= lat_size - lat_size // 4)
    group = sector % (row_count // 8)
    cut = lax.dynamic_slice_in_dim(cutoff.astype(jnp.float32), group * 8, 8)
    damp = lax.dynamic_slice_in_dim(damping, group * 8, 8)
    gain = damp * cut * cut
    cut = jnp.where(is_polar, cut, jnp.float32(NLON))
    cuts = jnp.stack([cut, gain], axis=1)

    filtered = filter_rows(owned, cuts)
    fields = lax.all_to_all(filtered, "lon", split_axis=0, concat_axis=0, tiled=True)

    even = band % 2 == 0
    groups = row_count // 8
    low = jnp.stack([fields[f * groups, 0] for f in (1, 2, 3)])
    high = jnp.stack([fields[f * groups + groups - 1, 7] for f in (1, 2, 3)])
    pairs = {0: [], 1: []}
    for z in range(lat_size):
        for e in range(lon_size):
            here = z * lon_size + e
            across = z * lon_size + (e + lon_size // 2) % lon_size
            up = here + lon_size if z < lat_size - 1 else across
            down = here - lon_size if z > 0 else across
            pairs[0].append((here, up if z % 2 == 0 else down))
            pairs[1].append((here, down if z % 2 == 0 else up))
    first = lax.ppermute(jnp.where(even, high, low), ("lat", "lon"), pairs[0])
    second = lax.ppermute(jnp.where(even, low, high), ("lat", "lon"), pairs[1])

    lon_step = 2.0 * math.pi / NLON
    lat_step = math.pi / nlat
    rows = (band * row_count + jnp.arange(row_count, dtype=jnp.int32)).astype(jnp.float32)
    center = jnp.cos(-math.pi / 2 + (rows + 0.5) * lat_step)
    face = band * row_count + jnp.arange(row_count + 1, dtype=jnp.int32)
    cos_face = jnp.where(
        (face == 0) | (face == nlat), 0.0, jnp.cos(-math.pi / 2 + face.astype(jnp.float32) * lat_step)
    )
    quarter = 0.25 / center
    aspect = lon_step / lat_step
    coef = jnp.stack(
        [quarter, aspect * quarter * cos_face[1:], aspect * quarter * cos_face[:-1], 2.0 * quarter], axis=1
    )
    ratio = lon_step / (2.0 * lat_step)
    outs = stencil_main(fields, coef, ratio, row_count, width)
    return stencil_edge(even.astype(jnp.int32)[None], fields, first, second, coef, outs, ratio)


def solution(mesh):
    placed = (P(None, "lat", "lon"), P("lat", "lon"), P("lat", "lon"), P("lat"), P("lat"))
    return jax.shard_map(
        per_device,
        mesh=mesh,
        in_specs=placed,
        out_specs=(P(None, "lat", "lon"), P("lat", "lon"), P("lat", "lon")),
        check_vma=False,
    )
```

```python
import functools
import math

import jax
import jax.numpy as jnp
import numpy as np
from jax import lax
from jax.experimental import pallas as pl
from jax.experimental.pallas import tpu as pltpu
from jax.sharding import PartitionSpec as P

LEV = 8
NLON = 2880
LANE = 128
TILES = NLON * LEV // LANE
STEP = LANE // LEV
BATCH = 4
SMALL_GRANT = 12 << 20
WIDE = 768


def _lin(terms):
    total = None
    for weight, value in terms:
        if value is None or abs(weight) < 1e-12:
            continue
        if abs(weight - 1.0) < 1e-12:
            item = value
        else:
            item = value * np.float32(weight)
        total = item if total is None else total + item
    return total


def _odd_tables(size):
    half = (size - 1) // 2
    angle = [[2.0 * math.pi * ((j * k) % size) / size for j in range(half + 1)] for k in range(half + 1)]
    return half, angle


def odd_real_forward(values):
    size = len(values)
    half, angle = _odd_tables(size)
    plus = [values[j] + values[size - j] for j in range(1, half + 1)]
    minus = [values[j] - values[size - j] for j in range(1, half + 1)]
    out = [(_lin([(1.0, values[0])] + [(1.0, t) for t in plus]), None)]
    for k in range(1, half + 1):
        real = _lin([(1.0, values[0])] + [(math.cos(angle[k][j]), plus[j - 1]) for j in range(1, half + 1)])
        imag = _lin([(-math.sin(angle[k][j]), minus[j - 1]) for j in range(1, half + 1)])
        out.append((real, imag))
    return out


def odd_real_inverse(bins):
    half = len(bins) - 1
    size = 2 * half + 1
    _, angle = _odd_tables(size)
    doubled = [(b[0] * np.float32(2.0), b[1] * np.float32(2.0)) for b in bins[1:]]
    out = [None] * size
    out[0] = _lin([(1.0, bins[0][0])] + [(1.0, b[0]) for b in doubled])
    for n in range(1, half + 1):
        even = _lin([(1.0, bins[0][0])] + [(math.cos(angle[n][k]), doubled[k - 1][0]) for k in range(1, half + 1)])
        odd = _lin([(math.sin(angle[n][k]), doubled[k - 1][1]) for k in range(1, half + 1)])
        out[n] = even - odd
        out[size - n] = even + odd
    return out


def three(values, sign):
    (ar, ai), (br, bi), (cr, ci) = values
    tr, ti = br + cr, bi + ci
    mr, mi = ar - np.float32(0.5) * tr, ai - np.float32(0.5) * ti
    root = np.float32(sign * math.sqrt(0.75))
    er, ei = root * (br - cr), root * (bi - ci)
    return [(ar + tr, ai + ti), (mr - ei, mi + er), (mr + ei, mi - er)]


def nine(values, sign):
    inner = [three([values[n], values[n + 3], values[n + 6]], sign) for n in range(3)]
    out = [None] * 9
    for k in range(3):
        column = [inner[0][k]]
        for n in (1, 2):
            re, im = inner[n][k]
            if k:
                c = np.float32(math.cos(2.0 * math.pi * n * k / 9))
                s = np.float32(sign * math.sin(2.0 * math.pi * n * k / 9))
                re, im = re * c - im * s, re * s + im * c
            column.append((re, im))
        out[k], out[k + 3], out[k + 6] = three(column, sign)
    return out


def odd_complex(values, sign):
    size = len(values)
    if size == 9:
        return nine(values, sign)
    half, angle = _odd_tables(size)
    out = [None] * size
    plus = [(values[j][0] + values[size - j][0], values[j][1] + values[size - j][1]) for j in range(1, half + 1)]
    minus = [(values[j][0] - values[size - j][0], values[j][1] - values[size - j][1]) for j in range(1, half + 1)]
    out[0] = tuple(_lin([(1.0, values[0][part])] + [(1.0, t[part]) for t in plus]) for part in (0, 1))
    for k in range(1, half + 1):
        base = [
            _lin([(1.0, values[0][part])] + [(math.cos(angle[k][j]), plus[j - 1][part]) for j in range(1, half + 1)])
            for part in (0, 1)
        ]
        turn = [_lin([(math.sin(angle[k][j]), minus[j - 1][part]) for j in range(1, half + 1)]) for part in (0, 1)]
        low = (base[0] + turn[1], base[1] - turn[0])
        high = (base[0] - turn[1], base[1] + turn[0])
        if sign < 0:
            out[k], out[size - k] = low, high
        else:
            out[k], out[size - k] = high, low
    return out


COMPLEX_CLASSES = [(0, 1), (0, 2), (2, 1), (2, 2), (1, 0), (1, 1), (1, 2), (1, 3), (1, 4)]


def _tile_of(a, b, c):
    return (45 * a + 36 * b + 20 * c) % TILES


def _bin_of(alpha, beta, gamma):
    for kappa in range(TILES):
        if kappa % 4 == alpha and kappa % 5 == beta and kappa % 9 == gamma:
            return kappa
    raise ValueError


def _bin_list():
    bins = []
    for alpha in (0, 2):
        bins += [(alpha, 0, gamma) for gamma in range(5)]
    for alpha, beta in COMPLEX_CLASSES:
        bins += [(alpha, beta, gamma) for gamma in range(9)]
    return bins


BINS = _bin_list()
COUNT = len(BINS)
SLOT = {key: index for index, key in enumerate(BINS)}
REAL_ROWS = {(0, 0): 0, (2, 0): 1}
COMPLEX_ROWS = {key: 2 + 2 * index for index, key in enumerate(COMPLEX_CLASSES)}


@functools.lru_cache(maxsize=1)
def tables():
    kappa = np.array([_bin_of(*key) for key in BINS])
    phase = (np.arange(LANE) // LEV)[None, :]
    turn = 2.0 * np.pi * ((kappa[:, None] * phase) % NLON) / NLON
    wave = kappa[:, None] + TILES * phase
    wave = np.minimum(wave, NLON - wave).astype(np.float64)
    rows = np.stack(
        [np.cos(turn), np.sin(turn), wave, 1.0 / (np.maximum(wave, 1.0) ** 2 * NLON)], axis=0
    ).astype(np.float32)
    s = np.arange(LANE) // LEV
    level = np.arange(LANE) % LEV
    same = (level[:, None] == level[None, :]).astype(np.float64)
    angle = 2.0 * np.pi * ((s[:, None] * s[None, :]) % STEP) / STEP
    cosines = np.cos(angle) * same
    sines = np.sin(angle) * same
    forward = np.block([[cosines, -sines], [sines, cosines]]).astype(np.float32)

    def split(matrix):
        high = matrix.astype(jnp.bfloat16)
        low = (matrix - high.astype(np.float32)).astype(jnp.bfloat16)
        return np.concatenate([high, high, low], axis=0)

    return rows, split(forward), split(forward.T)


def split_dot(value, matrix):
    high = value.astype(jnp.bfloat16)
    low = (value - high.astype(jnp.float32)).astype(jnp.bfloat16)
    return jnp.dot(jnp.concatenate([high, low, high], axis=1), matrix, preferred_element_type=jnp.float32)


ALL_CLASSES = [(0, 0), (2, 0)] + COMPLEX_CLASSES
CLASS_CUTS = (0, 4, 6, 8, 11)
CLASS_GROUPS = [ALL_CLASSES[first:last] for first, last in zip(CLASS_CUTS[:-1], CLASS_CUTS[1:])]


def filter_kernel(x_ref, cut_ref, rows_ref, forward_ref, inverse_ref, out_ref, full, mid, stage, result, sem):
    sectors = x_ref.shape[0]
    span = x_ref.shape[2]
    lane = lax.broadcasted_iota(jnp.int32, (8, LANE), 1)
    turned = {}

    def source(d, t):
        if (d, t) not in turned:
            value = x_ref[d, :, LANE * t : min(LANE * (t + 1), span)]
            if value.shape[1] < LANE:
                value = jnp.concatenate([value, jnp.zeros((8, LANE - value.shape[1]), jnp.float32)], axis=1)
            shift = d * span % LANE
            turned[(d, t)] = pltpu.roll(value, shift, 1) if shift else value
        return turned[(d, t)]

    for p in range(TILES):
        edges = []
        for j in range(0, LANE, LEV):
            d, rest = divmod(LANE * p + j, span)
            key = (d, rest // LANE)
            if not edges or edges[-1][1:] != key:
                edges.append((j,) + key)
        value = source(*edges[-1][1:])
        for (_, d, t), (stop, _, _) in reversed(list(zip(edges[:-1], edges[1:]))):
            value = jnp.where(lane < stop, source(d, t), value)
        full[:, LANE * (p + 1) : LANE * (p + 2)] = value

    def tile(p):
        return slice(LANE * (p + 1), LANE * (p + 2))

    for c in range(9):
        quarter = []
        for b in range(5):
            v = [full[:, tile(_tile_of(a, b, c))] for a in range(4)]
            even, odd = v[0] + v[2], v[1] + v[3]
            quarter.append((even + odd, even - odd, v[0] - v[2], v[3] - v[1]))
        zero = odd_real_forward([q[0] for q in quarter])
        two = odd_real_forward([q[1] for q in quarter])
        one = odd_complex([(q[2], q[3]) for q in quarter], -1)
        mid[0, c] = zero[0][0]
        mid[1, c] = two[0][0]
        pieces = {(0, 1): zero[1], (0, 2): zero[2], (2, 1): two[1], (2, 2): two[2]}
        for beta in range(5):
            pieces[(1, beta)] = one[beta]
        for key, value in pieces.items():
            row = COMPLEX_ROWS[key]
            mid[row, c] = value[0]
            mid[row + 1, c] = value[1]

    def put(slot, value):
        cos_row = rows_ref[0, slot : slot + 1, :]
        sin_row = rows_ref[1, slot : slot + 1, :]
        where = slice(8 * slot, 8 * slot + 8)
        if value[1] is None:
            stage[where, :LANE] = value[0] * cos_row
            stage[where, LANE:] = -(value[0] * sin_row)
        else:
            stage[where, :LANE] = value[0] * cos_row + value[1] * sin_row
            stage[where, LANE:] = value[1] * cos_row - value[0] * sin_row

    def take(slot, real):
        cos_row = rows_ref[0, slot : slot + 1, :]
        sin_row = rows_ref[1, slot : slot + 1, :]
        where = slice(8 * slot, 8 * slot + 8)
        re, im = stage[where, :LANE], stage[where, LANE:]
        if real:
            return (re * cos_row - im * sin_row, None)
        return (re * cos_row - im * sin_row, im * cos_row + re * sin_row)

    cut = jnp.broadcast_to(cut_ref[:, 0:1], (8, LANE))
    gain = jnp.broadcast_to(cut_ref[:, 1:2], (8, LANE))
    for classes in CLASS_GROUPS:
        slots = [SLOT[key] for key in BINS if key[:2] in classes]
        start, count = slots[0], len(slots)
        for key in classes:
            if key in REAL_ROWS:
                row = REAL_ROWS[key]
                values = odd_real_forward([mid[row, c] for c in range(9)])
            else:
                row = COMPLEX_ROWS[key]
                values = odd_complex([(mid[row, c], mid[row + 1, c]) for c in range(9)], -1)
            for gamma, value in enumerate(values):
                put(SLOT[key + (gamma,)], value)
        where = slice(8 * start, 8 * (start + count))
        spectrum = split_dot(stage[where, :], forward_ref[...])
        scaled = []
        for index in range(count):
            slot = start + index
            wave = rows_ref[2, slot : slot + 1, :]
            decay = rows_ref[3, slot : slot + 1, :]
            factor = jnp.where(wave > cut, gain * decay, np.float32(1.0 / NLON))
            part = spectrum[8 * index : 8 * index + 8, :]
            scaled.append(part * jnp.concatenate([factor, factor], axis=1))
        stage[where, :] = split_dot(jnp.concatenate(scaled, axis=0), inverse_ref[...])
        for key in classes:
            if key in REAL_ROWS:
                row = REAL_ROWS[key]
                values = odd_real_inverse([take(SLOT[key + (gamma,)], gamma == 0) for gamma in range(5)])
                for c in range(9):
                    mid[row, c] = values[c]
            else:
                row = COMPLEX_ROWS[key]
                values = odd_complex([take(SLOT[key + (gamma,)], False) for gamma in range(9)], 1)
                for c in range(9):
                    mid[row, c] = values[c][0]
                    mid[row + 1, c] = values[c][1]

    for c in range(9):

        def piece(key):
            row = COMPLEX_ROWS[key]
            return (mid[row, c], mid[row + 1, c])

        zero = odd_real_inverse([(mid[0, c], None), piece((0, 1)), piece((0, 2))])
        two = odd_real_inverse([(mid[1, c], None), piece((2, 1)), piece((2, 2))])
        one = odd_complex([piece((1, beta)) for beta in range(5)], 1)
        for b in range(5):
            even, odd = zero[b] + two[b], zero[b] - two[b]
            re2, im2 = one[b][0] + one[b][0], one[b][1] + one[b][1]
            values = (even + re2, odd - im2, even - re2, odd + im2)
            for a in range(4):
                p = _tile_of(a, b, c)
                full[:, tile(p)] = values[a]
                if p == 0:
                    full[:, tile(TILES)] = values[a]
                if p == TILES - 1:
                    full[:, tile(-1)] = values[a]

    writes = []
    for d in range(sectors):
        first, shift = divmod(LANE + d * span, LANE)
        pieces = []
        for t in range(span // LANE + 2):
            piece = full[:, LANE * (first + t) : LANE * (first + t + 1)]
            pieces.append(pltpu.roll(piece, LANE - shift, 1) if shift else piece)
        west = pieces[0] if shift else full[:, LANE * (first - 1) : LANE * first]
        for t in range(WIDE // LANE):
            value = jnp.where(lane < LANE - shift, pieces[t], pieces[t + 1]) if shift else pieces[t]
            if t == WIDE // LANE - 1:
                value = jnp.where(lane < LANE - LEV, value, west)
            result[d, :, LANE * t : LANE * (t + 1)] = value
        if d % BATCH == BATCH - 1:
            here = slice(d + 1 - BATCH, d + 1)
            writes.append(pltpu.make_async_copy(result.at[here], out_ref.at[here], sem.at[d // BATCH]))
            writes[-1].start()
    for write in writes:
        write.wait()


def filter_rows(blocks, cuts):
    rows, forward, inverse = tables()
    return pl.pallas_call(
        filter_kernel,
        out_shape=jax.ShapeDtypeStruct((blocks.shape[0], 8, WIDE), jnp.float32),
        in_specs=[pl.BlockSpec(memory_space=pltpu.VMEM)] * 5,
        out_specs=pl.BlockSpec(memory_space=pl.ANY),
        scratch_shapes=[
            pltpu.VMEM((8, (TILES + 2) * LANE), jnp.float32),
            pltpu.VMEM((20, 9, 8, LANE), jnp.float32),
            pltpu.VMEM((8 * COUNT, 2 * LANE), jnp.float32),
            pltpu.VMEM((blocks.shape[0], 8, WIDE), jnp.float32),
            pltpu.SemaphoreType.DMA((blocks.shape[0] // BATCH,)),
        ],
        compiler_params=pltpu.CompilerParams(vmem_limit_bytes=SMALL_GRANT),
        name="polar_filter",
    )(blocks, cuts, jnp.asarray(rows), jnp.asarray(forward), jnp.asarray(inverse))


def pack_kernel(pieces, winds_ref, layer_ref, tracer_ref, out_ref, buffer, in_sem, out_sem):
    blocks = layer_ref.shape[0]
    sources = [(winds_ref, 2 * blocks, 0), (layer_ref, blocks, 2 * blocks), (tracer_ref, blocks, 3 * blocks)]
    size = 4 * blocks // pieces
    inward, outward = [], []
    for ref, count, base in sources:
        for start in range(0, count, size):
            index = (base + start) // size
            here = slice(base + start, base + start + size)
            inward.append(pltpu.make_async_copy(ref.at[start : start + size], buffer.at[here], in_sem.at[index]))
            outward.append(pltpu.make_async_copy(buffer.at[here], out_ref.at[here], out_sem.at[index]))
    for copy in inward:
        copy.start()
    for first, then in zip(inward, outward):
        first.wait()
        then.start()
    for copy in outward:
        copy.wait()


def pack(winds, thickness, tracer):
    row_count, width = thickness.shape
    blocks = row_count // 8
    pieces = 4
    anywhere = pl.BlockSpec(memory_space=pl.ANY)
    return pl.pallas_call(
        functools.partial(pack_kernel, pieces),
        out_shape=jax.ShapeDtypeStruct((4 * blocks, 8, width), jnp.float32),
        in_specs=[anywhere, anywhere, anywhere],
        out_specs=anywhere,
        scratch_shapes=[
            pltpu.VMEM((4 * blocks, 8, width), jnp.float32),
            pltpu.SemaphoreType.DMA((pieces,)),
            pltpu.SemaphoreType.DMA((pieces,)),
        ],
        name="pack",
    )(
        winds.reshape(2 * blocks, 8, width),
        thickness.reshape(blocks, 8, width),
        tracer.reshape(blocks, 8, width),
    )


def east(x):
    return pltpu.roll(x, WIDE - LEV, 1)


def west(x):
    return pltpu.roll(x, LEV, 1)


def update(ratio, u, mid_rows, south_rows, north_rows, coef):
    v, h, q = mid_rows
    v_s, h_s, q_s = south_rows
    v_n, h_n, q_n = north_rows
    zonal, to_north, to_south, slope = (coef[:, k : k + 1] for k in range(4))
    h_e = east(h)
    su = u + east(u)
    fx = su * (h + h_e)
    gx = su * (q + east(q))
    wind_n = (v + v_n) * to_north
    wind_s = (v_s + v) * to_south
    new_h = h - (zonal * (fx - west(fx)) + (wind_n * (h + h_n) - wind_s * (h_s + h)))
    new_q = q - (zonal * (gx - west(gx)) + (wind_n * (q + q_n) - wind_s * (q_s + q)))
    new_v = v - np.float32(ratio) * (h_n - h_s)
    return slope * (h_e - west(h)), new_v, new_h, new_q


def main_kernel(ratio, field_ref, coef_ref, winds_ref, layer_ref, tracer_ref, out, sem):
    groups = field_ref.shape[0] // 4
    span = layer_ref.shape[1]
    sub = lax.broadcasted_iota(jnp.int32, (8, WIDE), 0)
    writes = []

    def write(k, g, value, target):
        out[k, g] = value[:, :span]
        writes.append(pltpu.make_async_copy(out.at[k, g], target, sem.at[k, g]))
        writes[-1].start()

    def shifted(f, g):
        x = field_ref[groups * f + g]
        south = jnp.where(sub == 0, pltpu.roll(field_ref[groups * f + g - 1], 1, 0), pltpu.roll(x, 1, 0))
        north = jnp.where(sub == 7, pltpu.roll(field_ref[groups * f + g + 1], 7, 0), pltpu.roll(x, 7, 0))
        return x, south, north

    for g in range(groups):
        rows = slice(8 * g, 8 * g + 8)
        u = field_ref[g]
        if 0 < g < groups - 1:
            mid_rows, south_rows, north_rows = zip(*(shifted(f, g) for f in (1, 2, 3)))
            du, new_v, new_h, new_q = update(ratio, u, mid_rows, south_rows, north_rows, coef_ref[rows, :])
            write(1, g, new_v, winds_ref.at[1, rows])
            write(2, g, new_h, layer_ref.at[rows])
            write(3, g, new_q, tracer_ref.at[rows])
        else:
            h = field_ref[2 * groups + g]
            du = coef_ref[rows, 3:4] * (east(h) - west(h))
        write(0, g, u - du, winds_ref.at[0, rows])
    for copy in writes:
        copy.wait()


def edge_kernel(
    ratio, even_ref, field_ref, second_ref, first_ref, coef_ref, w_in, l_in, t_in, winds_ref, layer_ref, tracer_ref, out, sem
):
    del w_in, l_in, t_in
    groups = field_ref.shape[0] // 4
    is_even = even_ref[0] > 0
    span = layer_ref.shape[1]
    sub = lax.broadcasted_iota(jnp.int32, (8, WIDE), 0)
    writes = []
    for side, g in enumerate((0, groups - 1)):
        rows = slice(8 * g, 8 * g + 8)
        near, far = (second_ref, first_ref) if side == 0 else (first_ref, second_ref)
        mid_rows, south_rows, north_rows = [], [], []
        for f in (1, 2, 3):
            x = field_ref[groups * f + g]
            halo = jnp.where(is_even, near[f - 1 : f, :], far[f - 1 : f, :])
            if side == 0:
                south = jnp.where(sub == 0, halo, pltpu.roll(x, 1, 0))
                north = jnp.where(sub == 7, pltpu.roll(field_ref[groups * f + g + 1], 7, 0), pltpu.roll(x, 7, 0))
            else:
                south = jnp.where(sub == 0, pltpu.roll(field_ref[groups * f + g - 1], 1, 0), pltpu.roll(x, 1, 0))
                north = jnp.where(sub == 7, halo, pltpu.roll(x, 7, 0))
            mid_rows.append(x)
            south_rows.append(south)
            north_rows.append(north)
        _, new_v, new_h, new_q = update(ratio, field_ref[g], mid_rows, south_rows, north_rows, coef_ref[rows, :])
        for k, (value, target) in enumerate(
            ((new_v, winds_ref.at[1, rows]), (new_h, layer_ref.at[rows]), (new_q, tracer_ref.at[rows]))
        ):
            out[side, k] = value[:, :span]
            writes.append(pltpu.make_async_copy(out.at[side, k], target, sem.at[side, k]))
            writes[-1].start()
    for write in writes:
        write.wait()


def stencil_main(fields, coef, ratio, row_count, width):
    vmem = pl.BlockSpec(memory_space=pltpu.VMEM)
    anywhere = pl.BlockSpec(memory_space=pl.ANY)
    return pl.pallas_call(
        functools.partial(main_kernel, ratio),
        out_shape=(
            jax.ShapeDtypeStruct((2, row_count, width), jnp.float32),
            jax.ShapeDtypeStruct((row_count, width), jnp.float32),
            jax.ShapeDtypeStruct((row_count, width), jnp.float32),
        ),
        in_specs=[vmem, vmem],
        out_specs=(anywhere, anywhere, anywhere),
        scratch_shapes=[
            pltpu.VMEM((4, row_count // 8, 8, width), jnp.float32),
            pltpu.SemaphoreType.DMA((4, row_count // 8)),
        ],
        compiler_params=pltpu.CompilerParams(vmem_limit_bytes=SMALL_GRANT),
        cost_estimate=pl.CostEstimate(flops=10_000_000, bytes_accessed=1_600_000, transcendentals=0),
        name="stencil_main",
    )(fields, coef)


def stencil_edge(even, fields, first, second, coef, outs, ratio):
    vmem = pl.BlockSpec(memory_space=pltpu.VMEM)
    anywhere = pl.BlockSpec(memory_space=pl.ANY)
    width = outs[1].shape[1]
    return pl.pallas_call(
        functools.partial(edge_kernel, ratio),
        out_shape=tuple(jax.ShapeDtypeStruct(out.shape, jnp.float32) for out in outs),
        in_specs=[pl.BlockSpec(memory_space=pltpu.SMEM), vmem, vmem, vmem, vmem, anywhere, anywhere, anywhere],
        out_specs=(anywhere, anywhere, anywhere),
        scratch_shapes=[pltpu.VMEM((2, 3, 8, width), jnp.float32), pltpu.SemaphoreType.DMA((2, 3))],
        input_output_aliases={5: 0, 6: 1, 7: 2},
        compiler_params=pltpu.CompilerParams(vmem_limit_bytes=SMALL_GRANT),
        name="stencil_edge",
    )(even, fields, second, first, coef, *outs)


def per_device(winds, thickness, tracer, cutoff, damping):
    lat_size = lax.axis_size("lat")
    lon_size = lax.axis_size("lon")
    band = lax.axis_index("lat")
    sector = lax.axis_index("lon")
    row_count, width = thickness.shape
    nlat = row_count * lat_size

    blocks = pack(winds, thickness, tracer)
    owned = lax.all_to_all(blocks, "lon", split_axis=0, concat_axis=0, tiled=True)

    is_polar = (band < lat_size // 4) | (band >= lat_size - lat_size // 4)
    group = sector % (row_count // 8)
    cut = lax.dynamic_slice_in_dim(cutoff.astype(jnp.float32), group * 8, 8)
    damp = lax.dynamic_slice_in_dim(damping, group * 8, 8)
    gain = damp * cut * cut
    cut = jnp.where(is_polar, cut, jnp.float32(NLON))
    cuts = jnp.stack([cut, gain], axis=1)

    filtered = filter_rows(owned, cuts)
    fields = lax.all_to_all(filtered, "lon", split_axis=0, concat_axis=0, tiled=True)

    even = band % 2 == 0
    groups = row_count // 8
    low = jnp.stack([fields[f * groups, 0] for f in (1, 2, 3)])
    high = jnp.stack([fields[f * groups + groups - 1, 7] for f in (1, 2, 3)])
    pairs = {0: [], 1: []}
    for z in range(lat_size):
        for e in range(lon_size):
            here = z * lon_size + e
            across = z * lon_size + (e + lon_size // 2) % lon_size
            up = here + lon_size if z < lat_size - 1 else across
            down = here - lon_size if z > 0 else across
            pairs[0].append((here, up if z % 2 == 0 else down))
            pairs[1].append((here, down if z % 2 == 0 else up))
    first = lax.ppermute(jnp.where(even, high, low), ("lat", "lon"), pairs[0])
    second = lax.ppermute(jnp.where(even, low, high), ("lat", "lon"), pairs[1])

    lon_step = 2.0 * math.pi / NLON
    lat_step = math.pi / nlat
    rows = (band * row_count + jnp.arange(row_count, dtype=jnp.int32)).astype(jnp.float32)
    center = jnp.cos(-math.pi / 2 + (rows + 0.5) * lat_step)
    face = band * row_count + jnp.arange(row_count + 1, dtype=jnp.int32)
    cos_face = jnp.where(
        (face == 0) | (face == nlat), 0.0, jnp.cos(-math.pi / 2 + face.astype(jnp.float32) * lat_step)
    )
    quarter = 0.25 / center
    aspect = lon_step / lat_step
    coef = jnp.stack(
        [quarter, aspect * quarter * cos_face[1:], aspect * quarter * cos_face[:-1], 2.0 * quarter], axis=1
    )
    ratio = lon_step / (2.0 * lat_step)
    outs = stencil_main(fields, coef, ratio, row_count, width)
    return stencil_edge(even.astype(jnp.int32)[None], fields, first, second, coef, outs, ratio)


def solution(mesh):
    placed = (P(None, "lat", "lon"), P("lat", "lon"), P("lat", "lon"), P("lat"), P("lat"))
    return jax.shard_map(
        per_device,
        mesh=mesh,
        in_specs=placed,
        out_specs=(P(None, "lat", "lon"), P("lat", "lon"), P("lat", "lon")),
        check_vma=False,
    )
```

```python
import functools
import math

import jax
import jax.numpy as jnp
import numpy as np
from jax import lax
from jax.experimental import pallas as pl
from jax.experimental.pallas import tpu as pltpu
from jax.sharding import PartitionSpec as P

LEV = 8
NLON = 2880
LANE = 128
TILES = NLON * LEV // LANE
STEP = LANE // LEV
BATCH = 4
SMALL_GRANT = 12 << 20
WIDE = 768


def _lin(terms):
    total = None
    for weight, value in terms:
        if value is None or abs(weight) < 1e-12:
            continue
        if abs(weight - 1.0) < 1e-12:
            item = value
        else:
            item = value * np.float32(weight)
        total = item if total is None else total + item
    return total


def _odd_tables(size):
    half = (size - 1) // 2
    angle = [[2.0 * math.pi * ((j * k) % size) / size for j in range(half + 1)] for k in range(half + 1)]
    return half, angle


def odd_real_forward(values):
    size = len(values)
    half, angle = _odd_tables(size)
    plus = [values[j] + values[size - j] for j in range(1, half + 1)]
    minus = [values[j] - values[size - j] for j in range(1, half + 1)]
    out = [(_lin([(1.0, values[0])] + [(1.0, t) for t in plus]), None)]
    for k in range(1, half + 1):
        real = _lin([(1.0, values[0])] + [(math.cos(angle[k][j]), plus[j - 1]) for j in range(1, half + 1)])
        imag = _lin([(-math.sin(angle[k][j]), minus[j - 1]) for j in range(1, half + 1)])
        out.append((real, imag))
    return out


def odd_real_inverse(bins):
    half = len(bins) - 1
    size = 2 * half + 1
    _, angle = _odd_tables(size)
    doubled = [(b[0] * np.float32(2.0), b[1] * np.float32(2.0)) for b in bins[1:]]
    out = [None] * size
    out[0] = _lin([(1.0, bins[0][0])] + [(1.0, b[0]) for b in doubled])
    for n in range(1, half + 1):
        even = _lin([(1.0, bins[0][0])] + [(math.cos(angle[n][k]), doubled[k - 1][0]) for k in range(1, half + 1)])
        odd = _lin([(math.sin(angle[n][k]), doubled[k - 1][1]) for k in range(1, half + 1)])
        out[n] = even - odd
        out[size - n] = even + odd
    return out


def three(values, sign):
    (ar, ai), (br, bi), (cr, ci) = values
    tr, ti = br + cr, bi + ci
    mr, mi = ar - np.float32(0.5) * tr, ai - np.float32(0.5) * ti
    root = np.float32(sign * math.sqrt(0.75))
    er, ei = root * (br - cr), root * (bi - ci)
    return [(ar + tr, ai + ti), (mr - ei, mi + er), (mr + ei, mi - er)]


def nine(values, sign):
    inner = [three([values[n], values[n + 3], values[n + 6]], sign) for n in range(3)]
    out = [None] * 9
    for k in range(3):
        column = [inner[0][k]]
        for n in (1, 2):
            re, im = inner[n][k]
            if k:
                c = np.float32(math.cos(2.0 * math.pi * n * k / 9))
                s = np.float32(sign * math.sin(2.0 * math.pi * n * k / 9))
                re, im = re * c - im * s, re * s + im * c
            column.append((re, im))
        out[k], out[k + 3], out[k + 6] = three(column, sign)
    return out


def odd_complex(values, sign):
    size = len(values)
    if size == 9:
        return nine(values, sign)
    half, angle = _odd_tables(size)
    out = [None] * size
    plus = [(values[j][0] + values[size - j][0], values[j][1] + values[size - j][1]) for j in range(1, half + 1)]
    minus = [(values[j][0] - values[size - j][0], values[j][1] - values[size - j][1]) for j in range(1, half + 1)]
    out[0] = tuple(_lin([(1.0, values[0][part])] + [(1.0, t[part]) for t in plus]) for part in (0, 1))
    for k in range(1, half + 1):
        base = [
            _lin([(1.0, values[0][part])] + [(math.cos(angle[k][j]), plus[j - 1][part]) for j in range(1, half + 1)])
            for part in (0, 1)
        ]
        turn = [_lin([(math.sin(angle[k][j]), minus[j - 1][part]) for j in range(1, half + 1)]) for part in (0, 1)]
        low = (base[0] + turn[1], base[1] - turn[0])
        high = (base[0] - turn[1], base[1] + turn[0])
        if sign < 0:
            out[k], out[size - k] = low, high
        else:
            out[k], out[size - k] = high, low
    return out


COMPLEX_CLASSES = [(0, 1), (0, 2), (2, 1), (2, 2), (1, 0), (1, 1), (1, 2), (1, 3), (1, 4)]


def _tile_of(a, b, c):
    return (45 * a + 36 * b + 20 * c) % TILES


def _bin_of(alpha, beta, gamma):
    for kappa in range(TILES):
        if kappa % 4 == alpha and kappa % 5 == beta and kappa % 9 == gamma:
            return kappa
    raise ValueError


def _bin_list():
    bins = []
    for alpha in (0, 2):
        bins += [(alpha, 0, gamma) for gamma in range(5)]
    for alpha, beta in COMPLEX_CLASSES:
        bins += [(alpha, beta, gamma) for gamma in range(9)]
    return bins


BINS = _bin_list()
COUNT = len(BINS)
SLOT = {key: index for index, key in enumerate(BINS)}
REAL_ROWS = {(0, 0): 0, (2, 0): 1}
COMPLEX_ROWS = {key: 2 + 2 * index for index, key in enumerate(COMPLEX_CLASSES)}


@functools.lru_cache(maxsize=1)
def tables():
    kappa = np.array([_bin_of(*key) for key in BINS])
    phase = (np.arange(LANE) // LEV)[None, :]
    turn = 2.0 * np.pi * ((kappa[:, None] * phase) % NLON) / NLON
    wave = kappa[:, None] + TILES * phase
    wave = np.minimum(wave, NLON - wave).astype(np.float64)
    rows = np.stack(
        [np.cos(turn), np.sin(turn), wave, 1.0 / (np.maximum(wave, 1.0) ** 2 * NLON)], axis=0
    ).astype(np.float32)
    s = np.arange(LANE) // LEV
    level = np.arange(LANE) % LEV
    same = (level[:, None] == level[None, :]).astype(np.float64)
    angle = 2.0 * np.pi * ((s[:, None] * s[None, :]) % STEP) / STEP
    cosines = np.cos(angle) * same
    sines = np.sin(angle) * same
    forward = np.block([[cosines, -sines], [sines, cosines]]).astype(np.float32)

    def split(matrix):
        high = matrix.astype(jnp.bfloat16)
        low = (matrix - high.astype(np.float32)).astype(jnp.bfloat16)
        return np.concatenate([high, high, low], axis=0)

    return rows, split(forward), split(forward.T)


def split_dot(value, matrix):
    high = value.astype(jnp.bfloat16)
    low = (value - high.astype(jnp.float32)).astype(jnp.bfloat16)
    return jnp.dot(jnp.concatenate([high, low, high], axis=1), matrix, preferred_element_type=jnp.float32)


ALL_CLASSES = [(0, 0), (2, 0)] + COMPLEX_CLASSES
CLASS_CUTS = (0, 4, 6, 8, 11)
CLASS_GROUPS = [ALL_CLASSES[first:last] for first, last in zip(CLASS_CUTS[:-1], CLASS_CUTS[1:])]


def filter_kernel(x_ref, cut_ref, rows_ref, forward_ref, inverse_ref, early_ref, out_ref, full, mid, stage, result, sem):
    del early_ref
    sectors = x_ref.shape[0]
    span = x_ref.shape[2]
    lane = lax.broadcasted_iota(jnp.int32, (8, LANE), 1)
    turned = {}

    def source(d, t):
        if (d, t) not in turned:
            value = x_ref[d, :, LANE * t : min(LANE * (t + 1), span)]
            if value.shape[1] < LANE:
                value = jnp.concatenate([value, jnp.zeros((8, LANE - value.shape[1]), jnp.float32)], axis=1)
            shift = d * span % LANE
            turned[(d, t)] = pltpu.roll(value, shift, 1) if shift else value
        return turned[(d, t)]

    for p in range(TILES):
        edges = []
        for j in range(0, LANE, LEV):
            d, rest = divmod(LANE * p + j, span)
            key = (d, rest // LANE)
            if not edges or edges[-1][1:] != key:
                edges.append((j,) + key)
        value = source(*edges[-1][1:])
        for (_, d, t), (stop, _, _) in reversed(list(zip(edges[:-1], edges[1:]))):
            value = jnp.where(lane < stop, source(d, t), value)
        full[:, LANE * (p + 1) : LANE * (p + 2)] = value

    def tile(p):
        return slice(LANE * (p + 1), LANE * (p + 2))

    for c in range(9):
        quarter = []
        for b in range(5):
            v = [full[:, tile(_tile_of(a, b, c))] for a in range(4)]
            even, odd = v[0] + v[2], v[1] + v[3]
            quarter.append((even + odd, even - odd, v[0] - v[2], v[3] - v[1]))
        zero = odd_real_forward([q[0] for q in quarter])
        two = odd_real_forward([q[1] for q in quarter])
        one = odd_complex([(q[2], q[3]) for q in quarter], -1)
        mid[0, c] = zero[0][0]
        mid[1, c] = two[0][0]
        pieces = {(0, 1): zero[1], (0, 2): zero[2], (2, 1): two[1], (2, 2): two[2]}
        for beta in range(5):
            pieces[(1, beta)] = one[beta]
        for key, value in pieces.items():
            row = COMPLEX_ROWS[key]
            mid[row, c] = value[0]
            mid[row + 1, c] = value[1]

    def put(slot, value):
        cos_row = rows_ref[0, slot : slot + 1, :]
        sin_row = rows_ref[1, slot : slot + 1, :]
        where = slice(8 * slot, 8 * slot + 8)
        if value[1] is None:
            stage[where, :LANE] = value[0] * cos_row
            stage[where, LANE:] = -(value[0] * sin_row)
        else:
            stage[where, :LANE] = value[0] * cos_row + value[1] * sin_row
            stage[where, LANE:] = value[1] * cos_row - value[0] * sin_row

    def take(slot, real):
        cos_row = rows_ref[0, slot : slot + 1, :]
        sin_row = rows_ref[1, slot : slot + 1, :]
        where = slice(8 * slot, 8 * slot + 8)
        re, im = stage[where, :LANE], stage[where, LANE:]
        if real:
            return (re * cos_row - im * sin_row, None)
        return (re * cos_row - im * sin_row, im * cos_row + re * sin_row)

    cut = jnp.broadcast_to(cut_ref[:, 0:1], (8, LANE))
    gain = jnp.broadcast_to(cut_ref[:, 1:2], (8, LANE))
    for classes in CLASS_GROUPS:
        slots = [SLOT[key] for key in BINS if key[:2] in classes]
        start, count = slots[0], len(slots)
        for key in classes:
            if key in REAL_ROWS:
                row = REAL_ROWS[key]
                values = odd_real_forward([mid[row, c] for c in range(9)])
            else:
                row = COMPLEX_ROWS[key]
                values = odd_complex([(mid[row, c], mid[row + 1, c]) for c in range(9)], -1)
            for gamma, value in enumerate(values):
                put(SLOT[key + (gamma,)], value)
        where = slice(8 * start, 8 * (start + count))
        spectrum = split_dot(stage[where, :], forward_ref[...])
        scaled = []
        for index in range(count):
            slot = start + index
            wave = rows_ref[2, slot : slot + 1, :]
            decay = rows_ref[3, slot : slot + 1, :]
            factor = jnp.where(wave > cut, gain * decay, np.float32(1.0 / NLON))
            part = spectrum[8 * index : 8 * index + 8, :]
            scaled.append(part * jnp.concatenate([factor, factor], axis=1))
        stage[where, :] = split_dot(jnp.concatenate(scaled, axis=0), inverse_ref[...])
        for key in classes:
            if key in REAL_ROWS:
                row = REAL_ROWS[key]
                values = odd_real_inverse([take(SLOT[key + (gamma,)], gamma == 0) for gamma in range(5)])
                for c in range(9):
                    mid[row, c] = values[c]
            else:
                row = COMPLEX_ROWS[key]
                values = odd_complex([take(SLOT[key + (gamma,)], False) for gamma in range(9)], 1)
                for c in range(9):
                    mid[row, c] = values[c][0]
                    mid[row + 1, c] = values[c][1]

    for c in range(9):

        def piece(key):
            row = COMPLEX_ROWS[key]
            return (mid[row, c], mid[row + 1, c])

        zero = odd_real_inverse([(mid[0, c], None), piece((0, 1)), piece((0, 2))])
        two = odd_real_inverse([(mid[1, c], None), piece((2, 1)), piece((2, 2))])
        one = odd_complex([piece((1, beta)) for beta in range(5)], 1)
        for b in range(5):
            even, odd = zero[b] + two[b], zero[b] - two[b]
            re2, im2 = one[b][0] + one[b][0], one[b][1] + one[b][1]
            values = (even + re2, odd - im2, even - re2, odd + im2)
            for a in range(4):
                p = _tile_of(a, b, c)
                full[:, tile(p)] = values[a]
                if p == 0:
                    full[:, tile(TILES)] = values[a]
                if p == TILES - 1:
                    full[:, tile(-1)] = values[a]

    writes = []
    for d in range(sectors):
        first, shift = divmod(LANE + d * span, LANE)
        pieces = []
        for t in range(span // LANE + 2):
            piece = full[:, LANE * (first + t) : LANE * (first + t + 1)]
            pieces.append(pltpu.roll(piece, LANE - shift, 1) if shift else piece)
        west = pieces[0] if shift else full[:, LANE * (first - 1) : LANE * first]
        for t in range(WIDE // LANE):
            value = jnp.where(lane < LANE - shift, pieces[t], pieces[t + 1]) if shift else pieces[t]
            if t == WIDE // LANE - 1:
                value = jnp.where(lane < LANE - LEV, value, west)
            result[d, :, LANE * t : LANE * (t + 1)] = value
        if d % BATCH == BATCH - 1:
            here = slice(d + 1 - BATCH, d + 1)
            writes.append(pltpu.make_async_copy(result.at[here], out_ref.at[here], sem.at[d // BATCH]))
            writes[-1].start()
    for write in writes:
        write.wait()


def filter_rows(blocks, cuts, early):
    rows, forward, inverse = tables()
    return pl.pallas_call(
        filter_kernel,
        out_shape=jax.ShapeDtypeStruct((blocks.shape[0], 8, WIDE), jnp.float32),
        in_specs=[pl.BlockSpec(memory_space=pltpu.VMEM)] * 5 + [pl.BlockSpec(memory_space=pl.ANY)],
        out_specs=pl.BlockSpec(memory_space=pl.ANY),
        scratch_shapes=[
            pltpu.VMEM((8, (TILES + 2) * LANE), jnp.float32),
            pltpu.VMEM((20, 9, 8, LANE), jnp.float32),
            pltpu.VMEM((8 * COUNT, 2 * LANE), jnp.float32),
            pltpu.VMEM((blocks.shape[0], 8, WIDE), jnp.float32),
            pltpu.SemaphoreType.DMA((blocks.shape[0] // BATCH,)),
        ],
        compiler_params=pltpu.CompilerParams(vmem_limit_bytes=SMALL_GRANT),
        name="polar_filter",
    )(blocks, cuts, jnp.asarray(rows), jnp.asarray(forward), jnp.asarray(inverse), early)


def pack_kernel(pieces, winds_ref, layer_ref, tracer_ref, out_ref, buffer, in_sem, out_sem):
    blocks = layer_ref.shape[0]
    sources = [(winds_ref, 2 * blocks, 0), (layer_ref, blocks, 2 * blocks), (tracer_ref, blocks, 3 * blocks)]
    size = 4 * blocks // pieces
    inward, outward = [], []
    for ref, count, base in sources:
        for start in range(0, count, size):
            index = (base + start) // size
            here = slice(base + start, base + start + size)
            inward.append(pltpu.make_async_copy(ref.at[start : start + size], buffer.at[here], in_sem.at[index]))
            outward.append(pltpu.make_async_copy(buffer.at[here], out_ref.at[here], out_sem.at[index]))
    for copy in inward:
        copy.start()
    for first, then in zip(inward, outward):
        first.wait()
        then.start()
    for copy in outward:
        copy.wait()


def pack(winds, thickness, tracer):
    row_count, width = thickness.shape
    blocks = row_count // 8
    pieces = 4
    anywhere = pl.BlockSpec(memory_space=pl.ANY)
    return pl.pallas_call(
        functools.partial(pack_kernel, pieces),
        out_shape=jax.ShapeDtypeStruct((4 * blocks, 8, width), jnp.float32),
        in_specs=[anywhere, anywhere, anywhere],
        out_specs=anywhere,
        scratch_shapes=[
            pltpu.VMEM((4 * blocks, 8, width), jnp.float32),
            pltpu.SemaphoreType.DMA((pieces,)),
            pltpu.SemaphoreType.DMA((pieces,)),
        ],
        name="pack",
    )(
        winds.reshape(2 * blocks, 8, width),
        thickness.reshape(blocks, 8, width),
        tracer.reshape(blocks, 8, width),
    )


def east(x):
    return pltpu.roll(x, WIDE - LEV, 1)


def west(x):
    return pltpu.roll(x, LEV, 1)


def update(ratio, u, mid_rows, south_rows, north_rows, coef):
    v, h, q = mid_rows
    v_s, h_s, q_s = south_rows
    v_n, h_n, q_n = north_rows
    zonal, to_north, to_south, slope = (coef[:, k : k + 1] for k in range(4))
    h_e = east(h)
    su = u + east(u)
    fx = su * (h + h_e)
    gx = su * (q + east(q))
    wind_n = (v + v_n) * to_north
    wind_s = (v_s + v) * to_south
    new_h = h - (zonal * (fx - west(fx)) + (wind_n * (h + h_n) - wind_s * (h_s + h)))
    new_q = q - (zonal * (gx - west(gx)) + (wind_n * (q + q_n) - wind_s * (q_s + q)))
    new_v = v - np.float32(ratio) * (h_n - h_s)
    return slope * (h_e - west(h)), new_v, new_h, new_q


def main_kernel(ratio, field_ref, coef_ref, winds_ref, layer_ref, tracer_ref, out, sem):
    groups = field_ref.shape[0] // 4
    span = layer_ref.shape[1]
    sub = lax.broadcasted_iota(jnp.int32, (8, WIDE), 0)
    writes = []

    def shifted(f, g):
        x = field_ref[groups * f + g]
        south = jnp.where(sub == 0, pltpu.roll(field_ref[groups * f + g - 1], 1, 0), pltpu.roll(x, 1, 0))
        north = jnp.where(sub == 7, pltpu.roll(field_ref[groups * f + g + 1], 7, 0), pltpu.roll(x, 7, 0))
        return x, south, north

    for g in range(groups):
        rows = slice(8 * g, 8 * g + 8)
        u = field_ref[g]
        if 0 < g < groups - 1:
            mid_rows, south_rows, north_rows = zip(*(shifted(f, g) for f in (1, 2, 3)))
            du, new_v, new_h, new_q = update(ratio, u, mid_rows, south_rows, north_rows, coef_ref[rows, :])
            out[1, rows, :] = new_v[:, :span]
            out[2, rows, :] = new_h[:, :span]
            out[3, rows, :] = new_q[:, :span]
        else:
            h = field_ref[2 * groups + g]
            du = coef_ref[rows, 3:4] * (east(h) - west(h))
        out[0, rows, :] = (u - du)[:, :span]
        if g in (groups // 2 - 1, groups - 1):
            part = len(writes) // 4
            half = groups // 2
            all_rows = slice(8 * half * part, 8 * half * (part + 1))
            inner = slice(8, 8 * half) if part == 0 else slice(8 * half, 8 * (groups - 1))
            targets = (
                (0, all_rows, winds_ref.at[0, all_rows]),
                (1, inner, winds_ref.at[1, inner]),
                (2, inner, layer_ref.at[inner]),
                (3, inner, tracer_ref.at[inner]),
            )
            for k, where, target in targets:
                writes.append(pltpu.make_async_copy(out.at[k, where], target, sem.at[part, k]))
                writes[-1].start()
    for copy in writes:
        copy.wait()


def edge_kernel(
    ratio, even_ref, field_ref, first_ref, second_ref, coef_ref, w_in, l_in, t_in, winds_ref, layer_ref, tracer_ref, out, sem
):
    del w_in, l_in, t_in
    groups = field_ref.shape[0] // 4
    is_even = even_ref[0] > 0
    span = layer_ref.shape[1]
    sub = lax.broadcasted_iota(jnp.int32, (8, WIDE), 0)
    writes = []
    for side, g in enumerate((0, groups - 1)):
        rows = slice(8 * g, 8 * g + 8)
        near, far = (second_ref, first_ref) if side == 0 else (first_ref, second_ref)
        mid_rows, south_rows, north_rows = [], [], []
        for f in (1, 2, 3):
            x = field_ref[groups * f + g]
            halo = jnp.where(is_even, near[f - 1 : f, :], far[f - 1 : f, :])
            if side == 0:
                south = jnp.where(sub == 0, halo, pltpu.roll(x, 1, 0))
                north = jnp.where(sub == 7, pltpu.roll(field_ref[groups * f + g + 1], 7, 0), pltpu.roll(x, 7, 0))
            else:
                south = jnp.where(sub == 0, pltpu.roll(field_ref[groups * f + g - 1], 1, 0), pltpu.roll(x, 1, 0))
                north = jnp.where(sub == 7, halo, pltpu.roll(x, 7, 0))
            mid_rows.append(x)
            south_rows.append(south)
            north_rows.append(north)
        _, new_v, new_h, new_q = update(ratio, field_ref[g], mid_rows, south_rows, north_rows, coef_ref[rows, :])
        for k, (value, target) in enumerate(
            ((new_v, winds_ref.at[1, rows]), (new_h, layer_ref.at[rows]), (new_q, tracer_ref.at[rows]))
        ):
            out[side, k] = value[:, :span]
            writes.append(pltpu.make_async_copy(out.at[side, k], target, sem.at[side, k]))
            writes[-1].start()
    for write in writes:
        write.wait()


def stencil_main(fields, coef, ratio, row_count, width):
    vmem = pl.BlockSpec(memory_space=pltpu.VMEM)
    anywhere = pl.BlockSpec(memory_space=pl.ANY)
    return pl.pallas_call(
        functools.partial(main_kernel, ratio),
        out_shape=(
            jax.ShapeDtypeStruct((2, row_count, width), jnp.float32),
            jax.ShapeDtypeStruct((row_count, width), jnp.float32),
            jax.ShapeDtypeStruct((row_count, width), jnp.float32),
        ),
        in_specs=[vmem, vmem],
        out_specs=(anywhere, anywhere, anywhere),
        scratch_shapes=[
            pltpu.VMEM((4, row_count, width), jnp.float32),
            pltpu.SemaphoreType.DMA((2, 4)),
        ],
        compiler_params=pltpu.CompilerParams(vmem_limit_bytes=SMALL_GRANT),
        cost_estimate=pl.CostEstimate(flops=10_000_000, bytes_accessed=1_600_000, transcendentals=0),
        name="stencil_main",
    )(fields, coef)


def stencil_edge(even, fields, first, second, coef, outs, ratio):
    vmem = pl.BlockSpec(memory_space=pltpu.VMEM)
    anywhere = pl.BlockSpec(memory_space=pl.ANY)
    width = outs[1].shape[1]
    return pl.pallas_call(
        functools.partial(edge_kernel, ratio),
        out_shape=tuple(jax.ShapeDtypeStruct(out.shape, jnp.float32) for out in outs),
        in_specs=[pl.BlockSpec(memory_space=pltpu.SMEM), vmem, vmem, vmem, vmem, anywhere, anywhere, anywhere],
        out_specs=(anywhere, anywhere, anywhere),
        scratch_shapes=[pltpu.VMEM((2, 3, 8, width), jnp.float32), pltpu.SemaphoreType.DMA((2, 3))],
        input_output_aliases={5: 0, 6: 1, 7: 2},
        compiler_params=pltpu.CompilerParams(vmem_limit_bytes=SMALL_GRANT),
        name="stencil_edge",
    )(even, fields, first, second, coef, *outs)


def per_device(winds, thickness, tracer, cutoff, damping):
    lat_size = lax.axis_size("lat")
    lon_size = lax.axis_size("lon")
    band = lax.axis_index("lat")
    sector = lax.axis_index("lon")
    row_count, width = thickness.shape
    nlat = row_count * lat_size

    blocks = pack(winds, thickness, tracer)
    owned = lax.all_to_all(blocks, "lon", split_axis=0, concat_axis=0, tiled=True)

    is_polar = (band < lat_size // 4) | (band >= lat_size - lat_size // 4)
    group = sector % (row_count // 8)
    cut = lax.dynamic_slice_in_dim(cutoff.astype(jnp.float32), group * 8, 8)
    damp = lax.dynamic_slice_in_dim(damping, group * 8, 8)
    gain = damp * cut * cut
    cut = jnp.where(is_polar, cut, jnp.float32(NLON))
    cuts = jnp.stack([cut, gain], axis=1)

    lon_step = 2.0 * math.pi / NLON
    lat_step = math.pi / nlat
    rows = (band * row_count + jnp.arange(row_count, dtype=jnp.int32)).astype(jnp.float32)
    center = jnp.cos(-math.pi / 2 + (rows + 0.5) * lat_step)
    face = band * row_count + jnp.arange(row_count + 1, dtype=jnp.int32)
    cos_face = jnp.where(
        (face == 0) | (face == nlat), 0.0, jnp.cos(-math.pi / 2 + face.astype(jnp.float32) * lat_step)
    )
    quarter = 0.25 / center
    aspect = lon_step / lat_step
    coef = jnp.stack(
        [quarter, aspect * quarter * cos_face[1:], aspect * quarter * cos_face[:-1], 2.0 * quarter], axis=1
    )

    filtered = filter_rows(owned, cuts, coef)
    fields = lax.all_to_all(filtered, "lon", split_axis=0, concat_axis=0, tiled=True)

    even = band % 2 == 0
    groups = row_count // 8
    low = jnp.stack([fields[f * groups, 0] for f in (1, 2, 3)])
    high = jnp.stack([fields[f * groups + groups - 1, 7] for f in (1, 2, 3)])
    pairs = {0: [], 1: []}
    for z in range(lat_size):
        for e in range(lon_size):
            here = z * lon_size + e
            across = z * lon_size + (e + lon_size // 2) % lon_size
            up = here + lon_size if z < lat_size - 1 else across
            down = here - lon_size if z > 0 else across
            pairs[0].append((here, up if z % 2 == 0 else down))
            pairs[1].append((here, down if z % 2 == 0 else up))
    first = lax.ppermute(jnp.where(even, high, low), ("lat", "lon"), pairs[0])
    second = lax.ppermute(jnp.where(even, low, high), ("lat", "lon"), pairs[1])

    ratio = lon_step / (2.0 * lat_step)
    outs = stencil_main(fields, coef, ratio, row_count, width)
    return stencil_edge(even.astype(jnp.int32)[None], fields, first, second, coef, outs, ratio)


def solution(mesh):
    placed = (P(None, "lat", "lon"), P("lat", "lon"), P("lat", "lon"), P("lat"), P("lat"))
    return jax.shard_map(
        per_device,
        mesh=mesh,
        in_specs=placed,
        out_specs=(P(None, "lat", "lon"), P("lat", "lon"), P("lat", "lon")),
        check_vma=False,
    )
```

```python
import functools
import math

import jax
import jax.numpy as jnp
import numpy as np
from jax import lax
from jax.experimental import pallas as pl
from jax.experimental.pallas import tpu as pltpu
from jax.sharding import PartitionSpec as P


LEV = 8
NLON = 2880
LANE = 128
TILES = NLON * LEV // LANE
STEP = LANE // LEV
BATCH = 4
SMALL_GRANT = 12 << 20
WIDE = 768


def _lin(terms):
    total = None
    for weight, value in terms:
        if value is None or abs(weight) < 1e-12:
            continue
        if abs(weight - 1.0) < 1e-12:
            item = value
        else:
            item = value * np.float32(weight)
        total = item if total is None else total + item
    return total


def _odd_tables(size):
    half = (size - 1) // 2
    angle = [[2.0 * math.pi * ((j * k) % size) / size for j in range(half + 1)] for k in range(half + 1)]
    return half, angle


def odd_real_forward(values):
    size = len(values)
    half, angle = _odd_tables(size)
    plus = [values[j] + values[size - j] for j in range(1, half + 1)]
    minus = [values[j] - values[size - j] for j in range(1, half + 1)]
    out = [(_lin([(1.0, values[0])] + [(1.0, t) for t in plus]), None)]
    for k in range(1, half + 1):
        real = _lin([(1.0, values[0])] + [(math.cos(angle[k][j]), plus[j - 1]) for j in range(1, half + 1)])
        imag = _lin([(-math.sin(angle[k][j]), minus[j - 1]) for j in range(1, half + 1)])
        out.append((real, imag))
    return out


def odd_real_inverse(bins):
    half = len(bins) - 1
    size = 2 * half + 1
    _, angle = _odd_tables(size)
    doubled = [(b[0] * np.float32(2.0), b[1] * np.float32(2.0)) for b in bins[1:]]
    out = [None] * size
    out[0] = _lin([(1.0, bins[0][0])] + [(1.0, b[0]) for b in doubled])
    for n in range(1, half + 1):
        even = _lin([(1.0, bins[0][0])] + [(math.cos(angle[n][k]), doubled[k - 1][0]) for k in range(1, half + 1)])
        odd = _lin([(math.sin(angle[n][k]), doubled[k - 1][1]) for k in range(1, half + 1)])
        out[n] = even - odd
        out[size - n] = even + odd
    return out


def three(values, sign):
    (ar, ai), (br, bi), (cr, ci) = values
    tr, ti = br + cr, bi + ci
    mr, mi = ar - np.float32(0.5) * tr, ai - np.float32(0.5) * ti
    root = np.float32(sign * math.sqrt(0.75))
    er, ei = root * (br - cr), root * (bi - ci)
    return [(ar + tr, ai + ti), (mr - ei, mi + er), (mr + ei, mi - er)]


def nine(values, sign):
    inner = [three([values[n], values[n + 3], values[n + 6]], sign) for n in range(3)]
    out = [None] * 9
    for k in range(3):
        column = [inner[0][k]]
        for n in (1, 2):
            re, im = inner[n][k]
            if k:
                c = np.float32(math.cos(2.0 * math.pi * n * k / 9))
                s = np.float32(sign * math.sin(2.0 * math.pi * n * k / 9))
                re, im = re * c - im * s, re * s + im * c
            column.append((re, im))
        out[k], out[k + 3], out[k + 6] = three(column, sign)
    return out


def odd_complex(values, sign):
    size = len(values)
    if size == 9:
        return nine(values, sign)
    half, angle = _odd_tables(size)
    out = [None] * size
    plus = [(values[j][0] + values[size - j][0], values[j][1] + values[size - j][1]) for j in range(1, half + 1)]
    minus = [(values[j][0] - values[size - j][0], values[j][1] - values[size - j][1]) for j in range(1, half + 1)]
    out[0] = tuple(_lin([(1.0, values[0][part])] + [(1.0, t[part]) for t in plus]) for part in (0, 1))
    for k in range(1, half + 1):
        base = [
            _lin([(1.0, values[0][part])] + [(math.cos(angle[k][j]), plus[j - 1][part]) for j in range(1, half + 1)])
            for part in (0, 1)
        ]
        turn = [_lin([(math.sin(angle[k][j]), minus[j - 1][part]) for j in range(1, half + 1)]) for part in (0, 1)]
        low = (base[0] + turn[1], base[1] - turn[0])
        high = (base[0] - turn[1], base[1] + turn[0])
        if sign < 0:
            out[k], out[size - k] = low, high
        else:
            out[k], out[size - k] = high, low
    return out


COMPLEX_CLASSES = [(0, 1), (0, 2), (2, 1), (2, 2), (1, 0), (1, 1), (1, 2), (1, 3), (1, 4)]


def _tile_of(a, b, c):
    return (45 * a + 36 * b + 20 * c) % TILES


def _bin_of(alpha, beta, gamma):
    for kappa in range(TILES):
        if kappa % 4 == alpha and kappa % 5 == beta and kappa % 9 == gamma:
            return kappa
    raise ValueError


def _bin_list():
    bins = []
    for alpha in (0, 2):
        bins += [(alpha, 0, gamma) for gamma in range(5)]
    for alpha, beta in COMPLEX_CLASSES:
        bins += [(alpha, beta, gamma) for gamma in range(9)]
    return bins


BINS = _bin_list()
COUNT = len(BINS)
SLOT = {key: index for index, key in enumerate(BINS)}
REAL_ROWS = {(0, 0): 0, (2, 0): 1}
COMPLEX_ROWS = {key: 2 + 2 * index for index, key in enumerate(COMPLEX_CLASSES)}


@functools.lru_cache(maxsize=1)
def tables():
    kappa = np.array([_bin_of(*key) for key in BINS])
    phase = (np.arange(LANE) // LEV)[None, :]
    turn = 2.0 * np.pi * ((kappa[:, None] * phase) % NLON) / NLON
    wave = kappa[:, None] + TILES * phase
    wave = np.minimum(wave, NLON - wave).astype(np.float64)
    rows = np.stack(
        [np.cos(turn), np.sin(turn), wave, 1.0 / (np.maximum(wave, 1.0) ** 2 * NLON)], axis=0
    ).astype(np.float32)
    s = np.arange(LANE) // LEV
    level = np.arange(LANE) % LEV
    same = (level[:, None] == level[None, :]).astype(np.float64)
    angle = 2.0 * np.pi * ((s[:, None] * s[None, :]) % STEP) / STEP
    cosines = np.cos(angle) * same
    sines = np.sin(angle) * same
    forward = np.block([[cosines, -sines], [sines, cosines]]).astype(np.float32)

    def split(matrix):
        high = matrix.astype(jnp.bfloat16)
        low = (matrix - high.astype(np.float32)).astype(jnp.bfloat16)
        return np.concatenate([high, high, low], axis=0)

    return rows, split(forward), split(forward.T)


def split_dot(value, matrix):
    high = value.astype(jnp.bfloat16)
    low = (value - high.astype(jnp.float32)).astype(jnp.bfloat16)
    return jnp.dot(jnp.concatenate([high, low, high], axis=1), matrix, preferred_element_type=jnp.float32)


ALL_CLASSES = [(0, 0), (2, 0)] + COMPLEX_CLASSES
CLASS_CUTS = (0, 4, 6, 8, 11)
CLASS_GROUPS = [ALL_CLASSES[first:last] for first, last in zip(CLASS_CUTS[:-1], CLASS_CUTS[1:])]


def circle_filter(source_tile, span, cut_ref, rows_ref, forward_ref, inverse_ref, full, mid, stage):
    lane = lax.broadcasted_iota(jnp.int32, (8, LANE), 1)
    turned = {}

    def source(d, t):
        if (d, t) not in turned:
            value = source_tile(d, t)
            shift = d * span % LANE
            if value is None:
                value = jnp.zeros((8, LANE), jnp.float32)
            elif shift:
                value = pltpu.roll(value, shift, 1)
            turned[(d, t)] = value
        return turned[(d, t)]

    for p in range(TILES):
        edges = []
        for j in range(0, LANE, LEV):
            d, rest = divmod(LANE * p + j, span)
            key = (d, rest // LANE)
            if not edges or edges[-1][1:] != key:
                edges.append((j,) + key)
        value = source(*edges[-1][1:])
        for (_, d, t), (stop, _, _) in reversed(list(zip(edges[:-1], edges[1:]))):
            value = jnp.where(lane < stop, source(d, t), value)
        full[:, LANE * (p + 1) : LANE * (p + 2)] = value

    def tile(p):
        return slice(LANE * (p + 1), LANE * (p + 2))

    for c in range(9):
        quarter = []
        for b in range(5):
            v = [full[:, tile(_tile_of(a, b, c))] for a in range(4)]
            even, odd = v[0] + v[2], v[1] + v[3]
            quarter.append((even + odd, even - odd, v[0] - v[2], v[3] - v[1]))
        zero = odd_real_forward([q[0] for q in quarter])
        two = odd_real_forward([q[1] for q in quarter])
        one = odd_complex([(q[2], q[3]) for q in quarter], -1)
        mid[0, c] = zero[0][0]
        mid[1, c] = two[0][0]
        pieces = {(0, 1): zero[1], (0, 2): zero[2], (2, 1): two[1], (2, 2): two[2]}
        for beta in range(5):
            pieces[(1, beta)] = one[beta]
        for key, value in pieces.items():
            row = COMPLEX_ROWS[key]
            mid[row, c] = value[0]
            mid[row + 1, c] = value[1]

    def put(slot, value):
        cos_row = rows_ref[0, slot : slot + 1, :]
        sin_row = rows_ref[1, slot : slot + 1, :]
        where = slice(8 * slot, 8 * slot + 8)
        if value[1] is None:
            stage[where, :LANE] = value[0] * cos_row
            stage[where, LANE:] = -(value[0] * sin_row)
        else:
            stage[where, :LANE] = value[0] * cos_row + value[1] * sin_row
            stage[where, LANE:] = value[1] * cos_row - value[0] * sin_row

    def take(slot, real):
        cos_row = rows_ref[0, slot : slot + 1, :]
        sin_row = rows_ref[1, slot : slot + 1, :]
        where = slice(8 * slot, 8 * slot + 8)
        re, im = stage[where, :LANE], stage[where, LANE:]
        if real:
            return (re * cos_row - im * sin_row, None)
        return (re * cos_row - im * sin_row, im * cos_row + re * sin_row)

    cut = jnp.broadcast_to(cut_ref[:, 0:1], (8, LANE))
    gain = jnp.broadcast_to(cut_ref[:, 1:2], (8, LANE))
    for classes in CLASS_GROUPS:
        slots = [SLOT[key] for key in BINS if key[:2] in classes]
        start, count = slots[0], len(slots)
        for key in classes:
            if key in REAL_ROWS:
                row = REAL_ROWS[key]
                values = odd_real_forward([mid[row, c] for c in range(9)])
            else:
                row = COMPLEX_ROWS[key]
                values = odd_complex([(mid[row, c], mid[row + 1, c]) for c in range(9)], -1)
            for gamma, value in enumerate(values):
                put(SLOT[key + (gamma,)], value)
        where = slice(8 * start, 8 * (start + count))
        spectrum = split_dot(stage[where, :], forward_ref[...])
        scaled = []
        for index in range(count):
            slot = start + index
            wave = rows_ref[2, slot : slot + 1, :]
            decay = rows_ref[3, slot : slot + 1, :]
            factor = jnp.where(wave > cut, gain * decay, np.float32(1.0 / NLON))
            part = spectrum[8 * index : 8 * index + 8, :]
            scaled.append(part * jnp.concatenate([factor, factor], axis=1))
        stage[where, :] = split_dot(jnp.concatenate(scaled, axis=0), inverse_ref[...])
        for key in classes:
            if key in REAL_ROWS:
                row = REAL_ROWS[key]
                values = odd_real_inverse([take(SLOT[key + (gamma,)], gamma == 0) for gamma in range(5)])
                for c in range(9):
                    mid[row, c] = values[c]
            else:
                row = COMPLEX_ROWS[key]
                values = odd_complex([take(SLOT[key + (gamma,)], False) for gamma in range(9)], 1)
                for c in range(9):
                    mid[row, c] = values[c][0]
                    mid[row + 1, c] = values[c][1]

    for c in range(9):

        def piece(key):
            row = COMPLEX_ROWS[key]
            return (mid[row, c], mid[row + 1, c])

        zero = odd_real_inverse([(mid[0, c], None), piece((0, 1)), piece((0, 2))])
        two = odd_real_inverse([(mid[1, c], None), piece((2, 1)), piece((2, 2))])
        one = odd_complex([piece((1, beta)) for beta in range(5)], 1)
        for b in range(5):
            even, odd = zero[b] + two[b], zero[b] - two[b]
            re2, im2 = one[b][0] + one[b][0], one[b][1] + one[b][1]
            values = (even + re2, odd - im2, even - re2, odd + im2)
            for a in range(4):
                p = _tile_of(a, b, c)
                full[:, tile(p)] = values[a]
                if p == 0:
                    full[:, tile(TILES)] = values[a]
                if p == TILES - 1:
                    full[:, tile(-1)] = values[a]


def filter_kernel(x_ref, cut_ref, rows_ref, forward_ref, inverse_ref, early_ref, out_ref, full, mid, stage, result, sem):
    del early_ref
    sectors = x_ref.shape[0]
    span = NLON * LEV // sectors
    lane = lax.broadcasted_iota(jnp.int32, (8, LANE), 1)

    def source_tile(d, t):
        return x_ref[d, :, LANE * t : LANE * (t + 1)]

    circle_filter(source_tile, span, cut_ref, rows_ref, forward_ref, inverse_ref, full, mid, stage)
    writes = []
    for d in range(sectors):
        first, shift = divmod(LANE + d * span, LANE)
        pieces = []
        for t in range(span // LANE + 2):
            piece = full[:, LANE * (first + t) : LANE * (first + t + 1)]
            pieces.append(pltpu.roll(piece, LANE - shift, 1) if shift else piece)
        west = pieces[0] if shift else full[:, LANE * (first - 1) : LANE * first]
        for t in range(WIDE // LANE):
            value = jnp.where(lane < LANE - shift, pieces[t], pieces[t + 1]) if shift else pieces[t]
            if t == WIDE // LANE - 1:
                value = jnp.where(lane < LANE - LEV, value, west)
            result[d, :, LANE * t : LANE * (t + 1)] = value
        if d % BATCH == BATCH - 1:
            here = slice(d + 1 - BATCH, d + 1)
            writes.append(pltpu.make_async_copy(result.at[here], out_ref.at[here], sem.at[d // BATCH]))
            writes[-1].start()
    for write in writes:
        write.wait()


PIECE = 48
AHEAD = 6
WINDOW = 10


def pole_kernel(where_ref, x_ref, cut_ref, rows_ref, forward_ref, inverse_ref, out_ref, full, mid, stage, wide, window):
    sectors = x_ref.shape[0]
    span = NLON * LEV // sectors
    lane = lax.broadcasted_iota(jnp.int32, (8, LANE), 1)

    def source_tile(d, t):
        if t:
            return None
        value = pltpu.roll(x_ref[d, :, WIDE - LANE : WIDE], PIECE, 1)
        return jnp.where(lane < PIECE, value, 0.0)

    circle_filter(source_tile, span, cut_ref, rows_ref, forward_ref, inverse_ref, full, mid, stage)
    wide[:, LANE * AHEAD : LANE * (AHEAD + TILES)] = full[:, LANE : LANE * (TILES + 1)]
    wide[:, : LANE * AHEAD] = full[:, LANE * (TILES + 1 - AHEAD) : LANE * (TILES + 1)]
    wide[:, LANE * (AHEAD + TILES) :] = full[:, LANE : LANE * 5]
    for k in range(2):
        tile = where_ref[2 * k]
        rest = where_ref[2 * k + 1]
        start = pl.multiple_of(tile * LANE, LANE)
        window[...] = pltpu.roll(wide[:, pl.ds(start, WINDOW * LANE)], WINDOW * LANE - rest, 1)
        total = None
        for r in range(8):
            first = 7 * PIECE - PIECE * r
            part = window[r : r + 1, first : first + span]
            total = part if total is None else total + part
        out_ref[k : k + 1, :span] = total


def pole_rows(where, blocks, cuts):
    rows, forward, inverse = tables()
    vmem = pl.BlockSpec(memory_space=pltpu.VMEM)
    return pl.pallas_call(
        pole_kernel,
        out_shape=jax.ShapeDtypeStruct((2, WIDE), jnp.float32),
        in_specs=[pl.BlockSpec(memory_space=pltpu.SMEM)] + [vmem] * 5,
        out_specs=vmem,
        scratch_shapes=[
            pltpu.VMEM((8, (TILES + 2) * LANE), jnp.float32),
            pltpu.VMEM((20, 9, 8, LANE), jnp.float32),
            pltpu.VMEM((8 * COUNT, 2 * LANE), jnp.float32),
            pltpu.VMEM((8, (AHEAD + TILES + 4) * LANE), jnp.float32),
            pltpu.VMEM((8, WINDOW * LANE), jnp.float32),
        ],
        compiler_params=pltpu.CompilerParams(vmem_limit_bytes=SMALL_GRANT),
        name="pole_filter",
    )(where, blocks, cuts, jnp.asarray(rows), jnp.asarray(forward), jnp.asarray(inverse))


def add_kernel(mine_ref, theirs_ref, out_ref):
    out_ref[...] = mine_ref[0:1, :] + theirs_ref[...]


def add_halves(mine, theirs):
    vmem = pl.BlockSpec(memory_space=pltpu.VMEM)
    return pl.pallas_call(
        add_kernel,
        out_shape=jax.ShapeDtypeStruct((1, WIDE), jnp.float32),
        in_specs=[vmem, vmem],
        out_specs=vmem,
        compiler_params=pltpu.CompilerParams(vmem_limit_bytes=SMALL_GRANT),
        name="pole_sum",
    )(mine, theirs)


def filter_rows(blocks, cuts, early):
    rows, forward, inverse = tables()
    return pl.pallas_call(
        filter_kernel,
        out_shape=jax.ShapeDtypeStruct((blocks.shape[0], 8, WIDE), jnp.float32),
        in_specs=[pl.BlockSpec(memory_space=pltpu.VMEM)] * 5 + [pl.BlockSpec(memory_space=pl.ANY)],
        out_specs=pl.BlockSpec(memory_space=pl.ANY),
        scratch_shapes=[
            pltpu.VMEM((8, (TILES + 2) * LANE), jnp.float32),
            pltpu.VMEM((20, 9, 8, LANE), jnp.float32),
            pltpu.VMEM((8 * COUNT, 2 * LANE), jnp.float32),
            pltpu.VMEM((blocks.shape[0], 8, WIDE), jnp.float32),
            pltpu.SemaphoreType.DMA((blocks.shape[0] // BATCH,)),
        ],
        compiler_params=pltpu.CompilerParams(vmem_limit_bytes=SMALL_GRANT),
        name="polar_filter",
    )(blocks, cuts, jnp.asarray(rows), jnp.asarray(forward), jnp.asarray(inverse), early)


def pack_kernel(north_ref, winds_ref, layer_ref, tracer_ref, out_ref, buffer, last, pole, in_sem, out_sem):
    blocks = layer_ref.shape[0]
    span = layer_ref.shape[2]
    whole = span // LANE * LANE
    sources = [(layer_ref, 0, blocks, 2 * blocks), (winds_ref, 0, blocks, 0), (winds_ref, blocks, blocks, blocks), (tracer_ref, 0, blocks, 3 * blocks)]
    inward = []
    for index, (ref, start, count, base) in enumerate(sources):
        inward.append(pltpu.make_async_copy(ref.at[start : start + count], buffer.at[base : base + count], in_sem.at[index]))
        inward[-1].start()
    outward = []
    for index, (_, _, count, base) in enumerate(sources):
        inward[index].wait()
        here = slice(base, base + count)
        outward.append(pltpu.make_async_copy(buffer.at[here, :, 0:whole], out_ref.at[here, :, 0:whole], out_sem.at[2 * index]))
        outward[-1].start()
        if index == 0:
            row = jnp.where(
                north_ref[0] > 0, buffer[3 * blocks - 1, 7:8, :], buffer[2 * blocks, 0:1, :]
            )
            pole[0:1, 0:span] = row
            pole[0:1, span:WIDE] = jnp.zeros((1, WIDE - span), jnp.float32)
            pieces = []
            for c in range(2):
                for r in range(8):
                    first = span // 2 * c + PIECE * r
                    stop = min(first + PIECE, span // 2 * (c + 1))
                    pole[8 + 8 * c + r : 9 + 8 * c + r, 0:PIECE] = jnp.zeros((1, PIECE), jnp.float32)
                    pole[8 + 8 * c + r : 9 + 8 * c + r, 0 : stop - first] = pole[0:1, first:stop]
                pieces.append(pole[8 + 8 * c : 16 + 8 * c, 0:PIECE])
        for w in range(base, base + count):
            last[w, :, 0 : span - whole] = buffer[w, :, whole:span]
            last[w, :, span - whole : LANE] = pieces[w % 2]
        outward.append(pltpu.make_async_copy(last.at[here], out_ref.at[here, :, whole:WIDE], out_sem.at[2 * index + 1]))
        outward[-1].start()
    for copy in outward:
        copy.wait()


def pack(north, winds, thickness, tracer):
    row_count, width = thickness.shape
    blocks = row_count // 8
    anywhere = pl.BlockSpec(memory_space=pl.ANY)
    return pl.pallas_call(
        pack_kernel,
        out_shape=jax.ShapeDtypeStruct((4 * blocks, 8, WIDE), jnp.float32),
        in_specs=[pl.BlockSpec(memory_space=pltpu.SMEM), anywhere, anywhere, anywhere],
        out_specs=anywhere,
        scratch_shapes=[
            pltpu.VMEM((4 * blocks, 8, width), jnp.float32),
            pltpu.VMEM((4 * blocks, 8, LANE), jnp.float32),
            pltpu.VMEM((24, WIDE), jnp.float32),
            pltpu.SemaphoreType.DMA((4,)),
            pltpu.SemaphoreType.DMA((8,)),
        ],
        name="pack",
    )(
        north,
        winds.reshape(2 * blocks, 8, width),
        thickness.reshape(blocks, 8, width),
        tracer.reshape(blocks, 8, width),
    )


def east(x):
    return pltpu.roll(x, WIDE - LEV, 1)


def west(x):
    return pltpu.roll(x, LEV, 1)


def update(ratio, u, mid_rows, south_rows, north_rows, coef):
    v, h, q = mid_rows
    v_s, h_s, q_s = south_rows
    v_n, h_n, q_n = north_rows
    zonal, to_north, to_south, slope = (coef[:, k : k + 1] for k in range(4))
    h_e = east(h)
    su = u + east(u)
    fx = su * (h + h_e)
    gx = su * (q + east(q))
    wind_n = (v + v_n) * to_north
    wind_s = (v_s + v) * to_south
    new_h = h - (zonal * (fx - west(fx)) + (wind_n * (h + h_n) - wind_s * (h_s + h)))
    new_q = q - (zonal * (gx - west(gx)) + (wind_n * (q + q_n) - wind_s * (q_s + q)))
    new_v = v - np.float32(ratio) * (h_n - h_s)
    return slope * (h_e - west(h)), new_v, new_h, new_q


def main_kernel(ratio, field_ref, coef_ref, winds_ref, layer_ref, tracer_ref, out, sem):
    groups = field_ref.shape[0] // 4
    span = layer_ref.shape[1]
    sub = lax.broadcasted_iota(jnp.int32, (8, WIDE), 0)
    writes = []

    def shifted(f, g):
        x = field_ref[groups * f + g]
        south = jnp.where(sub == 0, pltpu.roll(field_ref[groups * f + g - 1], 1, 0), pltpu.roll(x, 1, 0))
        north = jnp.where(sub == 7, pltpu.roll(field_ref[groups * f + g + 1], 7, 0), pltpu.roll(x, 7, 0))
        return x, south, north

    for g in range(groups):
        rows = slice(8 * g, 8 * g + 8)
        u = field_ref[g]
        if 0 < g < groups - 1:
            mid_rows, south_rows, north_rows = zip(*(shifted(f, g) for f in (1, 2, 3)))
            du, new_v, new_h, new_q = update(ratio, u, mid_rows, south_rows, north_rows, coef_ref[rows, :])
            out[1, rows, :] = new_v[:, :span]
            out[2, rows, :] = new_h[:, :span]
            out[3, rows, :] = new_q[:, :span]
        else:
            h = field_ref[2 * groups + g]
            du = coef_ref[rows, 3:4] * (east(h) - west(h))
        out[0, rows, :] = (u - du)[:, :span]
        if g in (groups // 2 - 1, groups - 1):
            part = len(writes) // 4
            half = groups // 2
            all_rows = slice(8 * half * part, 8 * half * (part + 1))
            inner = slice(8, 8 * half) if part == 0 else slice(8 * half, 8 * (groups - 1))
            targets = (
                (0, all_rows, winds_ref.at[0, all_rows]),
                (1, inner, winds_ref.at[1, inner]),
                (2, inner, layer_ref.at[inner]),
                (3, inner, tracer_ref.at[inner]),
            )
            for k, where, target in targets:
                writes.append(pltpu.make_async_copy(out.at[k, where], target, sem.at[part, k]))
                writes[-1].start()
    for copy in writes:
        copy.wait()


def edge_kernel(
    ratio, even_ref, field_ref, first_ref, second_ref, across_ref, coef_ref, w_in, l_in, t_in, winds_ref, layer_ref, tracer_ref, out, sem
):
    del w_in, l_in, t_in
    groups = field_ref.shape[0] // 4
    is_even = even_ref[0] > 0
    span = layer_ref.shape[1]
    sub = lax.broadcasted_iota(jnp.int32, (8, WIDE), 0)
    writes = []
    for side, g in enumerate((0, groups - 1)):
        rows = slice(8 * g, 8 * g + 8)
        near, far = (second_ref, first_ref) if side == 0 else (first_ref, second_ref)
        mid_rows, south_rows, north_rows = [], [], []
        for f in (1, 2, 3):
            x = field_ref[groups * f + g]
            halo = jnp.where(is_even, near[f - 1 : f, :], far[f - 1 : f, :])
            if f == 2:
                halo = jnp.where(even_ref[1] == side + 1, across_ref[...], halo)
            if side == 0:
                south = jnp.where(sub == 0, halo, pltpu.roll(x, 1, 0))
                north = jnp.where(sub == 7, pltpu.roll(field_ref[groups * f + g + 1], 7, 0), pltpu.roll(x, 7, 0))
            else:
                south = jnp.where(sub == 0, pltpu.roll(field_ref[groups * f + g - 1], 1, 0), pltpu.roll(x, 1, 0))
                north = jnp.where(sub == 7, halo, pltpu.roll(x, 7, 0))
            mid_rows.append(x)
            south_rows.append(south)
            north_rows.append(north)
        _, new_v, new_h, new_q = update(ratio, field_ref[g], mid_rows, south_rows, north_rows, coef_ref[rows, :])
        for k, (value, target) in enumerate(
            ((new_v, winds_ref.at[1, rows]), (new_h, layer_ref.at[rows]), (new_q, tracer_ref.at[rows]))
        ):
            out[side, k] = value[:, :span]
            writes.append(pltpu.make_async_copy(out.at[side, k], target, sem.at[side, k]))
            writes[-1].start()
    for write in writes:
        write.wait()


def stencil_main(fields, coef, ratio, row_count, width):
    vmem = pl.BlockSpec(memory_space=pltpu.VMEM)
    anywhere = pl.BlockSpec(memory_space=pl.ANY)
    return pl.pallas_call(
        functools.partial(main_kernel, ratio),
        out_shape=(
            jax.ShapeDtypeStruct((2, row_count, width), jnp.float32),
            jax.ShapeDtypeStruct((row_count, width), jnp.float32),
            jax.ShapeDtypeStruct((row_count, width), jnp.float32),
        ),
        in_specs=[vmem, vmem],
        out_specs=(anywhere, anywhere, anywhere),
        scratch_shapes=[
            pltpu.VMEM((4, row_count, width), jnp.float32),
            pltpu.SemaphoreType.DMA((2, 4)),
        ],
        compiler_params=pltpu.CompilerParams(vmem_limit_bytes=SMALL_GRANT),
        cost_estimate=pl.CostEstimate(flops=10_000_000, bytes_accessed=1_600_000, transcendentals=0),
        name="stencil_main",
    )(fields, coef)


def stencil_edge(even, fields, first, second, across, coef, outs, ratio):
    vmem = pl.BlockSpec(memory_space=pltpu.VMEM)
    anywhere = pl.BlockSpec(memory_space=pl.ANY)
    width = outs[1].shape[1]
    return pl.pallas_call(
        functools.partial(edge_kernel, ratio),
        out_shape=tuple(jax.ShapeDtypeStruct(out.shape, jnp.float32) for out in outs),
        in_specs=[pl.BlockSpec(memory_space=pltpu.SMEM), vmem, vmem, vmem, vmem, vmem, anywhere, anywhere, anywhere],
        out_specs=(anywhere, anywhere, anywhere),
        scratch_shapes=[pltpu.VMEM((2, 3, 8, width), jnp.float32), pltpu.SemaphoreType.DMA((2, 3))],
        input_output_aliases={6: 0, 7: 1, 8: 2},
        compiler_params=pltpu.CompilerParams(vmem_limit_bytes=SMALL_GRANT),
        name="stencil_edge",
    )(even, fields, first, second, across, coef, *outs)


def per_device(winds, thickness, tracer, cutoff, damping):
    lat_size = lax.axis_size("lat")
    lon_size = lax.axis_size("lon")
    band = lax.axis_index("lat")
    sector = lax.axis_index("lon")
    row_count, width = thickness.shape
    nlat = row_count * lat_size

    is_north = band == lat_size - 1
    blocks = pack(is_north.astype(jnp.int32)[None], winds, thickness, tracer)
    owned = lax.all_to_all(blocks, "lon", split_axis=0, concat_axis=0, tiled=True)

    is_polar = (band < lat_size // 4) | (band >= lat_size - lat_size // 4)
    group = sector % (row_count // 8)
    cut = lax.dynamic_slice_in_dim(cutoff.astype(jnp.float32), group * 8, 8)
    damp = lax.dynamic_slice_in_dim(damping, group * 8, 8)
    gain = damp * cut * cut
    cut = jnp.where(is_polar, cut, jnp.float32(NLON))
    cuts = jnp.stack([cut, gain], axis=1)

    lon_step = 2.0 * math.pi / NLON
    lat_step = math.pi / nlat
    rows = (band * row_count + jnp.arange(row_count, dtype=jnp.int32)).astype(jnp.float32)
    center = jnp.cos(-math.pi / 2 + (rows + 0.5) * lat_step)
    face = band * row_count + jnp.arange(row_count + 1, dtype=jnp.int32)
    cos_face = jnp.where(
        (face == 0) | (face == nlat), 0.0, jnp.cos(-math.pi / 2 + face.astype(jnp.float32) * lat_step)
    )
    quarter = 0.25 / center
    aspect = lon_step / lat_step
    coef = jnp.stack(
        [quarter, aspect * quarter * cos_face[1:], aspect * quarter * cos_face[:-1], 2.0 * quarter], axis=1
    )

    filtered = filter_rows(owned, cuts, coef)
    fields = lax.all_to_all(filtered, "lon", split_axis=0, concat_axis=0, tiled=True)
    core = sector % 2
    opposite = [(x + lon_size // 2) % lon_size for x in (sector, sector + 1 - 2 * core)]
    starts = [width * x - (width // 2) * core + LANE * AHEAD - 7 * PIECE for x in opposite]
    where = jnp.stack([starts[0] // LANE, starts[0] % LANE, starts[1] // LANE, starts[1] % LANE]).astype(jnp.int32)
    pole_cut = jnp.where(is_north, cutoff[-1], cutoff[0]).astype(jnp.float32)
    pole_damp = jnp.where(is_north, damping[-1], damping[0])
    pole_cuts = jnp.broadcast_to(jnp.stack([pole_cut, pole_damp * pole_cut * pole_cut])[None, :], (8, 2))
    halves = pole_rows(where, owned, pole_cuts)
    theirs = lax.ppermute(halves[1:2], "lon", [(x, x ^ 1) for x in range(lon_size)])
    across = add_halves(halves, theirs)

    even = band % 2 == 0
    groups = row_count // 8
    low = jnp.stack([fields[f * groups, 0] for f in (1, 2, 3)])
    high = jnp.stack([fields[f * groups + groups - 1, 7] for f in (1, 2, 3)])
    pairs = {0: [], 1: []}
    for z in range(lat_size):
        for e in range(lon_size):
            here = z * lon_size + e
            up, down = here + lon_size, here - lon_size
            pairs[0].append((here, up if z % 2 == 0 else down))
            if 0 < z < lat_size - 1:
                pairs[1].append((here, down if z % 2 == 0 else up))
    first = lax.ppermute(jnp.where(even, high, low), ("lat", "lon"), pairs[0])
    second = lax.ppermute(jnp.where(even, low, high), ("lat", "lon"), pairs[1])

    ratio = lon_step / (2.0 * lat_step)
    outs = stencil_main(fields, coef, ratio, row_count, width)
    state = jnp.stack([even.astype(jnp.int32), (band == 0).astype(jnp.int32) + 2 * is_north.astype(jnp.int32)])
    return stencil_edge(state, fields, first, second, across, coef, outs, ratio)


def solution(mesh):
    placed = (P(None, "lat", "lon"), P("lat", "lon"), P("lat", "lon"), P("lat"), P("lat"))
    return jax.shard_map(
        per_device,
        mesh=mesh,
        in_specs=placed,
        out_specs=(P(None, "lat", "lon"), P("lat", "lon"), P("lat", "lon")),
        check_vma=False,
    )
```

```python
import functools
import math

import jax
import jax.numpy as jnp
import numpy as np
from jax import lax
from jax.experimental import pallas as pl
from jax.experimental.pallas import tpu as pltpu
from jax.sharding import PartitionSpec as P


LEV = 8
NLON = 2880
LANE = 128
TILES = NLON * LEV // LANE
STEP = LANE // LEV
BATCH = 4
SMALL_GRANT = 12 << 20
WIDE = 768


def _lin(terms):
    total = None
    for weight, value in terms:
        if value is None or abs(weight) < 1e-12:
            continue
        if abs(weight - 1.0) < 1e-12:
            item = value
        else:
            item = value * np.float32(weight)
        total = item if total is None else total + item
    return total


def _odd_tables(size):
    half = (size - 1) // 2
    angle = [[2.0 * math.pi * ((j * k) % size) / size for j in range(half + 1)] for k in range(half + 1)]
    return half, angle


def odd_real_forward(values):
    size = len(values)
    half, angle = _odd_tables(size)
    plus = [values[j] + values[size - j] for j in range(1, half + 1)]
    minus = [values[j] - values[size - j] for j in range(1, half + 1)]
    out = [(_lin([(1.0, values[0])] + [(1.0, t) for t in plus]), None)]
    for k in range(1, half + 1):
        real = _lin([(1.0, values[0])] + [(math.cos(angle[k][j]), plus[j - 1]) for j in range(1, half + 1)])
        imag = _lin([(-math.sin(angle[k][j]), minus[j - 1]) for j in range(1, half + 1)])
        out.append((real, imag))
    return out


def odd_real_inverse(bins):
    half = len(bins) - 1
    size = 2 * half + 1
    _, angle = _odd_tables(size)
    doubled = [(b[0] * np.float32(2.0), b[1] * np.float32(2.0)) for b in bins[1:]]
    out = [None] * size
    out[0] = _lin([(1.0, bins[0][0])] + [(1.0, b[0]) for b in doubled])
    for n in range(1, half + 1):
        even = _lin([(1.0, bins[0][0])] + [(math.cos(angle[n][k]), doubled[k - 1][0]) for k in range(1, half + 1)])
        odd = _lin([(math.sin(angle[n][k]), doubled[k - 1][1]) for k in range(1, half + 1)])
        out[n] = even - odd
        out[size - n] = even + odd
    return out


def three(values, sign):
    (ar, ai), (br, bi), (cr, ci) = values
    tr, ti = br + cr, bi + ci
    mr, mi = ar - np.float32(0.5) * tr, ai - np.float32(0.5) * ti
    root = np.float32(sign * math.sqrt(0.75))
    er, ei = root * (br - cr), root * (bi - ci)
    return [(ar + tr, ai + ti), (mr - ei, mi + er), (mr + ei, mi - er)]


def nine(values, sign):
    inner = [three([values[n], values[n + 3], values[n + 6]], sign) for n in range(3)]
    out = [None] * 9
    for k in range(3):
        column = [inner[0][k]]
        for n in (1, 2):
            re, im = inner[n][k]
            if k:
                c = np.float32(math.cos(2.0 * math.pi * n * k / 9))
                s = np.float32(sign * math.sin(2.0 * math.pi * n * k / 9))
                re, im = re * c - im * s, re * s + im * c
            column.append((re, im))
        out[k], out[k + 3], out[k + 6] = three(column, sign)
    return out


def odd_complex(values, sign):
    size = len(values)
    if size == 9:
        return nine(values, sign)
    half, angle = _odd_tables(size)
    out = [None] * size
    plus = [(values[j][0] + values[size - j][0], values[j][1] + values[size - j][1]) for j in range(1, half + 1)]
    minus = [(values[j][0] - values[size - j][0], values[j][1] - values[size - j][1]) for j in range(1, half + 1)]
    out[0] = tuple(_lin([(1.0, values[0][part])] + [(1.0, t[part]) for t in plus]) for part in (0, 1))
    for k in range(1, half + 1):
        base = [
            _lin([(1.0, values[0][part])] + [(math.cos(angle[k][j]), plus[j - 1][part]) for j in range(1, half + 1)])
            for part in (0, 1)
        ]
        turn = [_lin([(math.sin(angle[k][j]), minus[j - 1][part]) for j in range(1, half + 1)]) for part in (0, 1)]
        low = (base[0] + turn[1], base[1] - turn[0])
        high = (base[0] - turn[1], base[1] + turn[0])
        if sign < 0:
            out[k], out[size - k] = low, high
        else:
            out[k], out[size - k] = high, low
    return out


COMPLEX_CLASSES = [(0, 1), (0, 2), (2, 1), (2, 2), (1, 0), (1, 1), (1, 2), (1, 3), (1, 4)]


def _tile_of(a, b, c):
    return (45 * a + 36 * b + 20 * c) % TILES


def _bin_of(alpha, beta, gamma):
    for kappa in range(TILES):
        if kappa % 4 == alpha and kappa % 5 == beta and kappa % 9 == gamma:
            return kappa
    raise ValueError


def _bin_list():
    bins = []
    for alpha in (0, 2):
        bins += [(alpha, 0, gamma) for gamma in range(5)]
    for alpha, beta in COMPLEX_CLASSES:
        bins += [(alpha, beta, gamma) for gamma in range(9)]
    return bins


BINS = _bin_list()
COUNT = len(BINS)
SLOT = {key: index for index, key in enumerate(BINS)}
REAL_ROWS = {(0, 0): 0, (2, 0): 1}
COMPLEX_ROWS = {key: 2 + 2 * index for index, key in enumerate(COMPLEX_CLASSES)}


@functools.lru_cache(maxsize=1)
def tables():
    kappa = np.array([_bin_of(*key) for key in BINS])
    phase = (np.arange(LANE) // LEV)[None, :]
    turn = 2.0 * np.pi * ((kappa[:, None] * phase) % NLON) / NLON
    wave = kappa[:, None] + TILES * phase
    wave = np.minimum(wave, NLON - wave).astype(np.float64)
    rows = np.stack(
        [np.cos(turn), np.sin(turn), wave, 1.0 / (np.maximum(wave, 1.0) ** 2 * NLON)], axis=0
    ).astype(np.float32)
    s = np.arange(LANE) // LEV
    level = np.arange(LANE) % LEV
    same = (level[:, None] == level[None, :]).astype(np.float64)
    angle = 2.0 * np.pi * ((s[:, None] * s[None, :]) % STEP) / STEP
    cosines = np.cos(angle) * same
    sines = np.sin(angle) * same
    forward = np.block([[cosines, -sines], [sines, cosines]]).astype(np.float32)

    def split(matrix):
        high = matrix.astype(jnp.bfloat16)
        low = (matrix - high.astype(np.float32)).astype(jnp.bfloat16)
        return np.concatenate([high, high, low], axis=0)

    return rows, split(forward), split(forward.T)


def split_dot(value, matrix):
    high = value.astype(jnp.bfloat16)
    low = (value - high.astype(jnp.float32)).astype(jnp.bfloat16)
    return jnp.dot(jnp.concatenate([high, low, high], axis=1), matrix, preferred_element_type=jnp.float32)


ALL_CLASSES = [(0, 0), (2, 0)] + COMPLEX_CLASSES
CLASS_CUTS = (0, 4, 6, 8, 11)
CLASS_GROUPS = [ALL_CLASSES[first:last] for first, last in zip(CLASS_CUTS[:-1], CLASS_CUTS[1:])]


def circle_filter(source_tile, span, cut_ref, rows_ref, forward_ref, inverse_ref, full, mid, stage):
    lane = lax.broadcasted_iota(jnp.int32, (8, LANE), 1)
    turned = {}

    def source(d, t):
        if (d, t) not in turned:
            value = source_tile(d, t)
            shift = d * span % LANE
            if value is None:
                value = jnp.zeros((8, LANE), jnp.float32)
            elif shift:
                value = pltpu.roll(value, shift, 1)
            turned[(d, t)] = value
        return turned[(d, t)]

    for p in range(TILES):
        edges = []
        for j in range(0, LANE, LEV):
            d, rest = divmod(LANE * p + j, span)
            key = (d, rest // LANE)
            if not edges or edges[-1][1:] != key:
                edges.append((j,) + key)
        value = source(*edges[-1][1:])
        for (_, d, t), (stop, _, _) in reversed(list(zip(edges[:-1], edges[1:]))):
            value = jnp.where(lane < stop, source(d, t), value)
        full[:, LANE * (p + 1) : LANE * (p + 2)] = value

    def tile(p):
        return slice(LANE * (p + 1), LANE * (p + 2))

    for c in range(9):
        quarter = []
        for b in range(5):
            v = [full[:, tile(_tile_of(a, b, c))] for a in range(4)]
            even, odd = v[0] + v[2], v[1] + v[3]
            quarter.append((even + odd, even - odd, v[0] - v[2], v[3] - v[1]))
        zero = odd_real_forward([q[0] for q in quarter])
        two = odd_real_forward([q[1] for q in quarter])
        one = odd_complex([(q[2], q[3]) for q in quarter], -1)
        mid[0, c] = zero[0][0]
        mid[1, c] = two[0][0]
        pieces = {(0, 1): zero[1], (0, 2): zero[2], (2, 1): two[1], (2, 2): two[2]}
        for beta in range(5):
            pieces[(1, beta)] = one[beta]
        for key, value in pieces.items():
            row = COMPLEX_ROWS[key]
            mid[row, c] = value[0]
            mid[row + 1, c] = value[1]

    def put(slot, value):
        cos_row = rows_ref[0, slot : slot + 1, :]
        sin_row = rows_ref[1, slot : slot + 1, :]
        where = slice(8 * slot, 8 * slot + 8)
        if value[1] is None:
            stage[where, :LANE] = value[0] * cos_row
            stage[where, LANE:] = -(value[0] * sin_row)
        else:
            stage[where, :LANE] = value[0] * cos_row + value[1] * sin_row
            stage[where, LANE:] = value[1] * cos_row - value[0] * sin_row

    def take(slot, real):
        cos_row = rows_ref[0, slot : slot + 1, :]
        sin_row = rows_ref[1, slot : slot + 1, :]
        where = slice(8 * slot, 8 * slot + 8)
        re, im = stage[where, :LANE], stage[where, LANE:]
        if real:
            return (re * cos_row - im * sin_row, None)
        return (re * cos_row - im * sin_row, im * cos_row + re * sin_row)

    cut = jnp.broadcast_to(cut_ref[:, 0:1], (8, LANE))
    gain = jnp.broadcast_to(cut_ref[:, 1:2], (8, LANE))
    for classes in CLASS_GROUPS:
        slots = [SLOT[key] for key in BINS if key[:2] in classes]
        start, count = slots[0], len(slots)
        for key in classes:
            if key in REAL_ROWS:
                row = REAL_ROWS[key]
                values = odd_real_forward([mid[row, c] for c in range(9)])
            else:
                row = COMPLEX_ROWS[key]
                values = odd_complex([(mid[row, c], mid[row + 1, c]) for c in range(9)], -1)
            for gamma, value in enumerate(values):
                put(SLOT[key + (gamma,)], value)
        where = slice(8 * start, 8 * (start + count))
        spectrum = split_dot(stage[where, :], forward_ref[...])
        scaled = []
        for index in range(count):
            slot = start + index
            wave = rows_ref[2, slot : slot + 1, :]
            decay = rows_ref[3, slot : slot + 1, :]
            factor = jnp.where(wave > cut, gain * decay, np.float32(1.0 / NLON))
            part = spectrum[8 * index : 8 * index + 8, :]
            scaled.append(part * jnp.concatenate([factor, factor], axis=1))
        stage[where, :] = split_dot(jnp.concatenate(scaled, axis=0), inverse_ref[...])
        for key in classes:
            if key in REAL_ROWS:
                row = REAL_ROWS[key]
                values = odd_real_inverse([take(SLOT[key + (gamma,)], gamma == 0) for gamma in range(5)])
                for c in range(9):
                    mid[row, c] = values[c]
            else:
                row = COMPLEX_ROWS[key]
                values = odd_complex([take(SLOT[key + (gamma,)], False) for gamma in range(9)], 1)
                for c in range(9):
                    mid[row, c] = values[c][0]
                    mid[row + 1, c] = values[c][1]

    for c in range(9):

        def piece(key):
            row = COMPLEX_ROWS[key]
            return (mid[row, c], mid[row + 1, c])

        zero = odd_real_inverse([(mid[0, c], None), piece((0, 1)), piece((0, 2))])
        two = odd_real_inverse([(mid[1, c], None), piece((2, 1)), piece((2, 2))])
        one = odd_complex([piece((1, beta)) for beta in range(5)], 1)
        for b in range(5):
            even, odd = zero[b] + two[b], zero[b] - two[b]
            re2, im2 = one[b][0] + one[b][0], one[b][1] + one[b][1]
            values = (even + re2, odd - im2, even - re2, odd + im2)
            for a in range(4):
                p = _tile_of(a, b, c)
                full[:, tile(p)] = values[a]
                if p == 0:
                    full[:, tile(TILES)] = values[a]
                if p == TILES - 1:
                    full[:, tile(-1)] = values[a]


def filter_kernel(x_ref, cut_ref, rows_ref, forward_ref, inverse_ref, early_ref, out_ref, full, mid, stage, result, sem):
    del early_ref
    sectors = x_ref.shape[0]
    span = NLON * LEV // sectors
    lane = lax.broadcasted_iota(jnp.int32, (8, LANE), 1)

    def source_tile(d, t):
        return x_ref[d, :, LANE * t : LANE * (t + 1)]

    circle_filter(source_tile, span, cut_ref, rows_ref, forward_ref, inverse_ref, full, mid, stage)
    writes = []
    for d in range(sectors):
        first, shift = divmod(LANE + d * span, LANE)
        pieces = []
        for t in range(span // LANE + 2):
            piece = full[:, LANE * (first + t) : LANE * (first + t + 1)]
            pieces.append(pltpu.roll(piece, LANE - shift, 1) if shift else piece)
        west = pieces[0] if shift else full[:, LANE * (first - 1) : LANE * first]
        for t in range(WIDE // LANE):
            value = jnp.where(lane < LANE - shift, pieces[t], pieces[t + 1]) if shift else pieces[t]
            if t == WIDE // LANE - 1:
                value = jnp.where(lane < LANE - LEV, value, west)
            result[d, :, LANE * t : LANE * (t + 1)] = value
        if d % BATCH == BATCH - 1:
            here = slice(d + 1 - BATCH, d + 1)
            writes.append(pltpu.make_async_copy(result.at[here], out_ref.at[here], sem.at[d // BATCH]))
            writes[-1].start()
    for write in writes:
        write.wait()


PIECE = 48
AHEAD = 6
WINDOW = 10


def pole_kernel(where_ref, x_ref, cut_ref, rows_ref, forward_ref, inverse_ref, out_ref, full, mid, stage, wide, window):
    sectors = x_ref.shape[0]
    span = NLON * LEV // sectors
    lane = lax.broadcasted_iota(jnp.int32, (8, LANE), 1)

    def source_tile(d, t):
        if t:
            return None
        value = pltpu.roll(x_ref[d, :, WIDE - LANE : WIDE], PIECE, 1)
        return jnp.where(lane < PIECE, value, 0.0)

    circle_filter(source_tile, span, cut_ref, rows_ref, forward_ref, inverse_ref, full, mid, stage)
    wide[:, LANE * AHEAD : LANE * (AHEAD + TILES)] = full[:, LANE : LANE * (TILES + 1)]
    wide[:, : LANE * AHEAD] = full[:, LANE * (TILES + 1 - AHEAD) : LANE * (TILES + 1)]
    wide[:, LANE * (AHEAD + TILES) :] = full[:, LANE : LANE * 5]
    for k in range(2):
        tile = where_ref[2 * k]
        rest = where_ref[2 * k + 1]
        start = pl.multiple_of(tile * LANE, LANE)
        window[...] = pltpu.roll(wide[:, pl.ds(start, WINDOW * LANE)], WINDOW * LANE - rest, 1)
        total = None
        for r in range(8):
            first = 7 * PIECE - PIECE * r
            part = window[r : r + 1, first : first + span]
            total = part if total is None else total + part
        out_ref[k : k + 1, :span] = total


def pole_rows(where, blocks, cuts):
    rows, forward, inverse = tables()
    vmem = pl.BlockSpec(memory_space=pltpu.VMEM)
    return pl.pallas_call(
        pole_kernel,
        out_shape=jax.ShapeDtypeStruct((2, WIDE), jnp.float32),
        in_specs=[pl.BlockSpec(memory_space=pltpu.SMEM)] + [vmem] * 5,
        out_specs=vmem,
        scratch_shapes=[
            pltpu.VMEM((8, (TILES + 2) * LANE), jnp.float32),
            pltpu.VMEM((20, 9, 8, LANE), jnp.float32),
            pltpu.VMEM((8 * COUNT, 2 * LANE), jnp.float32),
            pltpu.VMEM((8, (AHEAD + TILES + 4) * LANE), jnp.float32),
            pltpu.VMEM((8, WINDOW * LANE), jnp.float32),
        ],
        compiler_params=pltpu.CompilerParams(vmem_limit_bytes=SMALL_GRANT),
        name="pole_filter",
    )(where, blocks, cuts, jnp.asarray(rows), jnp.asarray(forward), jnp.asarray(inverse))


def add_kernel(mine_ref, theirs_ref, out_ref):
    out_ref[...] = mine_ref[0:1, :] + theirs_ref[...]


def add_halves(mine, theirs):
    vmem = pl.BlockSpec(memory_space=pltpu.VMEM)
    return pl.pallas_call(
        add_kernel,
        out_shape=jax.ShapeDtypeStruct((1, WIDE), jnp.float32),
        in_specs=[vmem, vmem],
        out_specs=vmem,
        compiler_params=pltpu.CompilerParams(vmem_limit_bytes=SMALL_GRANT),
        name="pole_sum",
    )(mine, theirs)


def filter_rows(blocks, cuts, early):
    rows, forward, inverse = tables()
    return pl.pallas_call(
        filter_kernel,
        out_shape=jax.ShapeDtypeStruct((blocks.shape[0], 8, WIDE), jnp.float32),
        in_specs=[pl.BlockSpec(memory_space=pltpu.VMEM)] * 5 + [pl.BlockSpec(memory_space=pl.ANY)],
        out_specs=pl.BlockSpec(memory_space=pl.ANY),
        scratch_shapes=[
            pltpu.VMEM((8, (TILES + 2) * LANE), jnp.float32),
            pltpu.VMEM((20, 9, 8, LANE), jnp.float32),
            pltpu.VMEM((8 * COUNT, 2 * LANE), jnp.float32),
            pltpu.VMEM((blocks.shape[0], 8, WIDE), jnp.float32),
            pltpu.SemaphoreType.DMA((blocks.shape[0] // BATCH,)),
        ],
        compiler_params=pltpu.CompilerParams(vmem_limit_bytes=SMALL_GRANT),
        name="polar_filter",
    )(blocks, cuts, jnp.asarray(rows), jnp.asarray(forward), jnp.asarray(inverse), early)


def pack_kernel(north_ref, winds_ref, layer_ref, tracer_ref, out_ref, buffer, last, pole, in_sem, out_sem):
    blocks = layer_ref.shape[0]
    span = layer_ref.shape[2]
    whole = span // LANE * LANE
    sources = [(layer_ref, 0, blocks, 2 * blocks), (winds_ref, 0, blocks, 0), (winds_ref, blocks, blocks, blocks), (tracer_ref, 0, blocks, 3 * blocks)]
    inward = []
    for index, (ref, start, count, base) in enumerate(sources):
        inward.append(pltpu.make_async_copy(ref.at[start : start + count], buffer.at[base : base + count], in_sem.at[index]))
        inward[-1].start()
    outward = []
    for index, (_, _, count, base) in enumerate(sources):
        inward[index].wait()
        here = slice(base, base + count)
        outward.append(pltpu.make_async_copy(buffer.at[here, :, 0:whole], out_ref.at[here, :, 0:whole], out_sem.at[2 * index]))
        outward[-1].start()
        if index == 0:
            row = jnp.where(
                north_ref[0] > 0, buffer[3 * blocks - 1, 7:8, :], buffer[2 * blocks, 0:1, :]
            )
            pole[0:1, 0:span] = row
            pole[0:1, span:WIDE] = jnp.zeros((1, WIDE - span), jnp.float32)
            pieces = []
            for c in range(2):
                for r in range(8):
                    first = span // 2 * c + PIECE * r
                    stop = min(first + PIECE, span // 2 * (c + 1))
                    pole[8 + 8 * c + r : 9 + 8 * c + r, 0:PIECE] = jnp.zeros((1, PIECE), jnp.float32)
                    pole[8 + 8 * c + r : 9 + 8 * c + r, 0 : stop - first] = pole[0:1, first:stop]
                pieces.append(pole[8 + 8 * c : 16 + 8 * c, 0:PIECE])
        for w in range(base, base + count):
            last[w, :, 0 : span - whole] = buffer[w, :, whole:span]
            last[w, :, span - whole : LANE] = pieces[w % 2]
        outward.append(pltpu.make_async_copy(last.at[here], out_ref.at[here, :, whole:WIDE], out_sem.at[2 * index + 1]))
        outward[-1].start()
    for copy in outward:
        copy.wait()


def pack(north, winds, thickness, tracer):
    row_count, width = thickness.shape
    blocks = row_count // 8
    anywhere = pl.BlockSpec(memory_space=pl.ANY)
    return pl.pallas_call(
        pack_kernel,
        out_shape=jax.ShapeDtypeStruct((4 * blocks, 8, WIDE), jnp.float32),
        in_specs=[pl.BlockSpec(memory_space=pltpu.SMEM), anywhere, anywhere, anywhere],
        out_specs=anywhere,
        scratch_shapes=[
            pltpu.VMEM((4 * blocks, 8, width), jnp.float32),
            pltpu.VMEM((4 * blocks, 8, LANE), jnp.float32),
            pltpu.VMEM((24, WIDE), jnp.float32),
            pltpu.SemaphoreType.DMA((4,)),
            pltpu.SemaphoreType.DMA((8,)),
        ],
        name="pack",
    )(
        north,
        winds.reshape(2 * blocks, 8, width),
        thickness.reshape(blocks, 8, width),
        tracer.reshape(blocks, 8, width),
    )


def east(x):
    return pltpu.roll(x, WIDE - LEV, 1)


def west(x):
    return pltpu.roll(x, LEV, 1)


def update(ratio, u, mid_rows, south_rows, north_rows, coef):
    v, h, q = mid_rows
    v_s, h_s, q_s = south_rows
    v_n, h_n, q_n = north_rows
    zonal, to_north, to_south, slope = (coef[:, k : k + 1] for k in range(4))
    h_e = east(h)
    su = u + east(u)
    fx = su * (h + h_e)
    gx = su * (q + east(q))
    wind_n = (v + v_n) * to_north
    wind_s = (v_s + v) * to_south
    new_h = h - (zonal * (fx - west(fx)) + (wind_n * (h + h_n) - wind_s * (h_s + h)))
    new_q = q - (zonal * (gx - west(gx)) + (wind_n * (q + q_n) - wind_s * (q_s + q)))
    new_v = v - np.float32(ratio) * (h_n - h_s)
    return slope * (h_e - west(h)), new_v, new_h, new_q


def main_kernel(ratio, field_ref, coef_ref, winds_ref, layer_ref, tracer_ref, out, sem):
    groups = field_ref.shape[0] // 4
    span = layer_ref.shape[1]
    sub = lax.broadcasted_iota(jnp.int32, (8, WIDE), 0)
    writes = []

    def shifted(f, g):
        x = field_ref[groups * f + g]
        south = jnp.where(sub == 0, pltpu.roll(field_ref[groups * f + g - 1], 1, 0), pltpu.roll(x, 1, 0))
        north = jnp.where(sub == 7, pltpu.roll(field_ref[groups * f + g + 1], 7, 0), pltpu.roll(x, 7, 0))
        return x, south, north

    for g in range(groups):
        rows = slice(8 * g, 8 * g + 8)
        u = field_ref[g]
        if 0 < g < groups - 1:
            mid_rows, south_rows, north_rows = zip(*(shifted(f, g) for f in (1, 2, 3)))
            du, new_v, new_h, new_q = update(ratio, u, mid_rows, south_rows, north_rows, coef_ref[rows, :])
            out[1, rows, :] = new_v[:, :span]
            out[2, rows, :] = new_h[:, :span]
            out[3, rows, :] = new_q[:, :span]
        else:
            h = field_ref[2 * groups + g]
            du = coef_ref[rows, 3:4] * (east(h) - west(h))
        out[0, rows, :] = (u - du)[:, :span]
        if g in (groups // 2 - 1, groups - 1):
            part = len(writes) // 4
            half = groups // 2
            all_rows = slice(8 * half * part, 8 * half * (part + 1))
            inner = slice(8, 8 * half) if part == 0 else slice(8 * half, 8 * (groups - 1))
            targets = (
                (0, all_rows, winds_ref.at[0, all_rows]),
                (1, inner, winds_ref.at[1, inner]),
                (2, inner, layer_ref.at[inner]),
                (3, inner, tracer_ref.at[inner]),
            )
            for k, where, target in targets:
                writes.append(pltpu.make_async_copy(out.at[k, where], target, sem.at[part, k]))
                writes[-1].start()
    for copy in writes:
        copy.wait()


def edge_kernel(
    ratio, state_ref, field_ref, second_ref, first_ref, across_ref, coef_ref, w_in, l_in, t_in, winds_ref, layer_ref, tracer_ref, out, sem
):
    del w_in, l_in, t_in
    groups = field_ref.shape[0] // 4
    is_even = state_ref[0] % 2 > 0
    pole = state_ref[0] // 2
    span = layer_ref.shape[1]
    sub = lax.broadcasted_iota(jnp.int32, (8, WIDE), 0)
    writes = []
    for side, g in enumerate((0, groups - 1)):
        rows = slice(8 * g, 8 * g + 8)
        near, far = (second_ref, first_ref) if side == 0 else (first_ref, second_ref)
        mid_rows, south_rows, north_rows = [], [], []
        for f in (1, 2, 3):
            x = field_ref[groups * f + g]
            halo = jnp.where(is_even, near[f - 1 : f, :], far[f - 1 : f, :])
            if f == 2:
                halo = jnp.where(pole == side + 1, across_ref[...], halo)
            if side == 0:
                south = jnp.where(sub == 0, halo, pltpu.roll(x, 1, 0))
                north = jnp.where(sub == 7, pltpu.roll(field_ref[groups * f + g + 1], 7, 0), pltpu.roll(x, 7, 0))
            else:
                south = jnp.where(sub == 0, pltpu.roll(field_ref[groups * f + g - 1], 1, 0), pltpu.roll(x, 1, 0))
                north = jnp.where(sub == 7, halo, pltpu.roll(x, 7, 0))
            mid_rows.append(x)
            south_rows.append(south)
            north_rows.append(north)
        _, new_v, new_h, new_q = update(ratio, field_ref[g], mid_rows, south_rows, north_rows, coef_ref[rows, :])
        for k, (value, target) in enumerate(
            ((new_v, winds_ref.at[1, rows]), (new_h, layer_ref.at[rows]), (new_q, tracer_ref.at[rows]))
        ):
            out[side, k] = value[:, :span]
            writes.append(pltpu.make_async_copy(out.at[side, k], target, sem.at[side, k]))
            writes[-1].start()
    for write in writes:
        write.wait()


def stencil_main(fields, coef, ratio, row_count, width):
    vmem = pl.BlockSpec(memory_space=pltpu.VMEM)
    anywhere = pl.BlockSpec(memory_space=pl.ANY)
    return pl.pallas_call(
        functools.partial(main_kernel, ratio),
        out_shape=(
            jax.ShapeDtypeStruct((2, row_count, width), jnp.float32),
            jax.ShapeDtypeStruct((row_count, width), jnp.float32),
            jax.ShapeDtypeStruct((row_count, width), jnp.float32),
        ),
        in_specs=[vmem, vmem],
        out_specs=(anywhere, anywhere, anywhere),
        scratch_shapes=[
            pltpu.VMEM((4, row_count, width), jnp.float32),
            pltpu.SemaphoreType.DMA((2, 4)),
        ],
        compiler_params=pltpu.CompilerParams(vmem_limit_bytes=SMALL_GRANT),
        cost_estimate=pl.CostEstimate(flops=10_000_000, bytes_accessed=1_600_000, transcendentals=0),
        name="stencil_main",
    )(fields, coef)


def stencil_edge(state, fields, first, second, across, coef, outs, ratio):
    vmem = pl.BlockSpec(memory_space=pltpu.VMEM)
    anywhere = pl.BlockSpec(memory_space=pl.ANY)
    width = outs[1].shape[1]
    return pl.pallas_call(
        functools.partial(edge_kernel, ratio),
        out_shape=tuple(jax.ShapeDtypeStruct(out.shape, jnp.float32) for out in outs),
        in_specs=[pl.BlockSpec(memory_space=pltpu.SMEM), vmem, vmem, vmem, vmem, vmem, anywhere, anywhere, anywhere],
        out_specs=(anywhere, anywhere, anywhere),
        scratch_shapes=[pltpu.VMEM((2, 3, 8, width), jnp.float32), pltpu.SemaphoreType.DMA((2, 3))],
        input_output_aliases={6: 0, 7: 1, 8: 2},
        compiler_params=pltpu.CompilerParams(vmem_limit_bytes=SMALL_GRANT),
        name="stencil_edge",
    )(state, fields, second, first, across, coef, *outs)


def per_device(winds, thickness, tracer, cutoff, damping):
    lat_size = lax.axis_size("lat")
    lon_size = lax.axis_size("lon")
    band = lax.axis_index("lat")
    sector = lax.axis_index("lon")
    row_count, width = thickness.shape
    nlat = row_count * lat_size

    is_north = band == lat_size - 1
    blocks = pack(is_north.astype(jnp.int32)[None], winds, thickness, tracer)
    owned = lax.all_to_all(blocks, "lon", split_axis=0, concat_axis=0, tiled=True)

    is_polar = (band < lat_size // 4) | (band >= lat_size - lat_size // 4)
    group = sector % (row_count // 8)
    cut = lax.dynamic_slice_in_dim(cutoff.astype(jnp.float32), group * 8, 8)
    damp = lax.dynamic_slice_in_dim(damping, group * 8, 8)
    gain = damp * cut * cut
    cut = jnp.where(is_polar, cut, jnp.float32(NLON))
    cuts = jnp.stack([cut, gain], axis=1)

    lon_step = 2.0 * math.pi / NLON
    lat_step = math.pi / nlat
    rows = (band * row_count + jnp.arange(row_count, dtype=jnp.int32)).astype(jnp.float32)
    center = jnp.cos(-math.pi / 2 + (rows + 0.5) * lat_step)
    face = band * row_count + jnp.arange(row_count + 1, dtype=jnp.int32)
    cos_face = jnp.where(
        (face == 0) | (face == nlat), 0.0, jnp.cos(-math.pi / 2 + face.astype(jnp.float32) * lat_step)
    )
    quarter = 0.25 / center
    aspect = lon_step / lat_step
    coef = jnp.stack(
        [quarter, aspect * quarter * cos_face[1:], aspect * quarter * cos_face[:-1], 2.0 * quarter], axis=1
    )

    filtered = filter_rows(owned, cuts, coef)
    fields = lax.all_to_all(filtered, "lon", split_axis=0, concat_axis=0, tiled=True)
    core = sector % 2
    opposite = [(x + lon_size // 2) % lon_size for x in (sector, sector + 1 - 2 * core)]
    starts = [width * x - (width // 2) * core + LANE * AHEAD - 7 * PIECE for x in opposite]
    where = jnp.stack([starts[0] // LANE, starts[0] % LANE, starts[1] // LANE, starts[1] % LANE]).astype(jnp.int32)
    pole_cut = jnp.where(is_north, cutoff[-1], cutoff[0]).astype(jnp.float32)
    pole_damp = jnp.where(is_north, damping[-1], damping[0])
    pole_cuts = jnp.broadcast_to(jnp.stack([pole_cut, pole_damp * pole_cut * pole_cut])[None, :], (8, 2))
    halves = pole_rows(where, owned, pole_cuts)
    theirs = lax.ppermute(halves[1:2], "lon", [(x, x ^ 1) for x in range(lon_size)])
    across = add_halves(halves, theirs)

    even = band % 2 == 0
    groups = row_count // 8
    low = jnp.stack([fields[f * groups, 0] for f in (1, 2, 3)])
    high = jnp.stack([fields[f * groups + groups - 1, 7] for f in (1, 2, 3)])
    pairs = {0: [], 1: []}
    for z in range(lat_size):
        for e in range(lon_size):
            here = z * lon_size + e
            up, down = here + lon_size, here - lon_size
            pairs[0].append((here, up if z % 2 == 0 else down))
            if 0 < z < lat_size - 1:
                pairs[1].append((here, down if z % 2 == 0 else up))
    first = lax.ppermute(jnp.where(even, high, low), ("lat", "lon"), pairs[0])
    second = lax.ppermute(jnp.where(even, low, high), ("lat", "lon"), pairs[1])

    ratio = lon_step / (2.0 * lat_step)
    outs = stencil_main(fields, coef, ratio, row_count, width)
    state = even.astype(jnp.int32) + 2 * (band == 0).astype(jnp.int32) + 4 * is_north.astype(jnp.int32)
    return stencil_edge(state[None], fields, first, second, across, coef, outs, ratio)


def solution(mesh):
    placed = (P(None, "lat", "lon"), P("lat", "lon"), P("lat", "lon"), P("lat"), P("lat"))
    return jax.shard_map(
        per_device,
        mesh=mesh,
        in_specs=placed,
        out_specs=(P(None, "lat", "lon"), P("lat", "lon"), P("lat", "lon")),
        check_vma=False,
    )
```

```python
import functools
import math

import jax
import jax.numpy as jnp
import numpy as np
from jax import lax
from jax.experimental import pallas as pl
from jax.experimental.pallas import tpu as pltpu
from jax.sharding import PartitionSpec as P


LEV = 8
NLON = 2880
LANE = 128
TILES = NLON * LEV // LANE
STEP = LANE // LEV
BATCH = 2
SMALL_GRANT = 12 << 20
WIDE = 768


def _lin(terms):
    total = None
    for weight, value in terms:
        if value is None or abs(weight) < 1e-12:
            continue
        if abs(weight - 1.0) < 1e-12:
            item = value
        else:
            item = value * np.float32(weight)
        total = item if total is None else total + item
    return total


def _odd_tables(size):
    half = (size - 1) // 2
    angle = [[2.0 * math.pi * ((j * k) % size) / size for j in range(half + 1)] for k in range(half + 1)]
    return half, angle


def odd_real_forward(values):
    size = len(values)
    half, angle = _odd_tables(size)
    plus = [values[j] + values[size - j] for j in range(1, half + 1)]
    minus = [values[j] - values[size - j] for j in range(1, half + 1)]
    out = [(_lin([(1.0, values[0])] + [(1.0, t) for t in plus]), None)]
    for k in range(1, half + 1):
        real = _lin([(1.0, values[0])] + [(math.cos(angle[k][j]), plus[j - 1]) for j in range(1, half + 1)])
        imag = _lin([(-math.sin(angle[k][j]), minus[j - 1]) for j in range(1, half + 1)])
        out.append((real, imag))
    return out


def odd_real_inverse(bins):
    half = len(bins) - 1
    size = 2 * half + 1
    _, angle = _odd_tables(size)
    doubled = [(b[0] * np.float32(2.0), b[1] * np.float32(2.0)) for b in bins[1:]]
    out = [None] * size
    out[0] = _lin([(1.0, bins[0][0])] + [(1.0, b[0]) for b in doubled])
    for n in range(1, half + 1):
        even = _lin([(1.0, bins[0][0])] + [(math.cos(angle[n][k]), doubled[k - 1][0]) for k in range(1, half + 1)])
        odd = _lin([(math.sin(angle[n][k]), doubled[k - 1][1]) for k in range(1, half + 1)])
        out[n] = even - odd
        out[size - n] = even + odd
    return out


def three(values, sign):
    (ar, ai), (br, bi), (cr, ci) = values
    tr, ti = br + cr, bi + ci
    mr, mi = ar - np.float32(0.5) * tr, ai - np.float32(0.5) * ti
    root = np.float32(sign * math.sqrt(0.75))
    er, ei = root * (br - cr), root * (bi - ci)
    return [(ar + tr, ai + ti), (mr - ei, mi + er), (mr + ei, mi - er)]


def nine(values, sign):
    inner = [three([values[n], values[n + 3], values[n + 6]], sign) for n in range(3)]
    out = [None] * 9
    for k in range(3):
        column = [inner[0][k]]
        for n in (1, 2):
            re, im = inner[n][k]
            if k:
                c = np.float32(math.cos(2.0 * math.pi * n * k / 9))
                s = np.float32(sign * math.sin(2.0 * math.pi * n * k / 9))
                re, im = re * c - im * s, re * s + im * c
            column.append((re, im))
        out[k], out[k + 3], out[k + 6] = three(column, sign)
    return out


def odd_complex(values, sign):
    size = len(values)
    if size == 9:
        return nine(values, sign)
    half, angle = _odd_tables(size)
    out = [None] * size
    plus = [(values[j][0] + values[size - j][0], values[j][1] + values[size - j][1]) for j in range(1, half + 1)]
    minus = [(values[j][0] - values[size - j][0], values[j][1] - values[size - j][1]) for j in range(1, half + 1)]
    out[0] = tuple(_lin([(1.0, values[0][part])] + [(1.0, t[part]) for t in plus]) for part in (0, 1))
    for k in range(1, half + 1):
        base = [
            _lin([(1.0, values[0][part])] + [(math.cos(angle[k][j]), plus[j - 1][part]) for j in range(1, half + 1)])
            for part in (0, 1)
        ]
        turn = [_lin([(math.sin(angle[k][j]), minus[j - 1][part]) for j in range(1, half + 1)]) for part in (0, 1)]
        low = (base[0] + turn[1], base[1] - turn[0])
        high = (base[0] - turn[1], base[1] + turn[0])
        if sign < 0:
            out[k], out[size - k] = low, high
        else:
            out[k], out[size - k] = high, low
    return out


COMPLEX_CLASSES = [(0, 1), (0, 2), (2, 1), (2, 2), (1, 0), (1, 1), (1, 2), (1, 3), (1, 4)]


def _tile_of(a, b, c):
    return (45 * a + 36 * b + 20 * c) % TILES


def _bin_of(alpha, beta, gamma):
    for kappa in range(TILES):
        if kappa % 4 == alpha and kappa % 5 == beta and kappa % 9 == gamma:
            return kappa
    raise ValueError


def _bin_list():
    bins = []
    for alpha in (0, 2):
        bins += [(alpha, 0, gamma) for gamma in range(5)]
    for alpha, beta in COMPLEX_CLASSES:
        bins += [(alpha, beta, gamma) for gamma in range(9)]
    return bins


BINS = _bin_list()
COUNT = len(BINS)
SLOT = {key: index for index, key in enumerate(BINS)}
REAL_ROWS = {(0, 0): 0, (2, 0): 1}
COMPLEX_ROWS = {key: 2 + 2 * index for index, key in enumerate(COMPLEX_CLASSES)}


@functools.lru_cache(maxsize=1)
def tables():
    kappa = np.array([_bin_of(*key) for key in BINS])
    phase = (np.arange(LANE) // LEV)[None, :]
    turn = 2.0 * np.pi * ((kappa[:, None] * phase) % NLON) / NLON
    wave = kappa[:, None] + TILES * phase
    wave = np.minimum(wave, NLON - wave).astype(np.float64)
    rows = np.stack(
        [np.cos(turn), np.sin(turn), wave, 1.0 / (np.maximum(wave, 1.0) ** 2 * NLON)], axis=0
    ).astype(np.float32)
    s = np.arange(LANE) // LEV
    level = np.arange(LANE) % LEV
    same = (level[:, None] == level[None, :]).astype(np.float64)
    angle = 2.0 * np.pi * ((s[:, None] * s[None, :]) % STEP) / STEP
    cosines = np.cos(angle) * same
    sines = np.sin(angle) * same
    forward = np.block([[cosines, -sines], [sines, cosines]]).astype(np.float32)

    def split(matrix):
        high = matrix.astype(jnp.bfloat16)
        low = (matrix - high.astype(np.float32)).astype(jnp.bfloat16)
        return np.concatenate([high, high, low], axis=0)

    return rows, split(forward), split(forward.T)


def split_dot(value, matrix):
    high = value.astype(jnp.bfloat16)
    low = (value - high.astype(jnp.float32)).astype(jnp.bfloat16)
    return jnp.dot(jnp.concatenate([high, low, high], axis=1), matrix, preferred_element_type=jnp.float32)


ALL_CLASSES = [(0, 0), (2, 0)] + COMPLEX_CLASSES
CLASS_CUTS = (0, 3, 5, 7, 9, 11)
CLASS_GROUPS = [ALL_CLASSES[first:last] for first, last in zip(CLASS_CUTS[:-1], CLASS_CUTS[1:])]


def circle_filter(source_tile, span, cut_ref, rows_ref, forward_ref, inverse_ref, full, mid, stage):
    lane = lax.broadcasted_iota(jnp.int32, (8, LANE), 1)
    turned = {}

    def source(d, t):
        if (d, t) not in turned:
            value = source_tile(d, t)
            shift = d * span % LANE
            if value is None:
                value = jnp.zeros((8, LANE), jnp.float32)
            elif shift:
                value = pltpu.roll(value, shift, 1)
            turned[(d, t)] = value
        return turned[(d, t)]

    for p in range(TILES):
        edges = []
        for j in range(0, LANE, LEV):
            d, rest = divmod(LANE * p + j, span)
            key = (d, rest // LANE)
            if not edges or edges[-1][1:] != key:
                edges.append((j,) + key)
        value = source(*edges[-1][1:])
        for (_, d, t), (stop, _, _) in reversed(list(zip(edges[:-1], edges[1:]))):
            value = jnp.where(lane < stop, source(d, t), value)
        full[:, LANE * (p + 1) : LANE * (p + 2)] = value

    def tile(p):
        return slice(LANE * (p + 1), LANE * (p + 2))

    for c in range(9):
        quarter = []
        for b in range(5):
            v = [full[:, tile(_tile_of(a, b, c))] for a in range(4)]
            even, odd = v[0] + v[2], v[1] + v[3]
            quarter.append((even + odd, even - odd, v[0] - v[2], v[3] - v[1]))
        zero = odd_real_forward([q[0] for q in quarter])
        two = odd_real_forward([q[1] for q in quarter])
        one = odd_complex([(q[2], q[3]) for q in quarter], -1)
        mid[0, c] = zero[0][0]
        mid[1, c] = two[0][0]
        pieces = {(0, 1): zero[1], (0, 2): zero[2], (2, 1): two[1], (2, 2): two[2]}
        for beta in range(5):
            pieces[(1, beta)] = one[beta]
        for key, value in pieces.items():
            row = COMPLEX_ROWS[key]
            mid[row, c] = value[0]
            mid[row + 1, c] = value[1]

    def put(slot, value):
        cos_row = rows_ref[0, slot : slot + 1, :]
        sin_row = rows_ref[1, slot : slot + 1, :]
        where = slice(8 * slot, 8 * slot + 8)
        if value[1] is None:
            stage[where, :LANE] = value[0] * cos_row
            stage[where, LANE:] = -(value[0] * sin_row)
        else:
            stage[where, :LANE] = value[0] * cos_row + value[1] * sin_row
            stage[where, LANE:] = value[1] * cos_row - value[0] * sin_row

    def take(slot, real):
        cos_row = rows_ref[0, slot : slot + 1, :]
        sin_row = rows_ref[1, slot : slot + 1, :]
        where = slice(8 * slot, 8 * slot + 8)
        re, im = stage[where, :LANE], stage[where, LANE:]
        if real:
            return (re * cos_row - im * sin_row, None)
        return (re * cos_row - im * sin_row, im * cos_row + re * sin_row)

    cut = jnp.broadcast_to(cut_ref[:, 0:1], (8, LANE))
    gain = jnp.broadcast_to(cut_ref[:, 1:2], (8, LANE))
    for classes in CLASS_GROUPS:
        slots = [SLOT[key] for key in BINS if key[:2] in classes]
        start, count = slots[0], len(slots)
        for key in classes:
            if key in REAL_ROWS:
                row = REAL_ROWS[key]
                values = odd_real_forward([mid[row, c] for c in range(9)])
            else:
                row = COMPLEX_ROWS[key]
                values = odd_complex([(mid[row, c], mid[row + 1, c]) for c in range(9)], -1)
            for gamma, value in enumerate(values):
                put(SLOT[key + (gamma,)], value)
        where = slice(8 * start, 8 * (start + count))
        spectrum = split_dot(stage[where, :], forward_ref[...])
        scaled = []
        for index in range(count):
            slot = start + index
            wave = rows_ref[2, slot : slot + 1, :]
            decay = rows_ref[3, slot : slot + 1, :]
            factor = jnp.where(wave > cut, gain * decay, np.float32(1.0 / NLON))
            part = spectrum[8 * index : 8 * index + 8, :]
            scaled.append(part * jnp.concatenate([factor, factor], axis=1))
        stage[where, :] = split_dot(jnp.concatenate(scaled, axis=0), inverse_ref[...])
        for key in classes:
            if key in REAL_ROWS:
                row = REAL_ROWS[key]
                values = odd_real_inverse([take(SLOT[key + (gamma,)], gamma == 0) for gamma in range(5)])
                for c in range(9):
                    mid[row, c] = values[c]
            else:
                row = COMPLEX_ROWS[key]
                values = odd_complex([take(SLOT[key + (gamma,)], False) for gamma in range(9)], 1)
                for c in range(9):
                    mid[row, c] = values[c][0]
                    mid[row + 1, c] = values[c][1]

    for c in range(9):

        def piece(key):
            row = COMPLEX_ROWS[key]
            return (mid[row, c], mid[row + 1, c])

        zero = odd_real_inverse([(mid[0, c], None), piece((0, 1)), piece((0, 2))])
        two = odd_real_inverse([(mid[1, c], None), piece((2, 1)), piece((2, 2))])
        one = odd_complex([piece((1, beta)) for beta in range(5)], 1)
        for b in range(5):
            even, odd = zero[b] + two[b], zero[b] - two[b]
            re2, im2 = one[b][0] + one[b][0], one[b][1] + one[b][1]
            values = (even + re2, odd - im2, even - re2, odd + im2)
            for a in range(4):
                p = _tile_of(a, b, c)
                full[:, tile(p)] = values[a]
                if p == 0:
                    full[:, tile(TILES)] = values[a]
                if p == TILES - 1:
                    full[:, tile(-1)] = values[a]


def filter_kernel(x_ref, cut_ref, rows_ref, forward_ref, inverse_ref, early_ref, out_ref, full, mid, stage, result, sem):
    del early_ref
    sectors = x_ref.shape[0]
    span = NLON * LEV // sectors
    lane = lax.broadcasted_iota(jnp.int32, (8, LANE), 1)

    def source_tile(d, t):
        return x_ref[d, :, LANE * t : LANE * (t + 1)]

    circle_filter(source_tile, span, cut_ref, rows_ref, forward_ref, inverse_ref, full, mid, stage)
    for d in range(sectors):
        first, shift = divmod(LANE + d * span, LANE)
        pieces = []
        for t in range(span // LANE + 2):
            piece = full[:, LANE * (first + t) : LANE * (first + t + 1)]
            pieces.append(pltpu.roll(piece, LANE - shift, 1) if shift else piece)
        west = pieces[0] if shift else full[:, LANE * (first - 1) : LANE * first]
        for t in range(WIDE // LANE):
            value = jnp.where(lane < LANE - shift, pieces[t], pieces[t + 1]) if shift else pieces[t]
            if t == WIDE // LANE - 1:
                value = jnp.where(lane < LANE - LEV, value, west)
            result[d, :, LANE * t : LANE * (t + 1)] = value
        if d % BATCH == BATCH - 1:
            here = slice(d + 1 - BATCH, d + 1)
            pltpu.make_async_copy(result.at[here], out_ref.at[here], sem).start()
    pltpu.make_async_copy(result, out_ref, sem).wait()


PIECE = 48
AHEAD = 6
WINDOW = 10


def pole_kernel(where_ref, x_ref, cut_ref, rows_ref, forward_ref, inverse_ref, out_ref, full, mid, stage, wide, window):
    sectors = x_ref.shape[0]
    span = NLON * LEV // sectors
    lane = lax.broadcasted_iota(jnp.int32, (8, LANE), 1)

    def source_tile(d, t):
        if t:
            return None
        value = pltpu.roll(x_ref[d, :, WIDE - LANE : WIDE], PIECE, 1)
        return jnp.where(lane < PIECE, value, 0.0)

    circle_filter(source_tile, span, cut_ref, rows_ref, forward_ref, inverse_ref, full, mid, stage)
    wide[:, LANE * AHEAD : LANE * (AHEAD + TILES)] = full[:, LANE : LANE * (TILES + 1)]
    wide[:, : LANE * AHEAD] = full[:, LANE * (TILES + 1 - AHEAD) : LANE * (TILES + 1)]
    wide[:, LANE * (AHEAD + TILES) :] = full[:, LANE : LANE * 5]
    for k in range(2):
        tile = where_ref[2 * k]
        rest = where_ref[2 * k + 1]
        start = pl.multiple_of(tile * LANE, LANE)
        window[...] = pltpu.roll(wide[:, pl.ds(start, WINDOW * LANE)], WINDOW * LANE - rest, 1)
        total = None
        for r in range(8):
            first = 7 * PIECE - PIECE * r
            part = window[r : r + 1, first : first + span]
            total = part if total is None else total + part
        out_ref[k : k + 1, :span] = total


def pole_rows(where, blocks, cuts):
    rows, forward, inverse = tables()
    vmem = pl.BlockSpec(memory_space=pltpu.VMEM)
    return pl.pallas_call(
        pole_kernel,
        out_shape=jax.ShapeDtypeStruct((2, WIDE), jnp.float32),
        in_specs=[pl.BlockSpec(memory_space=pltpu.SMEM)] + [vmem] * 5,
        out_specs=vmem,
        scratch_shapes=[
            pltpu.VMEM((8, (TILES + 2) * LANE), jnp.float32),
            pltpu.VMEM((20, 9, 8, LANE), jnp.float32),
            pltpu.VMEM((8 * COUNT, 2 * LANE), jnp.float32),
            pltpu.VMEM((8, (AHEAD + TILES + 4) * LANE), jnp.float32),
            pltpu.VMEM((8, WINDOW * LANE), jnp.float32),
        ],
        compiler_params=pltpu.CompilerParams(vmem_limit_bytes=SMALL_GRANT),
        name="pole_filter",
    )(where, blocks, cuts, jnp.asarray(rows), jnp.asarray(forward), jnp.asarray(inverse))


def add_kernel(mine_ref, theirs_ref, out_ref):
    out_ref[...] = mine_ref[0:1, :] + theirs_ref[...]


def add_halves(mine, theirs):
    vmem = pl.BlockSpec(memory_space=pltpu.VMEM)
    return pl.pallas_call(
        add_kernel,
        out_shape=jax.ShapeDtypeStruct((1, WIDE), jnp.float32),
        in_specs=[vmem, vmem],
        out_specs=vmem,
        compiler_params=pltpu.CompilerParams(vmem_limit_bytes=SMALL_GRANT),
        name="pole_sum",
    )(mine, theirs)


def filter_rows(blocks, cuts, early):
    rows, forward, inverse = tables()
    return pl.pallas_call(
        filter_kernel,
        out_shape=jax.ShapeDtypeStruct((blocks.shape[0], 8, WIDE), jnp.float32),
        in_specs=[pl.BlockSpec(memory_space=pltpu.VMEM)] * 5 + [pl.BlockSpec(memory_space=pl.ANY)],
        out_specs=pl.BlockSpec(memory_space=pl.ANY),
        scratch_shapes=[
            pltpu.VMEM((8, (TILES + 2) * LANE), jnp.float32),
            pltpu.VMEM((20, 9, 8, LANE), jnp.float32),
            pltpu.VMEM((8 * COUNT, 2 * LANE), jnp.float32),
            pltpu.VMEM((blocks.shape[0], 8, WIDE), jnp.float32),
            pltpu.SemaphoreType.DMA,
        ],
        compiler_params=pltpu.CompilerParams(vmem_limit_bytes=SMALL_GRANT),
        name="polar_filter",
    )(blocks, cuts, jnp.asarray(rows), jnp.asarray(forward), jnp.asarray(inverse), early)


def pack_kernel(north_ref, winds_ref, layer_ref, tracer_ref, out_ref, buffer, last, pole, in_sem, out_sem):
    blocks = layer_ref.shape[0]
    span = layer_ref.shape[2]
    whole = span // LANE * LANE
    sources = [(layer_ref, 0, blocks, 2 * blocks), (winds_ref, 0, blocks, 0), (winds_ref, blocks, blocks, blocks), (tracer_ref, 0, blocks, 3 * blocks)]
    inward = []
    for index, (ref, start, count, base) in enumerate(sources):
        inward.append(pltpu.make_async_copy(ref.at[start : start + count], buffer.at[base : base + count], in_sem.at[index]))
        inward[-1].start()
    for index, (_, _, count, base) in enumerate(sources):
        inward[index].wait()
        here = slice(base, base + count)
        pltpu.make_async_copy(buffer.at[here, :, 0:whole], out_ref.at[here, :, 0:whole], out_sem.at[0]).start()
        if index == 0:
            row = jnp.where(
                north_ref[0] > 0, buffer[3 * blocks - 1, 7:8, :], buffer[2 * blocks, 0:1, :]
            )
            pole[0:1, 0:span] = row
            pole[0:1, span:WIDE] = jnp.zeros((1, WIDE - span), jnp.float32)
            pieces = []
            for c in range(2):
                for r in range(8):
                    first = span // 2 * c + PIECE * r
                    stop = min(first + PIECE, span // 2 * (c + 1))
                    pole[8 + 8 * c + r : 9 + 8 * c + r, 0:PIECE] = jnp.zeros((1, PIECE), jnp.float32)
                    pole[8 + 8 * c + r : 9 + 8 * c + r, 0 : stop - first] = pole[0:1, first:stop]
                pieces.append(pole[8 + 8 * c : 16 + 8 * c, 0:PIECE])
        for w in range(base, base + count):
            last[w, :, 0 : span - whole] = buffer[w, :, whole:span]
            last[w, :, span - whole : LANE] = pieces[w % 2]
        pltpu.make_async_copy(last.at[here], out_ref.at[here, :, whole:WIDE], out_sem.at[1]).start()
    pltpu.make_async_copy(buffer.at[:, :, 0:whole], out_ref.at[:, :, 0:whole], out_sem.at[0]).wait()
    pltpu.make_async_copy(last, out_ref.at[:, :, whole:WIDE], out_sem.at[1]).wait()


def pack(north, winds, thickness, tracer):
    row_count, width = thickness.shape
    blocks = row_count // 8
    anywhere = pl.BlockSpec(memory_space=pl.ANY)
    return pl.pallas_call(
        pack_kernel,
        out_shape=jax.ShapeDtypeStruct((4 * blocks, 8, WIDE), jnp.float32),
        in_specs=[pl.BlockSpec(memory_space=pltpu.SMEM), anywhere, anywhere, anywhere],
        out_specs=anywhere,
        scratch_shapes=[
            pltpu.VMEM((4 * blocks, 8, width), jnp.float32),
            pltpu.VMEM((4 * blocks, 8, LANE), jnp.float32),
            pltpu.VMEM((24, WIDE), jnp.float32),
            pltpu.SemaphoreType.DMA((4,)),
            pltpu.SemaphoreType.DMA((2,)),
        ],
        name="pack",
    )(
        north,
        winds.reshape(2 * blocks, 8, width),
        thickness.reshape(blocks, 8, width),
        tracer.reshape(blocks, 8, width),
    )


def east(x):
    return pltpu.roll(x, WIDE - LEV, 1)


def west(x):
    return pltpu.roll(x, LEV, 1)


def update(ratio, u, mid_rows, south_rows, north_rows, coef):
    v, h, q = mid_rows
    v_s, h_s, q_s = south_rows
    v_n, h_n, q_n = north_rows
    zonal, to_north, to_south, slope = (coef[:, k : k + 1] for k in range(4))
    h_e = east(h)
    su = u + east(u)
    fx = su * (h + h_e)
    gx = su * (q + east(q))
    wind_n = (v + v_n) * to_north
    wind_s = (v_s + v) * to_south
    new_h = h - (zonal * (fx - west(fx)) + (wind_n * (h + h_n) - wind_s * (h_s + h)))
    new_q = q - (zonal * (gx - west(gx)) + (wind_n * (q + q_n) - wind_s * (q_s + q)))
    new_v = v - np.float32(ratio) * (h_n - h_s)
    return slope * (h_e - west(h)), new_v, new_h, new_q


def main_kernel(ratio, field_ref, coef_ref, winds_ref, layer_ref, tracer_ref, out, sem):
    groups = field_ref.shape[0] // 4
    span = layer_ref.shape[1]
    sub = lax.broadcasted_iota(jnp.int32, (8, WIDE), 0)
    writes = []

    def shifted(f, g):
        x = field_ref[groups * f + g]
        south = jnp.where(sub == 0, pltpu.roll(field_ref[groups * f + g - 1], 1, 0), pltpu.roll(x, 1, 0))
        north = jnp.where(sub == 7, pltpu.roll(field_ref[groups * f + g + 1], 7, 0), pltpu.roll(x, 7, 0))
        return x, south, north

    for g in range(groups):
        rows = slice(8 * g, 8 * g + 8)
        u = field_ref[g]
        if 0 < g < groups - 1:
            mid_rows, south_rows, north_rows = zip(*(shifted(f, g) for f in (1, 2, 3)))
            du, new_v, new_h, new_q = update(ratio, u, mid_rows, south_rows, north_rows, coef_ref[rows, :])
            out[1, rows, :] = new_v[:, :span]
            out[2, rows, :] = new_h[:, :span]
            out[3, rows, :] = new_q[:, :span]
        else:
            h = field_ref[2 * groups + g]
            du = coef_ref[rows, 3:4] * (east(h) - west(h))
        out[0, rows, :] = (u - du)[:, :span]
        if g in (groups // 2 - 1, groups - 1):
            part = len(writes) // 4
            half = groups // 2
            all_rows = slice(8 * half * part, 8 * half * (part + 1))
            inner = slice(8, 8 * half) if part == 0 else slice(8 * half, 8 * (groups - 1))
            targets = (
                (0, all_rows, winds_ref.at[0, all_rows]),
                (1, inner, winds_ref.at[1, inner]),
                (2, inner, layer_ref.at[inner]),
                (3, inner, tracer_ref.at[inner]),
            )
            for k, where, target in targets:
                writes.append(pltpu.make_async_copy(out.at[k, where], target, sem.at[part, k]))
                writes[-1].start()
    for copy in writes:
        copy.wait()


def edge_kernel(
    ratio, state_ref, field_ref, second_ref, first_ref, across_ref, coef_ref, w_in, l_in, t_in, winds_ref, layer_ref, tracer_ref, out, sem
):
    del w_in, l_in, t_in
    groups = field_ref.shape[0] // 4
    is_even = state_ref[0] % 2 > 0
    pole = state_ref[0] // 2
    span = layer_ref.shape[1]
    sub = lax.broadcasted_iota(jnp.int32, (8, WIDE), 0)
    for side, g in enumerate((0, groups - 1)):
        rows = slice(8 * g, 8 * g + 8)
        near, far = (second_ref, first_ref) if side == 0 else (first_ref, second_ref)
        mid_rows, south_rows, north_rows = [], [], []
        for f in (1, 2, 3):
            x = field_ref[groups * f + g]
            halo = jnp.where(is_even, near[f - 1 : f, :], far[f - 1 : f, :])
            if f == 2:
                halo = jnp.where(pole == side + 1, across_ref[...], halo)
            if side == 0:
                south = jnp.where(sub == 0, halo, pltpu.roll(x, 1, 0))
                north = jnp.where(sub == 7, pltpu.roll(field_ref[groups * f + g + 1], 7, 0), pltpu.roll(x, 7, 0))
            else:
                south = jnp.where(sub == 0, pltpu.roll(field_ref[groups * f + g - 1], 1, 0), pltpu.roll(x, 1, 0))
                north = jnp.where(sub == 7, halo, pltpu.roll(x, 7, 0))
            mid_rows.append(x)
            south_rows.append(south)
            north_rows.append(north)
        _, new_v, new_h, new_q = update(ratio, field_ref[g], mid_rows, south_rows, north_rows, coef_ref[rows, :])
        for k, (value, target) in enumerate(
            ((new_v, winds_ref.at[1, rows]), (new_h, layer_ref.at[rows]), (new_q, tracer_ref.at[rows]))
        ):
            piece = slice(8 * (3 * side + k), 8 * (3 * side + k) + 8)
            out[piece, :] = value[:, :span]
            pltpu.make_async_copy(out.at[piece], target, sem).start()
    pltpu.make_async_copy(out, winds_ref.at[1, 0 : out.shape[0]], sem).wait()


def stencil_main(fields, coef, ratio, row_count, width):
    vmem = pl.BlockSpec(memory_space=pltpu.VMEM)
    anywhere = pl.BlockSpec(memory_space=pl.ANY)
    return pl.pallas_call(
        functools.partial(main_kernel, ratio),
        out_shape=(
            jax.ShapeDtypeStruct((2, row_count, width), jnp.float32),
            jax.ShapeDtypeStruct((row_count, width), jnp.float32),
            jax.ShapeDtypeStruct((row_count, width), jnp.float32),
        ),
        in_specs=[vmem, vmem],
        out_specs=(anywhere, anywhere, anywhere),
        scratch_shapes=[
            pltpu.VMEM((4, row_count, width), jnp.float32),
            pltpu.SemaphoreType.DMA((2, 4)),
        ],
        compiler_params=pltpu.CompilerParams(vmem_limit_bytes=SMALL_GRANT),
        cost_estimate=pl.CostEstimate(flops=10_000_000, bytes_accessed=1_600_000, transcendentals=0),
        name="stencil_main",
    )(fields, coef)


def stencil_edge(state, fields, first, second, across, coef, outs, ratio):
    vmem = pl.BlockSpec(memory_space=pltpu.VMEM)
    anywhere = pl.BlockSpec(memory_space=pl.ANY)
    width = outs[1].shape[1]
    return pl.pallas_call(
        functools.partial(edge_kernel, ratio),
        out_shape=tuple(jax.ShapeDtypeStruct(out.shape, jnp.float32) for out in outs),
        in_specs=[pl.BlockSpec(memory_space=pltpu.SMEM), vmem, vmem, vmem, vmem, vmem, anywhere, anywhere, anywhere],
        out_specs=(anywhere, anywhere, anywhere),
        scratch_shapes=[pltpu.VMEM((48, width), jnp.float32), pltpu.SemaphoreType.DMA],
        input_output_aliases={6: 0, 7: 1, 8: 2},
        compiler_params=pltpu.CompilerParams(vmem_limit_bytes=SMALL_GRANT),
        name="stencil_edge",
    )(state, fields, second, first, across, coef, *outs)


def per_device(winds, thickness, tracer, cutoff, damping):
    lat_size = lax.axis_size("lat")
    lon_size = lax.axis_size("lon")
    band = lax.axis_index("lat")
    sector = lax.axis_index("lon")
    row_count, width = thickness.shape
    nlat = row_count * lat_size

    is_north = band == lat_size - 1
    blocks = pack(is_north.astype(jnp.int32)[None], winds, thickness, tracer)
    owned = lax.all_to_all(blocks, "lon", split_axis=0, concat_axis=0, tiled=True)

    is_polar = (band < lat_size // 4) | (band >= lat_size - lat_size // 4)
    group = sector % (row_count // 8)
    cut = lax.dynamic_slice_in_dim(cutoff.astype(jnp.float32), group * 8, 8)
    damp = lax.dynamic_slice_in_dim(damping, group * 8, 8)
    gain = damp * cut * cut
    cut = jnp.where(is_polar, cut, jnp.float32(NLON))
    cuts = jnp.stack([cut, gain], axis=1)

    lon_step = 2.0 * math.pi / NLON
    lat_step = math.pi / nlat
    rows = (band * row_count + jnp.arange(row_count, dtype=jnp.int32)).astype(jnp.float32)
    center = jnp.cos(-math.pi / 2 + (rows + 0.5) * lat_step)
    face = band * row_count + jnp.arange(row_count + 1, dtype=jnp.int32)
    cos_face = jnp.where(
        (face == 0) | (face == nlat), 0.0, jnp.cos(-math.pi / 2 + face.astype(jnp.float32) * lat_step)
    )
    quarter = 0.25 / center
    aspect = lon_step / lat_step
    coef = jnp.stack(
        [quarter, aspect * quarter * cos_face[1:], aspect * quarter * cos_face[:-1], 2.0 * quarter], axis=1
    )

    filtered = filter_rows(owned, cuts, coef)
    fields = lax.all_to_all(filtered, "lon", split_axis=0, concat_axis=0, tiled=True)
    core = sector % 2
    opposite = [(x + lon_size // 2) % lon_size for x in (sector, sector + 1 - 2 * core)]
    starts = [width * x - (width // 2) * core + LANE * AHEAD - 7 * PIECE for x in opposite]
    where = jnp.stack([starts[0] // LANE, starts[0] % LANE, starts[1] // LANE, starts[1] % LANE]).astype(jnp.int32)
    pole_cut = jnp.where(is_north, cutoff[-1], cutoff[0]).astype(jnp.float32)
    pole_damp = jnp.where(is_north, damping[-1], damping[0])
    pole_cuts = jnp.broadcast_to(jnp.stack([pole_cut, pole_damp * pole_cut * pole_cut])[None, :], (8, 2))
    halves = pole_rows(where, owned, pole_cuts)
    theirs = lax.ppermute(halves[1:2], "lon", [(x, x ^ 1) for x in range(lon_size)])
    across = add_halves(halves, theirs)

    even = band % 2 == 0
    groups = row_count // 8
    low = jnp.stack([fields[f * groups, 0] for f in (1, 2, 3)])
    high = jnp.stack([fields[f * groups + groups - 1, 7] for f in (1, 2, 3)])
    pairs = {0: [], 1: []}
    for z in range(lat_size):
        for e in range(lon_size):
            here = z * lon_size + e
            up, down = here + lon_size, here - lon_size
            pairs[0].append((here, up if z % 2 == 0 else down))
            if 0 < z < lat_size - 1:
                pairs[1].append((here, down if z % 2 == 0 else up))
    first = lax.ppermute(jnp.where(even, high, low), ("lat", "lon"), pairs[0])
    second = lax.ppermute(jnp.where(even, low, high), ("lat", "lon"), pairs[1])

    ratio = lon_step / (2.0 * lat_step)
    outs = stencil_main(fields, coef, ratio, row_count, width)
    state = even.astype(jnp.int32) + 2 * (band == 0).astype(jnp.int32) + 4 * is_north.astype(jnp.int32)
    return stencil_edge(state[None], fields, first, second, across, coef, outs, ratio)


def solution(mesh):
    placed = (P(None, "lat", "lon"), P("lat", "lon"), P("lat", "lon"), P("lat"), P("lat"))
    return jax.shard_map(
        per_device,
        mesh=mesh,
        in_specs=placed,
        out_specs=(P(None, "lat", "lon"), P("lat", "lon"), P("lat", "lon")),
        check_vma=False,
    )
```
